32 devices in a mesh: dp: 4 (over y, x), fsdp: 2 (over core), mp: 4 (over z).
Axes of the slice: x: 2, y: 2, z: 4, core: 2. Of those that a mesh axis runs over, the one named last changes fastest.
Arguments:
- dec_input: bfloat16 [128, 128, 1024], P(('dp', 'fsdp', 'mp')), may hold values from -6 to 6
- enc_output: bfloat16 [128, 1152, 1024], P(('dp', 'fsdp', 'mp')), may hold values from -6 to 6
- image_pairs: int32 [128], P(('dp', 'fsdp', 'mp')), may hold values from 1 to 2
- text_lengths: int32 [128], P(('dp', 'fsdp', 'mp')), may hold values from 1 to 128
- dec_lengths: int32 [128], P(('dp', 'fsdp', 'mp')), may hold values from 1 to 128
- self_query: bfloat16 [1024, 1024], P(('fsdp', 'mp')), may hold values from -0.09375 to 0.09375
- self_key: bfloat16 [1024, 1024], P(('fsdp', 'mp')), may hold values from -0.09375 to 0.09375
- self_value: bfloat16 [1024, 1024], P(('fsdp', 'mp')), may hold values from -0.1875 to 0.1875
- self_out: bfloat16 [1024, 1024], P(('fsdp', 'mp')), may hold values from -0.5 to 0.5
- cross_query: bfloat16 [1024, 1024], P(('fsdp', 'mp')), may hold values from -0.09375 to 0.09375
- cross_key: bfloat16 [1024, 1024], P(('fsdp', 'mp')), may hold values from -0.09375 to 0.09375
- cross_value: bfloat16 [1024, 1024], P(('fsdp', 'mp')), may hold values from -0.1875 to 0.1875
- cross_out: bfloat16 [1024, 1024], P(('fsdp', 'mp')), may hold values from -0.5 to 0.5
- ffn_gate: bfloat16 [1024, 2816], P(('fsdp', 'mp')), may hold values from -0.1875 to 0.1875
- ffn_up: bfloat16 [1024, 2816], P(('fsdp', 'mp')), may hold values from -0.1875 to 0.1875
- ffn_down: bfloat16 [2816, 1024], P(('fsdp', 'mp')), may hold values from -0.109375 to 0.109375
- norm_first: bfloat16 [1024], P(('fsdp', 'mp')), may hold values from 0.5 to 1.5
- norm_second: bfloat16 [1024], P(('fsdp', 'mp')), may hold values from 0.5 to 1.5
- norm_third: bfloat16 [1024], P(('fsdp', 'mp')), may hold values from 0.5 to 1.5
- bias_table: bfloat16 [32, 16], replicated, may hold values from -4 to 4
- cotangent: bfloat16 [128, 128, 1024], P(('dp', 'fsdp', 'mp')), may hold values from -6 to 6
Outputs:
- dec_output: bfloat16 [128, 128, 1024], P(('dp', 'fsdp', 'mp'))
- dec_input_grad: float32 [128, 128, 1024], P(('dp', 'fsdp', 'mp'))
- enc_output_grad: float32 [128, 1152, 1024], P(('dp', 'fsdp', 'mp'))
- self_query_grad: float32 [1024, 1024], P(('fsdp', 'mp'))
- self_key_grad: float32 [1024, 1024], P(('fsdp', 'mp'))
- self_value_grad: float32 [1024, 1024], P(('fsdp', 'mp'))
- self_out_grad: float32 [1024, 1024], P(('fsdp', 'mp'))
- cross_query_grad: float32 [1024, 1024], P(('fsdp', 'mp'))
- cross_key_grad: float32 [1024, 1024], P(('fsdp', 'mp'))
- cross_value_grad: float32 [1024, 1024], P(('fsdp', 'mp'))
- cross_out_grad: float32 [1024, 1024], P(('fsdp', 'mp'))
- ffn_gate_grad: float32 [1024, 2816], P(('fsdp', 'mp'))
- ffn_up_grad: float32 [1024, 2816], P(('fsdp', 'mp'))
- ffn_down_grad: float32 [2816, 1024], P(('fsdp', 'mp'))
- norm_first_grad: float32 [1024], P(('fsdp', 'mp'))
- norm_second_grad: float32 [1024], P(('fsdp', 'mp'))
- norm_third_grad: float32 [1024], P(('fsdp', 'mp'))
- bias_table_grad: float32 [32, 16], replicated
The draws below stay inside these ranges and needn't reach their ends.
Inputs may be any that keep to these rules, and one draw needn't show every extreme that they name: Item b has 2 * image_pairs[b] images, in the first slots of the encoder output. `text_lengths`: text tokens of item b stand in encoder slots 4 * 256 onward.
All inputs are finite; a program needn't handle non-finite values.
Results may differ from the reference program's by a relative error of at most 0.025.
The reference program's roundings to bfloat16 on the way count: a program that leaves them out, or rounds other values in their place, can miss the bound.
Values may be sent and summed in bfloat16 or wider, within the bound.
No kernel may reach another device: no remote copies, remote signals or barrier semaphores. Data moves between devices by JAX's collectives and lax.ppermute only.
A program may use at most 320 MiB of HBM per device.

```python
import math
import jax
import jax.numpy as jnp
import numpy as np
from jax import lax

D = 1024
HEADS = 16
HEAD_DIM = 64
FF = 2816
BUCKETS = 32
DEC_LEN = 128
PATCHES = 256
TEXT_LEN = 128
ENC_LEN = 1152
BATCH = 128


def with_ends(array, stream_key, smallest, largest):
    place = [jax.random.randint(jax.random.fold_in(stream_key, axis), (), 0, length) for axis, length in enumerate(array.shape)]
    main_axis = array.shape.index(max(array.shape))
    beside = place[:main_axis] + [(place[main_axis] + 1) % array.shape[main_axis]] + place[main_axis + 1:]
    return array.at[tuple(place)].set(smallest).at[tuple(beside)].set(largest)


def block_levels(own_key, extent, split, low, top_value):
    level, own = 1.0, jax.random.fold_in(own_key, 6)
    for position, parts in split:
        steps = jnp.exp(jax.random.uniform(jax.random.fold_in(own, position), (parts,), jnp.float32, low / len(split), top_value / len(split)))
        level = level * jnp.repeat(steps, extent[position] // parts).reshape([-1 if axis == position else 1 for axis in range(len(extent))])
    return level


def noise(own_key, extent, scale, limit, shards=(), kind=jnp.bfloat16):
    factor_of = block_levels(own_key, extent, shards, -0.22, 0.18) if shards else 1.0
    entries = jax.random.normal(own_key, extent, jnp.float32) * scale * factor_of
    return jnp.minimum(jnp.maximum(entries, -limit), limit).astype(kind)


def setup_inputs(seed: int = 0) -> dict:
    seeds = jax.random.split(jax.random.key(seed), 22)
    return {
        "dec_input": noise(seeds[0], (BATCH, DEC_LEN, D), 1.0, 6.0, ((0, 32),)),
        "enc_output": noise(seeds[1], (BATCH, ENC_LEN, D), 1.0, 6.0, ((0, 32),)),
        "image_pairs": with_ends(jax.random.randint(seeds[2], (BATCH,), 1, 3), jax.random.fold_in(seeds[2], 1), 1, 2).astype(jnp.int32),
        "text_lengths": with_ends(jax.random.randint(seeds[3], (BATCH,), 1, TEXT_LEN + 1), jax.random.fold_in(seeds[3], 1), 1, TEXT_LEN).astype(jnp.int32),
        "dec_lengths": with_ends(jax.random.randint(seeds[4], (BATCH,), 1, DEC_LEN + 1), jax.random.fold_in(seeds[4], 1), 1, DEC_LEN).astype(jnp.int32),
        "self_query": noise(seeds[5], (D, D), (4 * D) ** -0.5, 0.09375, ((0, 8),)),
        "self_key": noise(seeds[6], (D, D), (4 * D) ** -0.5, 0.09375, ((0, 8),)),
        "self_value": noise(seeds[7], (D, D), D ** -0.5, 0.1875, ((0, 8),)),
        "self_out": noise(seeds[8], (D, D), (D // 8) ** -0.5, 0.5, ((0, 8),)),
        "cross_query": noise(seeds[9], (D, D), (4 * D) ** -0.5, 0.09375, ((0, 8),)),
        "cross_key": noise(seeds[10], (D, D), (4 * D) ** -0.5, 0.09375, ((0, 8),)),
        "cross_value": noise(seeds[11], (D, D), D ** -0.5, 0.1875, ((0, 8),)),
        "cross_out": noise(seeds[12], (D, D), (D // 8) ** -0.5, 0.5, ((0, 8),)),
        "ffn_gate": noise(seeds[13], (D, FF), D ** -0.5, 0.1875, ((0, 8),)),
        "ffn_up": noise(seeds[14], (D, FF), D ** -0.5, 0.1875, ((0, 8),)),
        "ffn_down": noise(seeds[15], (FF, D), FF ** -0.5, 0.109375, ((0, 8),)),
        "norm_first": jnp.clip(1.0 + 0.1 * jax.random.normal(seeds[16], (D,), jnp.float32), 0.5, 1.5).astype(jnp.bfloat16),
        "norm_second": jnp.clip(1.0 + 0.1 * jax.random.normal(seeds[17], (D,), jnp.float32), 0.5, 1.5).astype(jnp.bfloat16),
        "norm_third": jnp.clip(1.0 + 0.1 * jax.random.normal(seeds[18], (D,), jnp.float32), 0.5, 1.5).astype(jnp.bfloat16),
        "bias_table": noise(seeds[19], (BUCKETS, HEADS), 1.0, 4.0),
        "cotangent": noise(seeds[20], (BATCH, DEC_LEN, D), 1.0, 6.0, ((0, 32),)),
    }


@jax.custom_vjp
def low(v):
    return lax.optimization_barrier(v.astype(jnp.bfloat16)).astype(jnp.float32)

@jax.custom_vjp
def low_back(v):
    return v

def low_keep(v):
    return (low(v), None)

def low_pass(kept, grad):
    return (grad,)

def back_keep(v):
    return (v, None)

def back_low(kept, grad):
    return (low(grad),)
low.defvjp(low_keep, low_pass)
low_back.defvjp(back_keep, back_low)
EPSILON = 1e-06
MASKED = -1000000000.0
GELU_COEF = 0.044715

def bucket_table(length):
    rows_index = np.arange(length)[:, None]
    cols_index = np.arange(length)[None, :]
    distance = np.maximum(rows_index - cols_index, 0)
    spread = np.floor(np.log(np.maximum(distance, 1) / 16.0) / np.log(8.0) * 16.0)
    far_bucket = np.minimum(16.0 + spread, 31.0)
    return np.where(distance < 16, distance, far_bucket).astype(np.int32)

def rounded(values):
    return low(low_back(values))

def product(left, right):
    return jnp.dot(left, right, precision=lax.Precision.HIGHEST)

def norm_rows(values, gain):
    return values * lax.rsqrt(lax.optimization_barrier(jnp.mean(values * values, axis=-1, keepdims=True)) + EPSILON) * gain

def gelu_tanh(values):
    return 0.5 * values * (1.0 + jnp.tanh(math.sqrt(2.0 / math.pi) * (values + GELU_COEF * values * values * values)))

def attend(queries, key_rows, value_rows, relative, valid_mask):
    query_heads = queries.reshape(queries.shape[0], HEADS, HEAD_DIM)
    key_heads = key_rows.reshape(key_rows.shape[0], HEADS, HEAD_DIM)
    value_heads = value_rows.reshape(value_rows.shape[0], HEADS, HEAD_DIM)
    scores = jnp.einsum('qhe,khe->hqk', query_heads, key_heads, precision=lax.Precision.HIGHEST) + relative
    scores = jnp.where(valid_mask, low_back(scores), MASKED)
    row_max = lax.optimization_barrier(jnp.max(scores, axis=-1, keepdims=True))
    powers = jnp.exp(scores - row_max)
    attention = low(powers / lax.optimization_barrier(jnp.sum(powers, axis=-1, keepdims=True)))
    mixture = jnp.einsum('hqk,khe->qhe', attention, value_heads, precision=lax.Precision.HIGHEST)
    return rounded(mixture.reshape(queries.shape[0], HEADS * HEAD_DIM))

def decoder_layer(params, dec_rows, enc_rows, buckets, self_valid, cross_valid):
    self_query, self_key, self_value, self_out, cross_query, cross_key, cross_value, cross_out, ffn_gate, ffn_up, ffn_down, norm_first, norm_second, norm_third, bias_table = params
    relative = jnp.transpose(bias_table[buckets], (2, 0, 1))
    normed = low(norm_rows(dec_rows, norm_first))
    queries = rounded(product(normed, self_query))
    key_rows = rounded(product(normed, self_key))
    value_rows = rounded(product(normed, self_value))
    first_sum = dec_rows + low_back(product(attend(queries, key_rows, value_rows, relative, self_valid), self_out))
    normed = low(norm_rows(first_sum, norm_second))
    cross_queries = rounded(product(normed, cross_query))
    cross_keys = rounded(product(enc_rows, cross_key))
    cross_values = rounded(product(enc_rows, cross_value))
    second_sum = first_sum + low_back(product(attend(cross_queries, cross_keys, cross_values, 0.0, cross_valid), cross_out))
    normed = low(norm_rows(second_sum, norm_third))
    gate_values = low_back(product(normed, ffn_gate))
    up_values = low_back(product(normed, ffn_up))
    hidden = low(gelu_tanh(gate_values) * up_values)
    return second_sum + low_back(product(hidden, ffn_down))

def reference(dec_input, enc_output, image_pairs, text_lengths, dec_lengths, self_query, self_key, self_value, self_out, cross_query, cross_key, cross_value, cross_out, ffn_gate, ffn_up, ffn_down, norm_first, norm_second, norm_third, bias_table, cotangent):
    params = tuple((weight.astype(jnp.float32) for weight in (self_query, self_key, self_value, self_out, cross_query, cross_key, cross_value, cross_out, ffn_gate, ffn_up, ffn_down, norm_first, norm_second, norm_third, bias_table)))
    buckets = jnp.asarray(bucket_table(DEC_LEN))
    positions = jnp.arange(DEC_LEN)
    enc_slots = jnp.arange(ENC_LEN)

    def scan_step(totals, sample):
        dec_rows, enc_rows, pair_count, text_count, valid_length, cot_rows = sample
        self_valid = (positions[None, :] <= positions[:, None]) & (positions[None, :] < valid_length)
        cross_valid = ((enc_slots < 2 * PATCHES * pair_count) | (enc_slots >= 4 * PATCHES) & (enc_slots < 4 * PATCHES + text_count))[None, :]

        def forward(weights, dec_part, enc_part):
            return decoder_layer(weights, dec_part, enc_part, buckets, self_valid, cross_valid)
        result, pullback = jax.vjp(forward, params, dec_rows.astype(jnp.float32), enc_rows.astype(jnp.float32))
        weight_grads, dec_grad, enc_grad = pullback(cot_rows.astype(jnp.float32))
        totals = jax.tree.map(jnp.add, totals, weight_grads)
        return (totals, (result.astype(jnp.bfloat16), dec_grad, enc_grad))
    zero_grads = tuple((jnp.zeros_like(weight) for weight in params))
    totals, (outputs, dec_grads, enc_grads) = lax.scan(scan_step, zero_grads, (dec_input, enc_output, image_pairs, text_lengths, dec_lengths, cotangent))
    return (outputs, dec_grads, enc_grads, totals[0], totals[1], totals[2], totals[3], totals[4], totals[5], totals[6], totals[7], totals[8], totals[9], totals[10], totals[11], totals[12], totals[13], totals[14])
```

```python
import functools
import math

import jax
import jax.numpy as jnp
import numpy as np
from jax import lax
from jax.experimental import pallas as pl
from jax.experimental.pallas import tpu as pltpu
from jax.sharding import PartitionSpec as P

PATCHES = 256
EPSILON = 1e-06
MASKED = -1000000000.0
GELU_COEF = 0.044715
BF = jnp.bfloat16
F32 = jnp.float32
ANY = pl.ANY


def bucket_table(length):
    rows_index = np.arange(length)[:, None]
    cols_index = np.arange(length)[None, :]
    distance = np.maximum(rows_index - cols_index, 0)
    spread = np.floor(np.log(np.maximum(distance, 1) / 16.0) / np.log(8.0) * 16.0)
    far_bucket = np.minimum(16.0 + spread, 31.0)
    return np.where(distance < 16, distance, far_bucket).astype(np.int32)


def norm_rows(values, gain):
    return values * lax.rsqrt(jnp.mean(values * values, axis=-1, keepdims=True) + EPSILON) * gain


def gelu_tanh(values):
    return (
        0.5
        * values
        * (
            1.0
            + jnp.tanh(math.sqrt(2.0 / math.pi) * (values + GELU_COEF * values * values * values))
        )
    )


def gated_unit(gate_values, up_values):
    return gelu_tanh(gate_values) * up_values


def matmul(left, right):
    return jnp.dot(left, right, preferred_element_type=F32)


def weight_grad(left, right):
    return lax.dot_general(left, right, (((0,), (0,)), ((), ())), preferred_element_type=F32)


def input_grad(upstream, weight):
    return lax.dot_general(upstream, weight, (((1,), (1,)), ((), ())), preferred_element_type=F32)


def attend_forward(queries, key_rows, value_rows, relative, valid_mask):
    scores = (
        jnp.einsum("bqhe,bkhe->bhqk", queries, key_rows, preferred_element_type=F32) + relative
    )
    scores = jnp.where(valid_mask, scores, MASKED)
    row_max = jnp.max(scores, axis=-1, keepdims=True)
    powers = jnp.exp(scores - row_max)
    total = jnp.sum(powers, axis=-1, keepdims=True)
    attention = (powers / total).astype(BF)
    mixture = jnp.einsum("bhqk,bkhe->bqhe", attention, value_rows, preferred_element_type=F32)
    return (mixture.astype(BF), row_max + jnp.log(total))


def attend_backward(queries, key_rows, value_rows, relative, valid_mask, log_total, mixture_grad):
    scores = (
        jnp.einsum("bqhe,bkhe->bhqk", queries, key_rows, preferred_element_type=F32) + relative
    )
    attention = jnp.where(valid_mask, jnp.exp(scores - log_total), 0.0)
    attention_grad = jnp.einsum(
        "bqhe,bkhe->bhqk", mixture_grad, value_rows, preferred_element_type=F32
    )
    row_delta = jnp.sum(attention * attention_grad, axis=-1, keepdims=True)
    score_grad = (attention * (attention_grad - row_delta)).astype(BF)
    query_grad = jnp.einsum(
        "bhqk,bkhe->bqhe", score_grad, key_rows, preferred_element_type=F32
    ).astype(BF)
    key_grad = jnp.einsum(
        "bhqk,bqhe->bkhe", score_grad, queries, preferred_element_type=F32
    ).astype(BF)
    value_grad = jnp.einsum(
        "bhqk,bqhe->bkhe", attention.astype(BF), mixture_grad, preferred_element_type=F32
    ).astype(BF)
    return (query_grad, key_grad, value_grad, score_grad)


def swap(value, axis, bit):
    size = lax.axis_size(axis)
    return lax.ppermute(value, axis, [(i, i ^ bit) for i in range(size)])


def place():
    return jnp.stack(
        [lax.axis_index("fsdp"), lax.axis_index("mp"), lax.axis_index("dp")]
    ).astype(jnp.int32)


def assemble_kernel(rows, cols, splits, me, *refs):
    pieces, outs = refs[:10], refs[10 : 10 + len(splits)]
    buf, in_sem, out_sem = refs[10 + len(splits) :]
    c, z, p = me[0], me[1], me[2]
    quarter = cols // 4
    blocks = []
    n = 0
    for other in range(2):
        for zr in range(4):
            row = pl.multiple_of(((c ^ other) * 4 + (z ^ zr)) * rows, rows)
            copies = []
            if zr == 0:
                copies.append(
                    pltpu.make_async_copy(
                        pieces[5 * other], buf.at[pl.ds(row, rows), :], in_sem.at[n]
                    )
                )
                n += 1
            else:
                for j in range(4):
                    col = pl.multiple_of((p ^ j) * quarter, 128)
                    copies.append(
                        pltpu.make_async_copy(
                            pieces[5 * other + 1 + j].at[zr - 1],
                            buf.at[pl.ds(row, rows), pl.ds(col, quarter)],
                            in_sem.at[n],
                        )
                    )
                    n += 1
            for copy in copies:
                copy.start()
            blocks.append((row, copies))
    pending = []
    n = 0
    for row, copies in blocks:
        for copy in copies:
            copy.wait()
        start = 0
        for out, width in zip(outs, splits):
            copy = pltpu.make_async_copy(
                buf.at[pl.ds(row, rows), pl.ds(start, width)],
                out.at[pl.ds(row, rows), :],
                out_sem.at[n],
            )
            copy.start()
            pending.append(copy)
            start += width
            n += 1
    for copy in pending:
        copy.wait()


def assemble(me, pieces, rows, splits):
    cols = sum(splits)
    total = 8 * rows
    return pl.pallas_call(
        functools.partial(assemble_kernel, rows, cols, splits),
        out_shape=[jax.ShapeDtypeStruct((total, width), BF) for width in splits],
        in_specs=[pl.BlockSpec(memory_space=pltpu.SMEM)] + [pl.BlockSpec(memory_space=ANY)] * 10,
        out_specs=[pl.BlockSpec(memory_space=ANY)] * len(splits),
        scratch_shapes=[
            pltpu.VMEM((total, cols), BF),
            pltpu.SemaphoreType.DMA((26,)),
            pltpu.SemaphoreType.DMA((8 * len(splits),)),
        ],
        cost_estimate=pl.CostEstimate(
            flops=0, bytes_accessed=4 * total * cols, transcendentals=0
        ),
    )(me, *pieces)


def gather_group(me, shards, token, flip):
    splits = tuple(shard.shape[1] for shard in shards)
    own = shards[0] if len(shards) == 1 else jnp.concatenate(shards, axis=1)
    rows, cols = own.shape
    quarter = cols // 4
    part = lax.dynamic_slice_in_dim(own, me[2] * quarter, quarter, axis=1)
    if token is not None:
        part, token = lax.optimization_barrier((part, token))
    along_z = [swap(part, "mp", bit) for bit in (1, 2, 3)]
    first, second = (1, 2) if flip else (2, 1)
    a0 = jnp.stack(along_z)
    hop = swap(a0, "dp", first)
    side = swap(a0, "dp", second)
    far = swap(hop, "dp", second)
    planes = [a0, hop, side, far] if flip else [a0, side, hop, far]
    mine = [own] + planes
    theirs = [swap(piece, "fsdp", 1) for piece in mine]
    full = assemble(me, mine + theirs, rows, splits)
    return full, tuple(along_z)


def rs_add_kernel(pos, ka_s, ka_k, kb_s, kb_k, ra_s, ra_k, rb_s, rb_k, sa, sb, keep):
    sa[...] = (ka_s[...].astype(F32) + ra_s[...].astype(F32)).astype(BF)
    sb[...] = (kb_s[...].astype(F32) + rb_s[...].astype(F32)).astype(BF)
    keep[0] = (ka_k[...].astype(F32) + ra_k[...].astype(F32)).astype(BF)
    keep[1] = (kb_k[...].astype(F32) + rb_k[...].astype(F32)).astype(BF)


def rs_z_kernel(pos, *refs):
    keeps, ras, rbs, outs = refs[:4], refs[4:8], refs[8:12], refs[12:]
    z = pos[1]
    for k in range(4):
        low = (z ^ k) < 2
        recv = jnp.where(low, ras[k][0].astype(F32), rbs[k][0].astype(F32))
        outs[k][...] = (keeps[k][0].astype(F32) + recv).astype(BF)


def rs_last_kernel(own, r1, r2, r3, out):
    out[...] = (
        (own[...].astype(F32) + r1[...].astype(F32)) + (r2[...].astype(F32) + r3[...].astype(F32))
    ).astype(BF)


def rs_place_kernel(splits, pos, p0, p1, p2, p3, *refs):
    outs, buf = refs[:-1], refs[-1]
    quarter = p0.shape[1]
    z, p = pos[1], pos[2]
    for j, piece in enumerate((p0, p1, p2, p3)):
        q = p ^ j
        x, y = q & 1, q >> 1
        col = jnp.where(z < 2, x * 2 + y, q) * quarter
        buf[:, pl.ds(pl.multiple_of(col, 128), quarter)] = piece[...].astype(F32)
    start = 0
    for out, width in zip(outs, splits):
        out[...] = buf[:, start : start + width]
        start += width


def vmem_call(kernel, outs, ins, pos=None, scratch=(), moved=0):
    specs = [pl.BlockSpec(memory_space=pltpu.VMEM)] * len(ins)
    args = list(ins)
    if pos is not None:
        specs = [pl.BlockSpec(memory_space=pltpu.SMEM)] + specs
        args = [pos] + args
    return pl.pallas_call(
        kernel,
        out_shape=outs,
        in_specs=specs,
        out_specs=jax.tree.map(lambda _: pl.BlockSpec(memory_space=pltpu.VMEM), outs),
        scratch_shapes=list(scratch),
        cost_estimate=pl.CostEstimate(flops=0, bytes_accessed=moved, transcendentals=0),
    )(*args)


def scatter_group(me, left, right, splits):
    total, cols = left.shape[1], right.shape[1]
    half, rows, quarter = total // 2, total // 8, cols // 4
    c, x, y = me[0], me[2] & 1, me[2] >> 1
    theirs = lax.dynamic_slice_in_dim(left, (1 - c) * half, half, axis=1)
    mine = lax.dynamic_slice_in_dim(left, c * half, half, axis=1)
    sent = weight_grad(theirs, right).astype(BF)
    got = swap(sent, "fsdp", 1)
    got, mine = lax.optimization_barrier((got, mine))
    kept = (weight_grad(mine, right) + got.astype(F32)).astype(BF)
    return scatter_tail(me, kept, splits)


def scatter_tail(me, kept, splits):
    half, cols = kept.shape
    rows, quarter = half // 4, cols // 4
    c, x, y = me[0], me[2] & 1, me[2] >> 1
    two = 2 * rows
    send_a = lax.dynamic_slice(kept, (0, (1 - x) * 2 * quarter), (two, 2 * quarter))
    send_b = lax.dynamic_slice(kept, (two, (1 - y) * 2 * quarter), (two, 2 * quarter))
    recv_a = swap(send_a, "dp", 1)
    recv_b = swap(send_b, "dp", 2)
    steps = 4 if rows % 64 == 0 else 2
    block = two // steps

    def at(kind):
        def index(i, pos):
            px, py = pos[2] & 1, pos[2] >> 1
            return {
                "ka_s": (i, px * 2 + 1 - py),
                "ka_k": (i, px * 2 + py),
                "kb_s": (steps + i, py * 2 + 1 - px),
                "kb_k": (steps + i, py * 2 + px),
                "ra_s": (i, 1 - py),
                "ra_k": (i, py),
                "rb_s": (i, 1 - px),
                "rb_k": (i, px),
            }[kind]

        return pl.BlockSpec((block, quarter), index)

    send_c, send_d, keep = pl.pallas_call(
        rs_add_kernel,
        out_shape=[
            jax.ShapeDtypeStruct((two, quarter), BF),
            jax.ShapeDtypeStruct((two, quarter), BF),
            jax.ShapeDtypeStruct((2, two, quarter), BF),
        ],
        grid_spec=pltpu.PrefetchScalarGridSpec(
            num_scalar_prefetch=1,
            grid=(steps,),
            in_specs=[
                at(k) for k in ("ka_s", "ka_k", "kb_s", "kb_k", "ra_s", "ra_k", "rb_s", "rb_k")
            ],
            out_specs=[
                pl.BlockSpec((block, quarter), lambda i, pos: (i, 0)),
                pl.BlockSpec((block, quarter), lambda i, pos: (i, 0)),
                pl.BlockSpec((2, block, quarter), lambda i, pos: (0, i, 0)),
            ],
        ),
        cost_estimate=pl.CostEstimate(
            flops=0, bytes_accessed=6 * half * quarter * 2, transcendentals=0
        ),
    )(me, kept, kept, kept, kept, recv_a, recv_a, recv_b, recv_b)
    recv_c = swap(send_c, "dp", 2).reshape(2, rows, quarter)
    recv_d = swap(send_d, "dp", 1).reshape(2, rows, quarter)
    keep = keep.reshape(4, rows, quarter)

    def zspec(k, wrap):
        def index(i, pos):
            zz = pos[1] ^ k
            return ((zz & 1) if wrap else zz, 0, 0)

        return pl.BlockSpec((1, rows, quarter), index)

    pieces = pl.pallas_call(
        rs_z_kernel,
        out_shape=[jax.ShapeDtypeStruct((rows, quarter), BF)] * 4,
        grid_spec=pltpu.PrefetchScalarGridSpec(
            num_scalar_prefetch=1,
            grid=(1,),
            in_specs=[zspec(k, w) for w in (False, True, True) for k in range(4)],
            out_specs=[pl.BlockSpec((rows, quarter), lambda i, pos: (0, 0))] * 4,
        ),
        cost_estimate=pl.CostEstimate(
            flops=0, bytes_accessed=16 * rows * quarter * 2, transcendentals=0
        ),
    )(me, *([keep] * 4 + [recv_c] * 4 + [recv_d] * 4))
    gots = [swap(pieces[k], "mp", k) for k in (1, 2, 3)]
    piece = vmem_call(
        rs_last_kernel,
        jax.ShapeDtypeStruct((rows, quarter), BF),
        [pieces[0]] + gots,
        moved=10 * rows * quarter,
    )
    around = [piece] + [swap(piece, "dp", k) for k in (1, 2, 3)]
    return vmem_call(
        functools.partial(rs_place_kernel, splits),
        [jax.ShapeDtypeStruct((rows, width), F32) for width in splits],
        around,
        pos=me,
        scratch=[pltpu.VMEM((rows, cols), F32)],
        moved=6 * rows * cols,
    )


def special(sizes):
    return sizes == (4, 2, 4)


def sum_everywhere(value, sizes):
    if special(sizes):
        for axis, bit in (("fsdp", 1), ("dp", 1), ("dp", 2), ("mp", 1), ("mp", 2)):
            value = value + swap(value, axis, bit)
        return value
    return lax.psum(value, ("dp", "fsdp", "mp"))


def gather_gains(gains, sizes):
    packed = jnp.stack(gains)
    if not special(sizes):
        return lax.all_gather(packed, ("fsdp", "mp"), axis=1, tiled=True)
    width = packed.shape[1]
    index = lax.axis_index("fsdp") * 4 + lax.axis_index("mp")
    whole = lax.dynamic_update_slice(
        jnp.zeros((packed.shape[0], 8 * width), F32), packed.astype(F32), (0, index * width)
    )
    for axis, bit in (("fsdp", 1), ("mp", 1), ("mp", 2)):
        whole = whole + swap(whole, axis, bit)
    return whole


def scatter_plain(left, right, splits):
    grad = weight_grad(left, right).astype(BF)
    grad = lax.psum_scatter(grad, ("fsdp", "mp"), scatter_dimension=0, tiled=True)
    grad = lax.psum(grad, "dp").astype(F32)
    return jnp.split(grad, np.cumsum(splits)[:-1], axis=1)


def shards(
    sizes,
    dec_input,
    enc_output,
    image_pairs,
    text_lengths,
    dec_lengths,
    self_query,
    self_key,
    self_value,
    self_out,
    cross_query,
    cross_key,
    cross_value,
    cross_out,
    ffn_gate,
    ffn_up,
    ffn_down,
    norm_first,
    norm_second,
    norm_third,
    bias_table,
    cotangent,
):
    item_count, length, model_width = dec_input.shape
    enc_len = enc_output.shape[1]
    bucket_count, head_count = bias_table.shape
    head_dim = model_width // head_count
    row_count = item_count * length
    enc_count = item_count * enc_len
    ff = ffn_gate.shape[1]
    me = place()

    gains = gather_gains((norm_first, norm_second, norm_third), sizes).astype(F32)
    gain_first, gain_second, gain_third = gains[0], gains[1], gains[2]
    groups = (
        (cross_key,),
        (cross_value,),
        (self_query, self_key, self_value),
        (self_out, cross_query),
        (cross_out,),
        (ffn_gate, ffn_up),
        (ffn_down,),
    )
    whole = []
    if special(sizes):
        token = None
        for number, group in enumerate(groups):
            full, token = gather_group(me, group, token, number % 2 == 0)
            whole.extend(full)
    else:
        for group in groups:
            for shard in group:
                whole.append(lax.all_gather(shard, ("fsdp", "mp"), axis=0, tiled=True))
    (
        ckey_full,
        cvalue_full,
        query_full,
        key_full,
        value_full,
        out_full,
        cquery_full,
        cout_full,
        gate_full,
        up_full,
        down_full,
    ) = whole

    def scatter(left, right, splits):
        if special(sizes):
            return scatter_group(me, left, right, splits)
        return scatter_plain(left, right, splits)

    positions = jnp.arange(length)
    causal = positions[None, :] <= positions[:, None]
    self_valid = causal[None, None, :, :] & (
        positions[None, None, None, :] < dec_lengths[:, None, None, None]
    )
    enc_slots = jnp.arange(enc_len)
    cross_valid = (enc_slots[None, :] < 2 * PATCHES * image_pairs[:, None]) | (
        enc_slots[None, :] >= 4 * PATCHES
    ) & (enc_slots[None, :] < 4 * PATCHES + text_lengths[:, None])
    cross_valid = cross_valid[:, None, None, :]
    buckets = jnp.asarray(bucket_table(length).reshape(-1))
    onehot = (buckets[:, None] == jnp.arange(bucket_count)[None, :]).astype(F32)
    relative = jnp.dot(onehot, bias_table.astype(F32), precision=lax.Precision.HIGHEST)
    relative = relative.reshape(length, length, head_count).transpose(2, 0, 1)

    def heads(rows, count):
        return rows.astype(BF).reshape(item_count, count, head_count, head_dim)

    inputs = dec_input.astype(F32).reshape(row_count, model_width)
    normed_first = norm_rows(inputs, gain_first).astype(BF)
    queries = heads(matmul(normed_first, query_full), length)
    key_rows = heads(matmul(normed_first, key_full), length)
    value_rows = heads(matmul(normed_first, value_full), length)
    self_mixed, self_lse = attend_forward(queries, key_rows, value_rows, relative, self_valid)
    self_flat = self_mixed.reshape(row_count, model_width)
    first_sum = inputs + matmul(self_flat, out_full)
    normed_second = norm_rows(first_sum, gain_second).astype(BF)
    cross_queries = heads(matmul(normed_second, cquery_full), length)
    enc_rows = enc_output.reshape(enc_count, model_width)
    cross_keys = heads(matmul(enc_rows, ckey_full), enc_len)
    cross_values = heads(matmul(enc_rows, cvalue_full), enc_len)
    cross_mixed, cross_lse = attend_forward(
        cross_queries, cross_keys, cross_values, 0.0, cross_valid
    )
    cross_flat = cross_mixed.reshape(row_count, model_width)
    second_sum = first_sum + matmul(cross_flat, cout_full)
    normed_third = norm_rows(second_sum, gain_third).astype(BF)
    gate_values = matmul(normed_third, gate_full)
    up_values = matmul(normed_third, up_full)
    hidden = gated_unit(gate_values, up_values).astype(BF)
    dec_output = (
        (second_sum + matmul(hidden, down_full)).astype(BF).reshape(item_count, length, model_width)
    )

    out_grad = cotangent.reshape(row_count, model_width)
    hidden_grad = input_grad(out_grad, down_full)
    unused_value, pullback = jax.vjp(gated_unit, gate_values, up_values)
    gate_grad, up_grad = pullback(hidden_grad)
    gu_grad = jnp.concatenate([gate_grad.astype(BF), up_grad.astype(BF)], axis=1)
    ffn_gate_grad, ffn_up_grad = scatter(normed_third, gu_grad, (ff, ff))
    (ffn_down_grad,) = scatter(hidden, out_grad, (model_width,))
    third_normed_grad = input_grad(gu_grad[:, :ff], gate_full) + input_grad(gu_grad[:, ff:], up_full)
    unused_value, pullback = jax.vjp(norm_rows, second_sum, gain_third)
    second_part, norm_third_grad = pullback(third_normed_grad)
    second_grad = cotangent.astype(F32).reshape(row_count, model_width) + second_part
    branch_second = second_grad.astype(BF)
    (cross_out_grad,) = scatter(cross_flat, branch_second, (model_width,))
    cross_mixed_grad = heads(input_grad(branch_second, cout_full), length)
    cq_grad, ck_grad, cv_grad, unused_scores = attend_backward(
        cross_queries, cross_keys, cross_values, 0.0, cross_valid, cross_lse, cross_mixed_grad
    )
    cq_rows = cq_grad.reshape(row_count, model_width)
    ck_rows = ck_grad.reshape(enc_count, model_width)
    cv_rows = cv_grad.reshape(enc_count, model_width)
    (cross_query_grad,) = scatter(normed_second, cq_rows, (model_width,))
    (cross_key_grad,) = scatter(enc_rows, ck_rows, (model_width,))
    (cross_value_grad,) = scatter(enc_rows, cv_rows, (model_width,))
    enc_output_grad = (input_grad(ck_rows, ckey_full) + input_grad(cv_rows, cvalue_full)).reshape(
        item_count, enc_len, model_width
    )
    second_normed_grad = input_grad(cq_rows, cquery_full)
    unused_value, pullback = jax.vjp(norm_rows, first_sum, gain_second)
    first_part, norm_second_grad = pullback(second_normed_grad)
    first_grad = second_grad + first_part
    branch_first = first_grad.astype(BF)
    (self_out_grad,) = scatter(self_flat, branch_first, (model_width,))
    self_mixed_grad = heads(input_grad(branch_first, out_full), length)
    q_grad, k_grad, v_grad, self_score_grad = attend_backward(
        queries, key_rows, value_rows, relative, self_valid, self_lse, self_mixed_grad
    )
    score_total = (
        jnp.sum(self_score_grad.astype(F32), axis=0)
        .transpose(1, 2, 0)
        .reshape(length * length, head_count)
    )
    table_part = lax.dot_general(
        onehot, score_total, (((0,), (0,)), ((), ())), precision=lax.Precision.HIGHEST
    )
    q_rows = q_grad.reshape(row_count, model_width)
    k_rows = k_grad.reshape(row_count, model_width)
    v_rows = v_grad.reshape(row_count, model_width)
    qkv_rows = jnp.concatenate([q_rows, k_rows, v_rows], axis=1)
    self_query_grad, self_key_grad, self_value_grad = scatter(
        normed_first, qkv_rows, (model_width,) * 3
    )
    first_normed_grad = (
        input_grad(q_rows, query_full)
        + input_grad(k_rows, key_full)
        + input_grad(v_rows, value_full)
    )
    unused_value, pullback = jax.vjp(norm_rows, inputs, gain_first)
    input_part, norm_first_grad = pullback(first_normed_grad)
    dec_input_grad = (first_grad + input_part).reshape(item_count, length, model_width)

    small = jnp.concatenate(
        [norm_first_grad, norm_second_grad, norm_third_grad, table_part.reshape(-1)]
    )
    small = sum_everywhere(small, sizes)
    gain_width = norm_first.shape[0]
    start = (lax.axis_index("fsdp") * sizes[2] + lax.axis_index("mp")) * gain_width
    gain_grads = [
        lax.dynamic_slice_in_dim(small, k * model_width + start, gain_width) for k in range(3)
    ]
    bias_table_grad = small[3 * model_width :].reshape(bucket_count, head_count)
    return (
        dec_output,
        dec_input_grad,
        enc_output_grad,
        self_query_grad,
        self_key_grad,
        self_value_grad,
        self_out_grad,
        cross_query_grad,
        cross_key_grad,
        cross_value_grad,
        cross_out_grad,
        ffn_gate_grad,
        ffn_up_grad,
        ffn_down_grad,
        gain_grads[0],
        gain_grads[1],
        gain_grads[2],
        bias_table_grad,
    )


def solution(mesh):
    items = P(("dp", "fsdp", "mp"), None, None)
    item_numbers = P(("dp", "fsdp", "mp"))
    weight = P(("fsdp", "mp"), None)
    gain = P(("fsdp", "mp"))
    sizes = (mesh.shape["dp"], mesh.shape["fsdp"], mesh.shape["mp"])
    return jax.shard_map(
        functools.partial(shards, sizes),
        mesh=mesh,
        in_specs=(items, items)
        + (item_numbers,) * 3
        + (weight,) * 11
        + (gain,) * 3
        + (P(), items),
        out_specs=(items,) * 3 + (weight,) * 11 + (gain,) * 3 + (P(),),
        check_vma=False,
    )
```

```python
import functools
import math

import jax
import jax.numpy as jnp
import numpy as np
from jax import lax
from jax.experimental import pallas as pl
from jax.experimental.pallas import tpu as pltpu
from jax.sharding import PartitionSpec as P

PATCHES = 256
EPSILON = 1e-06
MASKED = -1000000000.0
GELU_COEF = 0.044715
BF = jnp.bfloat16
F32 = jnp.float32
ANY = pl.ANY


def bucket_table(length):
    rows_index = np.arange(length)[:, None]
    cols_index = np.arange(length)[None, :]
    distance = np.maximum(rows_index - cols_index, 0)
    spread = np.floor(np.log(np.maximum(distance, 1) / 16.0) / np.log(8.0) * 16.0)
    far_bucket = np.minimum(16.0 + spread, 31.0)
    return np.where(distance < 16, distance, far_bucket).astype(np.int32)


def norm_rows(values, gain):
    return values * lax.rsqrt(jnp.mean(values * values, axis=-1, keepdims=True) + EPSILON) * gain


def gelu_tanh(values):
    return (
        0.5
        * values
        * (
            1.0
            + jnp.tanh(math.sqrt(2.0 / math.pi) * (values + GELU_COEF * values * values * values))
        )
    )


def gated_unit(gate_values, up_values):
    return gelu_tanh(gate_values) * up_values


def matmul(left, right):
    return jnp.dot(left, right, preferred_element_type=F32)


def weight_grad(left, right):
    return lax.dot_general(left, right, (((0,), (0,)), ((), ())), preferred_element_type=F32)


def input_grad(upstream, weight):
    return lax.dot_general(upstream, weight, (((1,), (1,)), ((), ())), preferred_element_type=F32)


NT=(((1,),(1,)),((),()))
TN=(((0,),(0,)),((),()))

def dot(a,b,dims=(((1,),(0,)),((),()))):
    return lax.dot_general(a,b,dims,preferred_element_type=F32)

def twice(block):
    low = lax.broadcasted_iota(jnp.int32, block.shape, 1) < block.shape[1]//2
    zero = jnp.zeros_like(block)
    return jnp.concatenate([jnp.where(low, block, zero), jnp.where(low, zero, block)], axis=0)

def once(rows):
    half = rows.shape[0]//2
    low = lax.broadcasted_iota(jnp.int32, (half, rows.shape[1]), 1) < rows.shape[1]//2
    return jnp.where(low, rows[:half], rows[half:])

def cross_fwd_kernel(pairs, texts, q_ref, k_ref, v_ref, o_ref, lse_ref):
    item = pl.program_id(0)
    slots = k_ref.shape[0]
    pos = lax.broadcasted_iota(jnp.int32, (1, slots), 1)
    valid = (pos < 2*PATCHES*pairs[item]) | ((pos >= 4*PATCHES) & (pos < 4*PATCHES + texts[item]))
    pen = jnp.where(valid, 0.0, MASKED)
    for t in range(q_ref.shape[1]//128):
        cols = slice(128*t, 128*t+128)
        q2 = twice(q_ref[:, cols])
        s = dot(q2, k_ref[:, cols], NT) + pen
        m = jnp.max(s, axis=1, keepdims=True)
        p = jnp.exp(s - m)
        total = jnp.sum(p, axis=1, keepdims=True)
        p = (p * (1.0/total)).astype(BF)
        o_ref[:, cols] = once(dot(p, v_ref[:, cols])).astype(BF)
        lse = m + jnp.log(total)
        lse_ref[t] = jnp.transpose(jnp.broadcast_to(lse, (lse.shape[0], 128)))[:1]

def cross_bwd_kernel(pairs, texts, q_ref, k_ref, v_ref, lse_ref, do_ref, dq_ref, dk_ref, dv_ref):
    item = pl.program_id(0)
    slots = k_ref.shape[0]
    pos = lax.broadcasted_iota(jnp.int32, (slots, 1), 0)
    valid = (pos < 2*PATCHES*pairs[item]) | ((pos >= 4*PATCHES) & (pos < 4*PATCHES + texts[item]))
    pen = jnp.where(valid, 0.0, MASKED)
    for t in range(q_ref.shape[1]//128):
        cols = slice(128*t, 128*t+128)
        q2 = twice(q_ref[:, cols])
        do2 = twice(do_ref[:, cols])
        s = dot(k_ref[:, cols], q2, NT)
        p = jnp.exp(s + (pen - lse_ref[t]))
        dp = dot(v_ref[:, cols], do2, NT)
        delta = jnp.sum(p*dp, axis=0, keepdims=True)
        ds = (p*(dp-delta)).astype(BF)
        dv_ref[:, cols] = dot(p.astype(BF), do2).astype(BF)
        dk_ref[:, cols] = dot(ds, q2).astype(BF)
        dq_ref[:, cols] = once(dot(ds, k_ref[:, cols], TN)).astype(BF)

def cross_specs(slots, length, width, n):
    small = pl.BlockSpec((length, width), lambda i, j, *_: (i, j))
    big = pl.BlockSpec((slots, width), lambda i, j, *_: (i, j))
    lse = pl.BlockSpec((width//128, 1, 256), lambda i, j, *_: (i*n+j, 0, 0))
    return small, big, lse

def cross_fwd(pairs, texts, q, k, v, width=512):
    items = pairs.shape[0]; slots = k.shape[0]//items; length = q.shape[0]//items; n = q.shape[1]//width
    small, big, lse = cross_specs(slots, length, width, n)
    return pl.pallas_call(cross_fwd_kernel, grid_spec=pltpu.PrefetchScalarGridSpec(num_scalar_prefetch=2, grid=(items, n),
        in_specs=[small, big, big], out_specs=[small, lse]),
        out_shape=[jax.ShapeDtypeStruct(q.shape, BF), jax.ShapeDtypeStruct((items*q.shape[1]//128, 1, 256), F32)],
        cost_estimate=pl.CostEstimate(flops=int(items*q.shape[1]//128*2*2*256*256*slots), bytes_accessed=2*k.size*2+q.size*4, transcendentals=0))(pairs, texts, q, k, v)

def cross_bwd(pairs, texts, q, k, v, lse, do, width=256):
    items = pairs.shape[0]; slots = k.shape[0]//items; length = q.shape[0]//items; n = q.shape[1]//width
    small, big, lspec = cross_specs(slots, length, width, n)
    return pl.pallas_call(cross_bwd_kernel, grid_spec=pltpu.PrefetchScalarGridSpec(num_scalar_prefetch=2, grid=(items, n),
        in_specs=[small, big, big, lspec, small], out_specs=[small, big, big]),
        out_shape=[jax.ShapeDtypeStruct(q.shape, BF), jax.ShapeDtypeStruct(k.shape, BF), jax.ShapeDtypeStruct(k.shape, BF)],
        cost_estimate=pl.CostEstimate(flops=int(items*q.shape[1]//128*5*2*256*256*slots), bytes_accessed=4*k.size*2+q.size*6, transcendentals=0))(pairs, texts, q, k, v, lse, do)

def self_fwd_kernel(lens, q_ref, k_ref, v_ref, bias_ref, o_ref, lse_ref):
    item = pl.program_id(0)
    length = k_ref.shape[0]
    key = lax.broadcasted_iota(jnp.int32, (length, 256), 0)
    query = lax.broadcasted_iota(jnp.int32, (length, 256), 1) & (length-1)
    valid = (key <= query) & (key < lens[item])
    for t in range(q_ref.shape[1]//128):
        cols = slice(128*t, 128*t+128)
        q2 = twice(q_ref[:, cols])
        s = jnp.where(valid, dot(k_ref[:, cols], q2, NT) + bias_ref[t], MASKED)
        m = jnp.max(s, axis=0, keepdims=True)
        p = jnp.exp(s - m)
        total = jnp.sum(p, axis=0, keepdims=True)
        p = (p * (1.0/total)).astype(BF)
        o_ref[:, cols] = once(dot(p, v_ref[:, cols], TN)).astype(BF)
        lse_ref[t] = m + jnp.log(total)

def self_bwd_kernel(lens, q_ref, k_ref, v_ref, bias_ref, lse_ref, do_ref, dq_ref, dk_ref, dv_ref, sum_ref):
    item = pl.program_id(1)
    length = k_ref.shape[0]
    key = lax.broadcasted_iota(jnp.int32, (length, 256), 0)
    query = lax.broadcasted_iota(jnp.int32, (length, 256), 1) & (length-1)
    valid = (key <= query) & (key < lens[item])
    @pl.when(item == 0)
    def _(): sum_ref[...] = jnp.zeros_like(sum_ref)
    for t in range(q_ref.shape[1]//128):
        cols = slice(128*t, 128*t+128)
        q2 = twice(q_ref[:, cols])
        do2 = twice(do_ref[:, cols])
        s = dot(k_ref[:, cols], q2, NT) + bias_ref[t]
        p = jnp.where(valid, jnp.exp(s - lse_ref[t]), 0.0)
        dp = dot(v_ref[:, cols], do2, NT)
        delta = jnp.sum(p*dp, axis=0, keepdims=True)
        ds = (p*(dp-delta)).astype(BF)
        dv_ref[:, cols] = dot(p.astype(BF), do2).astype(BF)
        dk_ref[:, cols] = dot(ds, q2).astype(BF)
        dq_ref[:, cols] = once(dot(ds, k_ref[:, cols], TN)).astype(BF)
        sum_ref[t] += ds.astype(F32)

def self_fwd(lens, q, k, v, bias, width=512):
    items = lens.shape[0]; length = q.shape[0]//items; n = q.shape[1]//width
    small, _, lse = cross_specs(length, length, width, n)
    return pl.pallas_call(self_fwd_kernel, grid_spec=pltpu.PrefetchScalarGridSpec(num_scalar_prefetch=1, grid=(items, n),
        in_specs=[small]*3+[pl.BlockSpec((width//128, length, 256), lambda i, j, *_: (j,0,0))], out_specs=[small, lse]),
        out_shape=[jax.ShapeDtypeStruct(q.shape, BF), jax.ShapeDtypeStruct((items*q.shape[1]//128, 1, 256), F32)],
        cost_estimate=pl.CostEstimate(flops=int(items*q.shape[1]//128*2*2*256*256*length), bytes_accessed=q.size*8, transcendentals=0))(lens, q, k, v, bias)

def self_bwd(lens, q, k, v, bias, lse, do, width=512):
    items = lens.shape[0]; length = q.shape[0]//items; n = q.shape[1]//width
    small = pl.BlockSpec((length, width), lambda j, i, *_: (i, j))
    lspec = pl.BlockSpec((width//128, 1, 256), lambda j, i, *_: (i*n+j, 0, 0))
    bspec = pl.BlockSpec((width//128, length, 256), lambda j, i, *_: (j,0,0))
    return pl.pallas_call(self_bwd_kernel, grid_spec=pltpu.PrefetchScalarGridSpec(num_scalar_prefetch=1, grid=(n, items),
        in_specs=[small]*3+[bspec, lspec, small], out_specs=[small]*3+[bspec]),
        out_shape=[jax.ShapeDtypeStruct(q.shape, BF)]*3+[jax.ShapeDtypeStruct(bias.shape, F32)],
        cost_estimate=pl.CostEstimate(flops=int(items*q.shape[1]//128*5*2*256*256*length), bytes_accessed=q.size*14, transcendentals=0))(lens, q, k, v, bias, lse, do)


def swap(value, axis, bit):
    size = lax.axis_size(axis)
    return lax.ppermute(value, axis, [(i, i ^ bit) for i in range(size)])


def place():
    return jnp.stack(
        [lax.axis_index("fsdp"), lax.axis_index("mp"), lax.axis_index("dp")]
    ).astype(jnp.int32)


def assemble_kernel(rows, cols, splits, me, *refs):
    pieces, outs = refs[:10], refs[10 : 10 + len(splits)]
    buf, in_sem, out_sem = refs[10 + len(splits) :]
    c, z, p = me[0], me[1], me[2]
    quarter = cols // 4
    blocks = []
    n = 0
    for other in range(2):
        for zr in range(4):
            row = pl.multiple_of(((c ^ other) * 4 + (z ^ zr)) * rows, rows)
            copies = []
            if zr == 0:
                copies.append(
                    pltpu.make_async_copy(
                        pieces[5 * other], buf.at[pl.ds(row, rows), :], in_sem.at[n]
                    )
                )
                n += 1
            else:
                for j in range(4):
                    col = pl.multiple_of((p ^ j) * quarter, 128)
                    copies.append(
                        pltpu.make_async_copy(
                            pieces[5 * other + 1 + j].at[zr - 1],
                            buf.at[pl.ds(row, rows), pl.ds(col, quarter)],
                            in_sem.at[n],
                        )
                    )
                    n += 1
            for copy in copies:
                copy.start()
            blocks.append((row, copies))
    pending = []
    n = 0
    for row, copies in blocks:
        for copy in copies:
            copy.wait()
        start = 0
        for out, width in zip(outs, splits):
            copy = pltpu.make_async_copy(
                buf.at[pl.ds(row, rows), pl.ds(start, width)],
                out.at[pl.ds(row, rows), :],
                out_sem.at[n],
            )
            copy.start()
            pending.append(copy)
            start += width
            n += 1
    for copy in pending:
        copy.wait()


def assemble(me, pieces, rows, splits):
    cols = sum(splits)
    total = 8 * rows
    return pl.pallas_call(
        functools.partial(assemble_kernel, rows, cols, splits),
        out_shape=[jax.ShapeDtypeStruct((total, width), BF) for width in splits],
        in_specs=[pl.BlockSpec(memory_space=pltpu.SMEM)] + [pl.BlockSpec(memory_space=ANY)] * 10,
        out_specs=[pl.BlockSpec(memory_space=ANY)] * len(splits),
        scratch_shapes=[
            pltpu.VMEM((total, cols), BF),
            pltpu.SemaphoreType.DMA((26,)),
            pltpu.SemaphoreType.DMA((8 * len(splits),)),
        ],
        cost_estimate=pl.CostEstimate(
            flops=0, bytes_accessed=4 * total * cols, transcendentals=0
        ),
    )(me, *pieces)


def gather_group(me, shards, token, flip):
    splits = tuple(shard.shape[1] for shard in shards)
    own = shards[0] if len(shards) == 1 else jnp.concatenate(shards, axis=1)
    rows, cols = own.shape
    quarter = cols // 4
    part = lax.dynamic_slice_in_dim(own, me[2] * quarter, quarter, axis=1)
    if token is not None:
        part, token = lax.optimization_barrier((part, token))
    along_z = [swap(part, "mp", bit) for bit in (1, 2, 3)]
    first, second = (1, 2) if flip else (2, 1)
    a0 = jnp.stack(along_z)
    hop = swap(a0, "dp", first)
    side = swap(a0, "dp", second)
    far = swap(hop, "dp", second)
    planes = [a0, hop, side, far] if flip else [a0, side, hop, far]
    mine = [own] + planes
    theirs = [swap(piece, "fsdp", 1) for piece in mine]
    full = assemble(me, mine + theirs, rows, splits)
    return full, tuple(along_z)


def rs_add_kernel(pos, ka_s, ka_k, kb_s, kb_k, ra_s, ra_k, rb_s, rb_k, sa, sb, keep):
    sa[...] = (ka_s[...].astype(F32) + ra_s[...].astype(F32)).astype(BF)
    sb[...] = (kb_s[...].astype(F32) + rb_s[...].astype(F32)).astype(BF)
    keep[0] = (ka_k[...].astype(F32) + ra_k[...].astype(F32)).astype(BF)
    keep[1] = (kb_k[...].astype(F32) + rb_k[...].astype(F32)).astype(BF)


def rs_z_kernel(pos, *refs):
    keeps, ras, rbs, outs = refs[:4], refs[4:8], refs[8:12], refs[12:]
    z = pos[1]
    for k in range(4):
        low = (z ^ k) < 2
        recv = jnp.where(low, ras[k][0].astype(F32), rbs[k][0].astype(F32))
        outs[k][...] = (keeps[k][0].astype(F32) + recv).astype(BF)


def rs_last_kernel(own, r1, r2, r3, out):
    out[...] = (
        (own[...].astype(F32) + r1[...].astype(F32)) + (r2[...].astype(F32) + r3[...].astype(F32))
    ).astype(BF)


def rs_place_kernel(splits, pos, p0, p1, p2, p3, *refs):
    outs, buf = refs[:-1], refs[-1]
    quarter = p0.shape[1]
    z, p = pos[1], pos[2]
    for j, piece in enumerate((p0, p1, p2, p3)):
        q = p ^ j
        x, y = q & 1, q >> 1
        col = jnp.where(z < 2, x * 2 + y, q) * quarter
        buf[:, pl.ds(pl.multiple_of(col, 128), quarter)] = piece[...].astype(F32)
    start = 0
    for out, width in zip(outs, splits):
        out[...] = buf[:, start : start + width]
        start += width


def vmem_call(kernel, outs, ins, pos=None, scratch=(), moved=0):
    specs = [pl.BlockSpec(memory_space=pltpu.VMEM)] * len(ins)
    args = list(ins)
    if pos is not None:
        specs = [pl.BlockSpec(memory_space=pltpu.SMEM)] + specs
        args = [pos] + args
    return pl.pallas_call(
        kernel,
        out_shape=outs,
        in_specs=specs,
        out_specs=jax.tree.map(lambda _: pl.BlockSpec(memory_space=pltpu.VMEM), outs),
        scratch_shapes=list(scratch),
        cost_estimate=pl.CostEstimate(flops=0, bytes_accessed=moved, transcendentals=0),
    )(*args)


def scatter_group(me, left, right, splits):
    total, cols = left.shape[1], right.shape[1]
    half, rows, quarter = total // 2, total // 8, cols // 4
    c, x, y = me[0], me[2] & 1, me[2] >> 1
    theirs = lax.dynamic_slice_in_dim(left, (1 - c) * half, half, axis=1)
    mine = lax.dynamic_slice_in_dim(left, c * half, half, axis=1)
    sent = weight_grad(theirs, right).astype(BF)
    got = swap(sent, "fsdp", 1)
    got, mine = lax.optimization_barrier((got, mine))
    kept = (weight_grad(mine, right) + got.astype(F32)).astype(BF)
    return scatter_tail(me, kept, splits)


def scatter_tail(me, kept, splits):
    half, cols = kept.shape
    rows, quarter = half // 4, cols // 4
    c, x, y = me[0], me[2] & 1, me[2] >> 1
    two = 2 * rows
    send_a = lax.dynamic_slice(kept, (0, (1 - x) * 2 * quarter), (two, 2 * quarter))
    send_b = lax.dynamic_slice(kept, (two, (1 - y) * 2 * quarter), (two, 2 * quarter))
    recv_a = swap(send_a, "dp", 1)
    recv_b = swap(send_b, "dp", 2)
    steps = 4 if rows % 64 == 0 else 2
    block = two // steps

    def at(kind):
        def index(i, pos):
            px, py = pos[2] & 1, pos[2] >> 1
            return {
                "ka_s": (i, px * 2 + 1 - py),
                "ka_k": (i, px * 2 + py),
                "kb_s": (steps + i, py * 2 + 1 - px),
                "kb_k": (steps + i, py * 2 + px),
                "ra_s": (i, 1 - py),
                "ra_k": (i, py),
                "rb_s": (i, 1 - px),
                "rb_k": (i, px),
            }[kind]

        return pl.BlockSpec((block, quarter), index)

    send_c, send_d, keep = pl.pallas_call(
        rs_add_kernel,
        out_shape=[
            jax.ShapeDtypeStruct((two, quarter), BF),
            jax.ShapeDtypeStruct((two, quarter), BF),
            jax.ShapeDtypeStruct((2, two, quarter), BF),
        ],
        grid_spec=pltpu.PrefetchScalarGridSpec(
            num_scalar_prefetch=1,
            grid=(steps,),
            in_specs=[
                at(k) for k in ("ka_s", "ka_k", "kb_s", "kb_k", "ra_s", "ra_k", "rb_s", "rb_k")
            ],
            out_specs=[
                pl.BlockSpec((block, quarter), lambda i, pos: (i, 0)),
                pl.BlockSpec((block, quarter), lambda i, pos: (i, 0)),
                pl.BlockSpec((2, block, quarter), lambda i, pos: (0, i, 0)),
            ],
        ),
        cost_estimate=pl.CostEstimate(
            flops=0, bytes_accessed=6 * half * quarter * 2, transcendentals=0
        ),
    )(me, kept, kept, kept, kept, recv_a, recv_a, recv_b, recv_b)
    recv_c = swap(send_c, "dp", 2).reshape(2, rows, quarter)
    recv_d = swap(send_d, "dp", 1).reshape(2, rows, quarter)
    keep = keep.reshape(4, rows, quarter)

    def zspec(k, wrap):
        def index(i, pos):
            zz = pos[1] ^ k
            return ((zz & 1) if wrap else zz, 0, 0)

        return pl.BlockSpec((1, rows, quarter), index)

    pieces = pl.pallas_call(
        rs_z_kernel,
        out_shape=[jax.ShapeDtypeStruct((rows, quarter), BF)] * 4,
        grid_spec=pltpu.PrefetchScalarGridSpec(
            num_scalar_prefetch=1,
            grid=(1,),
            in_specs=[zspec(k, w) for w in (False, True, True) for k in range(4)],
            out_specs=[pl.BlockSpec((rows, quarter), lambda i, pos: (0, 0))] * 4,
        ),
        cost_estimate=pl.CostEstimate(
            flops=0, bytes_accessed=16 * rows * quarter * 2, transcendentals=0
        ),
    )(me, *([keep] * 4 + [recv_c] * 4 + [recv_d] * 4))
    gots = [swap(pieces[k], "mp", k) for k in (1, 2, 3)]
    piece = vmem_call(
        rs_last_kernel,
        jax.ShapeDtypeStruct((rows, quarter), BF),
        [pieces[0]] + gots,
        moved=10 * rows * quarter,
    )
    around = [piece] + [swap(piece, "dp", k) for k in (1, 2, 3)]
    return vmem_call(
        functools.partial(rs_place_kernel, splits),
        [jax.ShapeDtypeStruct((rows, width), F32) for width in splits],
        around,
        pos=me,
        scratch=[pltpu.VMEM((rows, cols), F32)],
        moved=6 * rows * cols,
    )


def special(sizes):
    return sizes == (4, 2, 4)


def sum_everywhere(value, sizes):
    if special(sizes):
        for axis, bit in (("fsdp", 1), ("dp", 1), ("dp", 2), ("mp", 1), ("mp", 2)):
            value = value + swap(value, axis, bit)
        return value
    return lax.psum(value, ("dp", "fsdp", "mp"))


def gather_gains(gains, sizes):
    packed = jnp.stack(gains)
    if not special(sizes):
        return lax.all_gather(packed, ("fsdp", "mp"), axis=1, tiled=True)
    width = packed.shape[1]
    index = lax.axis_index("fsdp") * 4 + lax.axis_index("mp")
    whole = lax.dynamic_update_slice(
        jnp.zeros((packed.shape[0], 8 * width), F32), packed.astype(F32), (0, index * width)
    )
    for axis, bit in (("fsdp", 1), ("mp", 1), ("mp", 2)):
        whole = whole + swap(whole, axis, bit)
    return whole


def scatter_plain(left, right, splits):
    grad = weight_grad(left, right).astype(BF)
    grad = lax.psum_scatter(grad, ("fsdp", "mp"), scatter_dimension=0, tiled=True)
    grad = lax.psum(grad, "dp").astype(F32)
    return jnp.split(grad, np.cumsum(splits)[:-1], axis=1)


def shards(
    sizes,
    dec_input,
    enc_output,
    image_pairs,
    text_lengths,
    dec_lengths,
    self_query,
    self_key,
    self_value,
    self_out,
    cross_query,
    cross_key,
    cross_value,
    cross_out,
    ffn_gate,
    ffn_up,
    ffn_down,
    norm_first,
    norm_second,
    norm_third,
    bias_table,
    cotangent,
):
    item_count, length, model_width = dec_input.shape
    enc_len = enc_output.shape[1]
    bucket_count, head_count = bias_table.shape
    row_count = item_count * length
    enc_count = item_count * enc_len
    ff = ffn_gate.shape[1]
    me = place()

    gains = gather_gains((norm_first, norm_second, norm_third), sizes).astype(F32)
    gain_first, gain_second, gain_third = gains[0], gains[1], gains[2]
    groups = (
        (cross_key,),
        (cross_value,),
        (self_query, self_key, self_value),
        (self_out, cross_query),
        (cross_out,),
        (ffn_gate, ffn_up),
        (ffn_down,),
    )
    whole = []
    if special(sizes):
        token = None
        for number, group in enumerate(groups):
            full, token = gather_group(me, group, token, number % 2 == 0)
            whole.extend(full)
    else:
        for group in groups:
            for shard in group:
                whole.append(lax.all_gather(shard, ("fsdp", "mp"), axis=0, tiled=True))
    (
        ckey_full,
        cvalue_full,
        query_full,
        key_full,
        value_full,
        out_full,
        cquery_full,
        cout_full,
        gate_full,
        up_full,
        down_full,
    ) = whole

    def scatter(left, right, splits):
        if special(sizes):
            return scatter_group(me, left, right, splits)
        return scatter_plain(left, right, splits)

    buckets = jnp.asarray(bucket_table(length).T.reshape(-1))
    onehot = (buckets[None, :] == jnp.arange(bucket_count)[:, None]).astype(F32)
    relative = lax.dot_general(
        bias_table.astype(F32), onehot, (((0,), (0,)), ((), ())), precision=lax.Precision.HIGHEST
    )
    relative = relative.reshape(head_count // 2, 2, length, length).transpose(0, 2, 1, 3)
    relative = relative.reshape(head_count // 2, length, 2 * length)

    inputs = dec_input.astype(F32).reshape(row_count, model_width)
    normed_first = norm_rows(inputs, gain_first).astype(BF)
    queries = matmul(normed_first, query_full).astype(BF)
    key_rows = matmul(normed_first, key_full).astype(BF)
    value_rows = matmul(normed_first, value_full).astype(BF)
    self_flat, self_lse = self_fwd(dec_lengths, queries, key_rows, value_rows, relative)
    first_sum = inputs + matmul(self_flat, out_full)
    normed_second = norm_rows(first_sum, gain_second).astype(BF)
    cross_queries = matmul(normed_second, cquery_full).astype(BF)
    enc_rows = enc_output.reshape(enc_count, model_width)
    cross_keys = matmul(enc_rows, ckey_full).astype(BF)
    cross_values = matmul(enc_rows, cvalue_full).astype(BF)
    cross_flat, cross_lse = cross_fwd(
        image_pairs, text_lengths, cross_queries, cross_keys, cross_values
    )
    second_sum = first_sum + matmul(cross_flat, cout_full)
    normed_third = norm_rows(second_sum, gain_third).astype(BF)
    gate_values = matmul(normed_third, gate_full)
    up_values = matmul(normed_third, up_full)
    hidden = gated_unit(gate_values, up_values).astype(BF)
    dec_output = (
        (second_sum + matmul(hidden, down_full)).astype(BF).reshape(item_count, length, model_width)
    )

    out_grad = cotangent.reshape(row_count, model_width)
    hidden_grad = input_grad(out_grad, down_full)
    unused_value, pullback = jax.vjp(gated_unit, gate_values, up_values)
    gate_grad, up_grad = pullback(hidden_grad)
    gu_grad = jnp.concatenate([gate_grad.astype(BF), up_grad.astype(BF)], axis=1)
    ffn_gate_grad, ffn_up_grad = scatter(normed_third, gu_grad, (ff, ff))
    (ffn_down_grad,) = scatter(hidden, out_grad, (model_width,))
    third_normed_grad = input_grad(gu_grad[:, :ff], gate_full) + input_grad(gu_grad[:, ff:], up_full)
    unused_value, pullback = jax.vjp(norm_rows, second_sum, gain_third)
    second_part, norm_third_grad = pullback(third_normed_grad)
    second_grad = cotangent.astype(F32).reshape(row_count, model_width) + second_part
    branch_second = second_grad.astype(BF)
    (cross_out_grad,) = scatter(cross_flat, branch_second, (model_width,))
    cross_mixed_grad = input_grad(branch_second, cout_full).astype(BF)
    cq_rows, ck_rows, cv_rows = cross_bwd(
        image_pairs,
        text_lengths,
        cross_queries,
        cross_keys,
        cross_values,
        cross_lse,
        cross_mixed_grad,
    )
    (cross_query_grad,) = scatter(normed_second, cq_rows, (model_width,))
    (cross_key_grad,) = scatter(enc_rows, ck_rows, (model_width,))
    (cross_value_grad,) = scatter(enc_rows, cv_rows, (model_width,))
    enc_output_grad = (input_grad(ck_rows, ckey_full) + input_grad(cv_rows, cvalue_full)).reshape(
        item_count, enc_len, model_width
    )
    second_normed_grad = input_grad(cq_rows, cquery_full)
    unused_value, pullback = jax.vjp(norm_rows, first_sum, gain_second)
    first_part, norm_second_grad = pullback(second_normed_grad)
    first_grad = second_grad + first_part
    branch_first = first_grad.astype(BF)
    (self_out_grad,) = scatter(self_flat, branch_first, (model_width,))
    self_mixed_grad = input_grad(branch_first, out_full).astype(BF)
    q_rows, k_rows, v_rows, score_total = self_bwd(
        dec_lengths, queries, key_rows, value_rows, relative, self_lse, self_mixed_grad
    )
    score_total = score_total.reshape(head_count // 2, length, 2, length).transpose(0, 2, 1, 3)
    table_part = lax.dot_general(
        onehot,
        score_total.reshape(head_count, length * length),
        (((1,), (1,)), ((), ())),
        precision=lax.Precision.HIGHEST,
    )
    qkv_rows = jnp.concatenate([q_rows, k_rows, v_rows], axis=1)
    self_query_grad, self_key_grad, self_value_grad = scatter(
        normed_first, qkv_rows, (model_width,) * 3
    )
    first_normed_grad = (
        input_grad(q_rows, query_full)
        + input_grad(k_rows, key_full)
        + input_grad(v_rows, value_full)
    )
    unused_value, pullback = jax.vjp(norm_rows, inputs, gain_first)
    input_part, norm_first_grad = pullback(first_normed_grad)
    dec_input_grad = (first_grad + input_part).reshape(item_count, length, model_width)

    small = jnp.concatenate(
        [norm_first_grad, norm_second_grad, norm_third_grad, table_part.reshape(-1)]
    )
    small = sum_everywhere(small, sizes)
    gain_width = norm_first.shape[0]
    start = (lax.axis_index("fsdp") * sizes[2] + lax.axis_index("mp")) * gain_width
    gain_grads = [
        lax.dynamic_slice_in_dim(small, k * model_width + start, gain_width) for k in range(3)
    ]
    bias_table_grad = small[3 * model_width :].reshape(bucket_count, head_count)
    return (
        dec_output,
        dec_input_grad,
        enc_output_grad,
        self_query_grad,
        self_key_grad,
        self_value_grad,
        self_out_grad,
        cross_query_grad,
        cross_key_grad,
        cross_value_grad,
        cross_out_grad,
        ffn_gate_grad,
        ffn_up_grad,
        ffn_down_grad,
        gain_grads[0],
        gain_grads[1],
        gain_grads[2],
        bias_table_grad,
    )


def solution(mesh):
    items = P(("dp", "fsdp", "mp"), None, None)
    item_numbers = P(("dp", "fsdp", "mp"))
    weight = P(("fsdp", "mp"), None)
    gain = P(("fsdp", "mp"))
    sizes = (mesh.shape["dp"], mesh.shape["fsdp"], mesh.shape["mp"])
    return jax.shard_map(
        functools.partial(shards, sizes),
        mesh=mesh,
        in_specs=(items, items)
        + (item_numbers,) * 3
        + (weight,) * 11
        + (gain,) * 3
        + (P(), items),
        out_specs=(items,) * 3 + (weight,) * 11 + (gain,) * 3 + (P(),),
        check_vma=False,
    )
```

```python
import functools
import math

import jax
import jax.numpy as jnp
import numpy as np
from jax import lax
from jax.experimental import pallas as pl
from jax.experimental.pallas import tpu as pltpu
from jax.sharding import PartitionSpec as P

PATCHES = 256
EPSILON = 1e-06
MASKED = -1000000000.0
GELU_COEF = 0.044715
BF = jnp.bfloat16
F32 = jnp.float32
ANY = pl.ANY


def bucket_table(length):
    rows_index = np.arange(length)[:, None]
    cols_index = np.arange(length)[None, :]
    distance = np.maximum(rows_index - cols_index, 0)
    spread = np.floor(np.log(np.maximum(distance, 1) / 16.0) / np.log(8.0) * 16.0)
    far_bucket = np.minimum(16.0 + spread, 31.0)
    return np.where(distance < 16, distance, far_bucket).astype(np.int32)


def norm_rows(values, gain):
    return values * lax.rsqrt(jnp.mean(values * values, axis=-1, keepdims=True) + EPSILON) * gain


def gelu_tanh(values):
    return (
        0.5
        * values
        * (
            1.0
            + jnp.tanh(math.sqrt(2.0 / math.pi) * (values + GELU_COEF * values * values * values))
        )
    )


def gated_unit(gate_values, up_values):
    return gelu_tanh(gate_values) * up_values


def matmul(left, right):
    return jnp.dot(left, right, preferred_element_type=F32)


def weight_grad(left, right):
    return lax.dot_general(left, right, (((0,), (0,)), ((), ())), preferred_element_type=F32)


def input_grad(upstream, weight):
    return lax.dot_general(upstream, weight, (((1,), (1,)), ((), ())), preferred_element_type=F32)


NT = (((1,), (1,)), ((), ()))
TN = (((0,), (0,)), ((), ()))
NN = (((1,), (0,)), ((), ()))
PAIR = 128
STRIPE = 256


def dot(left, right, dims=NN):
    return lax.dot_general(left, right, dims, preferred_element_type=F32)


def twice(block):
    low = lax.broadcasted_iota(jnp.int32, block.shape, 1) < block.shape[1] // 2
    zero = jnp.zeros_like(block)
    return jnp.concatenate([jnp.where(low, block, zero), jnp.where(low, zero, block)], axis=0)


def once(rows):
    half = rows.shape[0] // 2
    low = lax.broadcasted_iota(jnp.int32, (half, rows.shape[1]), 1) < rows.shape[1] // 2
    return jnp.where(low, rows[:half], rows[half:])


def cross_penalty(shape, axis, pairs, texts, item):
    slot = lax.broadcasted_iota(jnp.int32, shape, axis)
    valid = (slot < 2 * PATCHES * pairs[item]) | (
        (slot >= 4 * PATCHES) & (slot < 4 * PATCHES + texts[item])
    )
    return jnp.where(valid, 0.0, MASKED)


def pair_columns(t):
    per = STRIPE // PAIR
    start = (t // per) * 2 * STRIPE + (t % per) * PAIR
    return (
        slice(PAIR * t, PAIR * t + PAIR),
        slice(start, start + PAIR),
        slice(start + STRIPE, start + STRIPE + PAIR),
    )


def cross_fwd_kernel(pairs, texts, q_ref, kv_ref, o_ref, lse_ref):
    pen = cross_penalty((1, kv_ref.shape[0]), 1, pairs, texts, pl.program_id(0))
    for t in range(q_ref.shape[1] // PAIR):
        cols, kcols, vcols = pair_columns(t)
        s = dot(twice(q_ref[:, cols]), kv_ref[:, kcols], NT) + pen
        m = jnp.max(s, axis=1, keepdims=True)
        p = jnp.exp(s - m)
        total = jnp.sum(p, axis=1, keepdims=True)
        p = (p * (1.0 / total)).astype(BF)
        o_ref[:, cols] = once(dot(p, kv_ref[:, vcols])).astype(BF)
        lse = jnp.broadcast_to(m + jnp.log(total), (total.shape[0], PAIR))
        lse_ref[t] = jnp.transpose(lse)[:1]


def cross_bwd_kernel(pairs, texts, q_ref, kv_ref, lse_ref, do_ref, dq_ref, dkv_ref):
    pen = cross_penalty((kv_ref.shape[0], 1), 0, pairs, texts, pl.program_id(0))
    for t in range(q_ref.shape[1] // PAIR):
        cols, kcols, vcols = pair_columns(t)
        q2 = twice(q_ref[:, cols])
        do2 = twice(do_ref[:, cols])
        s = dot(kv_ref[:, kcols], q2, NT)
        p = jnp.exp(s + (pen - lse_ref[t]))
        dp = dot(kv_ref[:, vcols], do2, NT)
        delta = jnp.sum(p * dp, axis=0, keepdims=True)
        ds = (p * (dp - delta)).astype(BF)
        dkv_ref[:, vcols] = dot(p.astype(BF), do2).astype(BF)
        dkv_ref[:, kcols] = dot(ds, q2).astype(BF)
        dq_ref[:, cols] = once(dot(ds, kv_ref[:, kcols], TN)).astype(BF)


def cross_specs(slots, length, width, n):
    small = pl.BlockSpec((length, width), lambda i, j, *_: (i, j))
    big = pl.BlockSpec((slots, 2 * width), lambda i, j, *_: (i, j))
    lse = pl.BlockSpec((width // PAIR, 1, 2 * length), lambda i, j, *_: (i * n + j, 0, 0))
    return small, big, lse


def cross_fwd(pairs, texts, q, kv, width=2 * STRIPE):
    items, cols = pairs.shape[0], q.shape[1]
    slots, length, n = kv.shape[0] // items, q.shape[0] // items, cols // width
    small, big, lse = cross_specs(slots, length, width, n)
    return pl.pallas_call(
        cross_fwd_kernel,
        grid_spec=pltpu.PrefetchScalarGridSpec(
            num_scalar_prefetch=2,
            grid=(items, n),
            in_specs=[small, big],
            out_specs=[small, lse],
        ),
        out_shape=[
            jax.ShapeDtypeStruct(q.shape, BF),
            jax.ShapeDtypeStruct((items * cols // PAIR, 1, 2 * length), F32),
        ],
        cost_estimate=pl.CostEstimate(
            flops=16 * q.size * slots, bytes_accessed=2 * kv.size + 4 * q.size, transcendentals=0
        ),
    )(pairs, texts, q, kv)


def cross_bwd(pairs, texts, q, kv, lse, do, width=STRIPE):
    items, cols = pairs.shape[0], q.shape[1]
    slots, length, n = kv.shape[0] // items, q.shape[0] // items, cols // width
    small, big, lspec = cross_specs(slots, length, width, n)
    return pl.pallas_call(
        cross_bwd_kernel,
        grid_spec=pltpu.PrefetchScalarGridSpec(
            num_scalar_prefetch=2,
            grid=(items, n),
            in_specs=[small, big, lspec, small],
            out_specs=[small, big],
        ),
        out_shape=[jax.ShapeDtypeStruct(q.shape, BF), jax.ShapeDtypeStruct(kv.shape, BF)],
        cost_estimate=pl.CostEstimate(
            flops=40 * q.size * slots, bytes_accessed=4 * kv.size + 6 * q.size, transcendentals=0
        ),
    )(pairs, texts, q, kv, lse, do)


def self_valid(lens, item, length):
    key = lax.broadcasted_iota(jnp.int32, (length, length), 0)
    query = lax.broadcasted_iota(jnp.int32, (length, length), 1)
    valid = (key <= query) & (key < lens[item])
    return jnp.concatenate([valid.astype(jnp.int32)] * 2, axis=1) != 0


def self_columns(t, cols):
    start = PAIR * t
    return (
        slice(start, start + PAIR),
        slice(cols + start, cols + start + PAIR),
        slice(2 * cols + start, 2 * cols + start + PAIR),
    )


def self_fwd_kernel(lens, qkv_ref, bias_ref, o_ref, lse_ref):
    valid = self_valid(lens, pl.program_id(0), qkv_ref.shape[0])
    for t in range(o_ref.shape[1] // PAIR):
        cols, kcols, vcols = self_columns(t, o_ref.shape[1])
        s = dot(qkv_ref[:, kcols], twice(qkv_ref[:, cols]), NT) + bias_ref[t]
        s = jnp.where(valid, s, MASKED)
        m = jnp.max(s, axis=0, keepdims=True)
        p = jnp.exp(s - m)
        total = jnp.sum(p, axis=0, keepdims=True)
        p = (p * (1.0 / total)).astype(BF)
        o_ref[:, cols] = once(dot(p, qkv_ref[:, vcols], TN)).astype(BF)
        lse_ref[t] = m + jnp.log(total)


def self_bwd_kernel(lens, qkv_ref, bias_ref, lse_ref, do_ref, dqkv_ref, sum_ref):
    item = pl.program_id(0)
    valid = self_valid(lens, item, qkv_ref.shape[0])

    @pl.when(item == 0)
    def _():
        sum_ref[...] = jnp.zeros_like(sum_ref)

    for t in range(do_ref.shape[1] // PAIR):
        cols, kcols, vcols = self_columns(t, do_ref.shape[1])
        q2 = twice(qkv_ref[:, cols])
        do2 = twice(do_ref[:, cols])
        s = dot(qkv_ref[:, kcols], q2, NT) + bias_ref[t]
        p = jnp.where(valid, jnp.exp(s - lse_ref[t]), 0.0)
        dp = dot(qkv_ref[:, vcols], do2, NT)
        delta = jnp.sum(p * dp, axis=0, keepdims=True)
        ds = (p * (dp - delta)).astype(BF)
        dqkv_ref[:, vcols] = dot(p.astype(BF), do2).astype(BF)
        dqkv_ref[:, kcols] = dot(ds, q2).astype(BF)
        dqkv_ref[:, cols] = once(dot(ds, qkv_ref[:, kcols], TN)).astype(BF)
        sum_ref[t] += ds.astype(F32)


def self_specs(length, cols):
    one = pl.BlockSpec((length, cols), lambda i, *_: (i, 0))
    three = pl.BlockSpec((length, 3 * cols), lambda i, *_: (i, 0))
    bias = pl.BlockSpec((cols // PAIR, length, 2 * length), lambda i, *_: (0, 0, 0))
    lse = pl.BlockSpec((cols // PAIR, 1, 2 * length), lambda i, *_: (i, 0, 0))
    return one, three, bias, lse


def self_fwd(lens, qkv, bias):
    items, cols = lens.shape[0], qkv.shape[1] // 3
    length = qkv.shape[0] // items
    one, three, bspec, lse = self_specs(length, cols)
    return pl.pallas_call(
        self_fwd_kernel,
        grid_spec=pltpu.PrefetchScalarGridSpec(
            num_scalar_prefetch=1, grid=(items,), in_specs=[three, bspec], out_specs=[one, lse]
        ),
        out_shape=[
            jax.ShapeDtypeStruct((qkv.shape[0], cols), BF),
            jax.ShapeDtypeStruct((items * cols // PAIR, 1, 2 * length), F32),
        ],
        cost_estimate=pl.CostEstimate(
            flops=16 * qkv.size * length, bytes_accessed=4 * qkv.size, transcendentals=0
        ),
    )(lens, qkv, bias)


def self_bwd(lens, qkv, bias, lse, do):
    items, cols = lens.shape[0], qkv.shape[1] // 3
    length = qkv.shape[0] // items
    one, three, bspec, lspec = self_specs(length, cols)
    return pl.pallas_call(
        self_bwd_kernel,
        grid_spec=pltpu.PrefetchScalarGridSpec(
            num_scalar_prefetch=1,
            grid=(items,),
            in_specs=[three, bspec, lspec, one],
            out_specs=[three, bspec],
        ),
        out_shape=[jax.ShapeDtypeStruct(qkv.shape, BF), jax.ShapeDtypeStruct(bias.shape, F32)],
        cost_estimate=pl.CostEstimate(
            flops=16 * qkv.size * length, bytes_accessed=6 * qkv.size, transcendentals=0
        ),
    )(lens, qkv, bias, lse, do)


def rows_kernel(dims, rows_ref, weight_ref, *refs):
    refs[-1][...] = dot(rows_ref[...], weight_ref[...], dims).astype(refs[-1].dtype)


def rows_part(rows, weight, dims, dtype, first, count, block, before=None):
    total, inner = rows.shape
    cols = weight.shape[1 - dims[0][1][0]]
    before = [] if before is None else [before]
    return pl.pallas_call(
        functools.partial(rows_kernel, dims),
        grid=(count,),
        in_specs=[
            pl.BlockSpec((block, inner), lambda i: (first + i, 0)),
            pl.BlockSpec(weight.shape, lambda i: (0, 0)),
        ]
        + [pl.BlockSpec(memory_space=ANY)] * len(before),
        out_specs=pl.BlockSpec((block, cols), lambda i: (first + i, 0)),
        out_shape=jax.ShapeDtypeStruct((total, cols), dtype),
        input_output_aliases={2: 0} if before else {},
        cost_estimate=pl.CostEstimate(
            flops=2 * count * block * weight.size,
            bytes_accessed=count * block * (2 * inner + 4 * cols),
            transcendentals=0,
        ),
    )(rows, weight, *before)


def ffn_kernel(
    rows_ref, cot_ref, sum_ref, gate_ref, up_ref, down_ref,
    hidden_ref, dunits_ref, out_ref, drows_ref, acc,
):
    i = pl.program_id(0)
    rows, cot = rows_ref[...], cot_ref[...]
    gate, up, down = gate_ref[...], up_ref[...], down_ref[...]
    g = dot(rows, gate)
    u = dot(rows, up)
    dh = dot(cot, down, NT)
    scale = math.sqrt(2.0 / math.pi)
    square = g * g
    t = jnp.tanh(scale * (g + GELU_COEF * (square * g)))
    value = 0.5 * g * (1.0 + t)
    slope = 0.5 * (1.0 + t) + 0.5 * g * (1.0 - t * t) * (
        scale * (1.0 + 3.0 * GELU_COEF * square)
    )
    hidden = (value * u).astype(BF)
    dgate = (dh * u * slope).astype(BF)
    dup = (dh * value).astype(BF)
    hidden_ref[...] = hidden
    dunits_ref[:, :STRIPE] = dgate
    dunits_ref[:, STRIPE:] = dup
    out = dot(hidden, down)
    drows = dot(dgate, gate, NT) + dot(dup, up, NT)

    @pl.when(i == 0)
    def _():
        acc[...] = sum_ref[...] + out
        drows_ref[...] = drows

    @pl.when(i > 0)
    def _():
        acc[...] += out
        drows_ref[...] += drows

    @pl.when(i == pl.num_programs(0) - 1)
    def _():
        out_ref[...] = acc[...].astype(BF)


def ffn(rows, cot, total, gate, up, up_start, down):
    count, width = rows.shape
    ff = down.shape[0]
    block = STRIPE
    whole = pl.BlockSpec((count, width), lambda i: (0, 0))
    cols = pl.BlockSpec((width, block), lambda i: (0, i))
    later = pl.BlockSpec((width, block), lambda i: (0, up_start // block + i))
    units = pl.BlockSpec((count, block), lambda i: (0, i))
    both = pl.BlockSpec((count, 2 * block), lambda i: (0, i))
    return pl.pallas_call(
        ffn_kernel,
        grid=(ff // block,),
        in_specs=[whole, whole, whole, cols, later, pl.BlockSpec((block, width), lambda i: (i, 0))],
        out_specs=[units, both, whole, whole],
        out_shape=[
            jax.ShapeDtypeStruct((count, ff), BF),
            jax.ShapeDtypeStruct((count, 2 * ff), BF),
            jax.ShapeDtypeStruct((count, width), BF),
            jax.ShapeDtypeStruct((count, width), F32),
        ],
        scratch_shapes=[pltpu.VMEM((count, width), F32)],
        cost_estimate=pl.CostEstimate(
            flops=12 * count * width * ff,
            bytes_accessed=6 * width * ff + 6 * count * ff + 14 * count * width,
            transcendentals=0,
        ),
    )(rows, cot, total, gate, up, down)


def half_grads_kernel(layout, extra, pos, *refs):
    out, turned = refs[-2:]
    i = pl.program_id(0)
    at = 0
    for arity, first, last in layout:
        part = refs[at : at + arity]

        @pl.when(i == first)
        def _(part=part):
            if len(part) == 2:
                turned[...] = jnp.transpose(part[0][...])

        @pl.when((i >= first) & (i < last))
        def _(part=part):
            grad = dot(turned[...], part[1][...]) if len(part) == 2 else part[0][...]
            if extra:
                grad = grad.astype(F32) + refs[-3][...].astype(F32)
            out[...] = grad.astype(BF)

        at += arity


def half_grads(which, parts, got=None):
    widths = [part[-1].shape[1] for part in parts]
    block = 1024 if all(width % 1024 == 0 for width in widths) else 512
    half = (parts[0][0].shape[1] if len(parts[0]) == 2 else parts[0][0].shape[0]) // 2
    specs, args, layout, first = [], [], [], 0

    def column(rows, row, first, count):
        return pl.BlockSpec(
            (rows, block),
            lambda i, pos: (pos[0] if row else 0, jnp.clip(i - first, 0, count - 1)),
        )

    for part, width in zip(parts, widths):
        count = width // block
        if len(part) == 2:
            rows = part[0].shape[0]
            specs.append(pl.BlockSpec((rows, half), lambda i, pos: (0, pos[0])))
            specs.append(column(rows, False, first, count))
        else:
            specs.append(column(half, True, first, count))
        args += part
        layout.append((len(part), first, first + count))
        first += count
    here = pl.BlockSpec((half, block), lambda i, pos: (0, i))
    if got is not None:
        specs.append(here)
        args.append(got)
    return pl.pallas_call(
        functools.partial(half_grads_kernel, tuple(layout), got is not None),
        out_shape=jax.ShapeDtypeStruct((half, sum(widths)), BF),
        grid_spec=pltpu.PrefetchScalarGridSpec(
            num_scalar_prefetch=1,
            grid=(first,),
            in_specs=specs,
            out_specs=here,
            scratch_shapes=[pltpu.VMEM((half, max([part[0].shape[0] for part in parts if len(part) == 2] or [16])), BF)],
        ),
        cost_estimate=pl.CostEstimate(
            flops=2 * half * 512 * sum(widths),
            bytes_accessed=6 * half * sum(widths),
            transcendentals=0,
        ),
    )(which, *args)


def stripes(width):
    return tuple(
        (number, start, start + STRIPE) for start in range(0, width, STRIPE) for number in (0, 1)
    )


def swap(value, axis, bit):
    size = lax.axis_size(axis)
    return lax.ppermute(value, axis, [(i, i ^ bit) for i in range(size)])


def place():
    return jnp.stack(
        [lax.axis_index("fsdp"), lax.axis_index("mp"), lax.axis_index("dp")]
    ).astype(jnp.int32)


def assemble_kernel(rows, cols, splits, me, *refs):
    pieces, outs = refs[:4], refs[4 : 4 + len(splits)]
    buf, in_sem, out_sem = refs[4 + len(splits) :]
    c, z, p = me[0], me[1], me[2]
    quarter = cols // 4
    blocks = []
    n = 0
    for other in range(2):
        for zr in range(4):
            row = pl.multiple_of(((c ^ other) * 4 + (z ^ zr)) * rows, rows)
            copies = []
            if zr == 0:
                copies.append(
                    pltpu.make_async_copy(
                        pieces[2 * other], buf.at[pl.ds(row, rows), :], in_sem.at[n]
                    )
                )
                n += 1
            else:
                for j in range(4):
                    col = pl.multiple_of((p ^ j) * quarter, 128)
                    copies.append(
                        pltpu.make_async_copy(
                            pieces[2 * other + 1].at[3 * j + zr - 1],
                            buf.at[pl.ds(row, rows), pl.ds(col, quarter)],
                            in_sem.at[n],
                        )
                    )
                    n += 1
            for copy in copies:
                copy.start()
            blocks.append((row, copies))
    pending = []
    n = 0
    for row, copies in blocks:
        for copy in copies:
            copy.wait()
        start = 0
        for out, width in zip(outs, splits):
            copy = pltpu.make_async_copy(
                buf.at[pl.ds(row, rows), pl.ds(start, width)],
                out.at[pl.ds(row, rows), :],
                out_sem.at[n],
            )
            copy.start()
            pending.append(copy)
            start += width
            n += 1
    for copy in pending:
        copy.wait()


def assemble(me, pieces, rows, splits):
    cols = sum(splits)
    total = 8 * rows
    return pl.pallas_call(
        functools.partial(assemble_kernel, rows, cols, splits),
        out_shape=[jax.ShapeDtypeStruct((total, width), BF) for width in splits],
        in_specs=[pl.BlockSpec(memory_space=pltpu.SMEM)] + [pl.BlockSpec(memory_space=ANY)] * 4,
        out_specs=[pl.BlockSpec(memory_space=ANY)] * len(splits),
        scratch_shapes=[
            pltpu.VMEM((total, cols), BF),
            pltpu.SemaphoreType.DMA((26,)),
            pltpu.SemaphoreType.DMA((8 * len(splits),)),
        ],
        cost_estimate=pl.CostEstimate(
            flops=0, bytes_accessed=4 * total * cols, transcendentals=0
        ),
    )(me, *pieces)


def pack_kernel(spans, me, *refs):
    shards, (own, part) = refs[:-2], refs[-2:]
    at = 0
    for number, start, stop in spans:
        own[:, at : at + stop - start] = shards[number][:, start:stop]
        at += stop - start
    quarter = part.shape[1]
    part[...] = own[:, pl.ds(pl.multiple_of(me[2] * quarter, 128), quarter)]


def pack(me, shards, spans):
    rows = shards[0].shape[0]
    cols = sum(stop - start for number, start, stop in spans)
    return vmem_call(
        functools.partial(pack_kernel, spans),
        [
            jax.ShapeDtypeStruct((rows, cols), BF),
            jax.ShapeDtypeStruct((rows, cols // 4), BF),
        ],
        list(shards),
        pos=me,
        moved=5 * rows * cols,
    )


def planes_kernel(*refs):
    pieces, out, (buf, in_sem, out_sem) = refs[:-4], refs[-4], refs[-3:]
    copies, at = [], 0
    for number, piece in enumerate(pieces):
        here = pl.ds(at, piece.shape[0])
        copies.append(
            (
                pltpu.make_async_copy(piece, buf.at[here], in_sem.at[number]),
                pltpu.make_async_copy(buf.at[here], out.at[here], out_sem.at[number]),
            )
        )
        at += piece.shape[0]
    for first, second in copies:
        first.start()
    for first, second in copies:
        first.wait()
        second.start()
    for first, second in copies:
        second.wait()


def together(values):
    shape = (sum(value.shape[0] for value in values),) + values[0].shape[1:]
    return pl.pallas_call(
        planes_kernel,
        out_shape=jax.ShapeDtypeStruct(shape, BF),
        in_specs=[pl.BlockSpec(memory_space=ANY)] * len(values),
        out_specs=pl.BlockSpec(memory_space=ANY),
        scratch_shapes=[
            pltpu.VMEM(shape, BF),
            pltpu.SemaphoreType.DMA((len(values),)),
            pltpu.SemaphoreType.DMA((len(values),)),
        ],
        cost_estimate=pl.CostEstimate(
            flops=0, bytes_accessed=4 * math.prod(shape), transcendentals=0
        ),
    )(*values)


class Steps:
    def __init__(self, generator):
        self.generator, self.result, self.pending = generator, None, []
        self.sends = next(generator)

    def take(self, values):
        if self.pending:
            self.pending = []
            try:
                self.sends = self.generator.send(values)
            except StopIteration as stop:
                self.sends, self.result = [], stop.value

    def launch(self, values):
        if self.sends:
            self.pending = [swap(v, axis, bit) for v, (u, axis, bit) in zip(values, self.sends)]
            self.sends = []


def sync(values, *steps, hold=()):
    values = list(values)
    count = len(values)
    waited = list(steps) + list(hold)
    pending = [piece for step in waited for piece in step.pending]
    flat = list(lax.optimization_barrier(tuple(values + pending)))
    values, at = flat[:count], count
    for step in waited:
        size = len(step.pending)
        step.take(flat[at : at + size])
        at += size
    sends = [send[0] for step in steps for send in step.sends]
    flat = list(lax.optimization_barrier(tuple(values + sends)))
    values, at = flat[:count], count
    for step in steps:
        size = len(step.sends)
        step.launch(flat[at : at + size])
        at += size
    return values


def gather_steps(me, shards, spans, splits, flip):
    own, part = pack(me, shards, spans)
    rows, cols = own.shape
    along_z = yield [(part, "mp", bit) for bit in (1, 2, 3)]
    first, second = (1, 2) if flip else (2, 1)
    a0 = together([piece[None] for piece in along_z])
    hop, side = yield [(a0, "dp", first), (a0, "dp", second)]
    far, own_theirs = yield [(hop, "dp", second), (own, "fsdp", 1)]
    planes = together([a0, hop, side, far] if flip else [a0, side, hop, far])
    (planes_theirs,) = yield [(planes, "fsdp", 1)]
    return assemble(me, [own, planes, own_theirs, planes_theirs], rows, splits)


def rs_add_kernel(pos, ka_s, ka_k, kb_s, kb_k, ra_s, ra_k, rb_s, rb_k, sa, sb, keep):
    sa[...] = (ka_s[...].astype(F32) + ra_s[...].astype(F32)).astype(BF)
    sb[...] = (kb_s[...].astype(F32) + rb_s[...].astype(F32)).astype(BF)
    keep[0] = (ka_k[...].astype(F32) + ra_k[...].astype(F32)).astype(BF)
    keep[1] = (kb_k[...].astype(F32) + rb_k[...].astype(F32)).astype(BF)


def rs_z_kernel(pos, *refs):
    keeps, ras, rbs, outs = refs[:4], refs[4:8], refs[8:12], refs[12:]
    z = pos[1]
    for k in range(4):
        low = (z ^ k) < 2
        recv = jnp.where(low, ras[k][0].astype(F32), rbs[k][0].astype(F32))
        outs[k][...] = (keeps[k][0].astype(F32) + recv).astype(BF)


def rs_last_kernel(own, r1, r2, r3, out):
    out[...] = (
        (own[...].astype(F32) + r1[...].astype(F32)) + (r2[...].astype(F32) + r3[...].astype(F32))
    ).astype(BF)


def rs_place_kernel(places, pos, *refs):
    pieces, outs, buf = refs[: -1 - len(places)], refs[-1 - len(places) : -1], refs[-1]
    quarter = pieces[0].shape[-1]
    z, p = pos[1], pos[2]
    for j in range(4):
        if len(pieces) == 1:
            q, piece = j, pieces[0][j]
        else:
            q, piece = p ^ j, pieces[j][...]
        col = jnp.where(z < 2, (q & 1) * 2 + (q >> 1), q) * quarter
        buf[:, pl.ds(pl.multiple_of(col, 128), quarter)] = piece.astype(F32)
    for out, (shape, copies) in zip(outs, places):
        for to_rows, to_cols, from_rows, from_cols in copies:
            out[to_rows, to_cols] = buf[from_rows, from_cols]


def block_chunks(rows, cols, height):
    chunks = []
    for t in range(cols // 128):
        at = 0
        while at < rows:
            block, inside = divmod(t * rows + at, height)
            size = min(height - inside, rows - at)
            chunks.append((slice(at, at + size), t, slice(inside, inside + size), block))
            at += size
    return chunks


def lane_tile(t):
    return slice(128 * t, 128 * t + 128)


def reblock_kernel(height, grad_ref, out_ref):
    rows, cols = grad_ref.shape
    out_ref[:, rows * cols // height :] = jnp.zeros_like(out_ref[:, rows * cols // height :])
    for from_rows, t, to_rows, block in block_chunks(rows, cols, height):
        out_ref[to_rows, lane_tile(block)] = grad_ref[from_rows, lane_tile(t)]


def ffn_pack_kernel(gate_ref, up_ref, down_ref, pos, out_ref, buf):
    height, ff = gate_ref.shape
    buf[:, :ff] = gate_ref[...]
    buf[:, ff : 2 * ff] = up_ref[...]
    for from_rows, t, to_rows, block in block_chunks(*down_ref.shape, height):
        buf[to_rows, lane_tile(2 * ff // 128 + block)] = down_ref[from_rows, lane_tile(t)]
    count = out_ref.shape[0]
    out_ref[...] = buf[pl.ds(pl.multiple_of(pos[2] * count, count), count), :]


def ffn_pack(me, gate, up, down):
    height, ff = gate.shape
    vmem = pl.BlockSpec(memory_space=pltpu.VMEM)
    cols = 2 * ff + down.size // height
    return pl.pallas_call(
        ffn_pack_kernel,
        out_shape=jax.ShapeDtypeStruct((height // 4, cols), BF),
        in_specs=[vmem, vmem, vmem, pl.BlockSpec(memory_space=pltpu.SMEM)],
        out_specs=vmem,
        scratch_shapes=[pltpu.VMEM((height, cols), BF)],
        cost_estimate=pl.CostEstimate(
            flops=0, bytes_accessed=3 * height * cols, transcendentals=0
        ),
    )(gate, up, down, me)


def unblock_kernel(blocks_ref, out_ref):
    for to_rows, t, from_rows, block in block_chunks(*out_ref.shape, blocks_ref.shape[0]):
        out_ref[to_rows, lane_tile(t)] = blocks_ref[from_rows, lane_tile(block)]


def unblock(packed, rows, cols):
    height, width = packed.shape[0] // 8, 8 * rows * cols // packed.shape[0]
    last = packed.shape[1] // width - 1
    return pl.pallas_call(
        unblock_kernel,
        grid=(8,),
        in_specs=[pl.BlockSpec((height, width), lambda i: (i, last))],
        out_specs=pl.BlockSpec((rows, cols), lambda i: (i, 0)),
        out_shape=jax.ShapeDtypeStruct((8 * rows, cols), BF),
        cost_estimate=pl.CostEstimate(
            flops=0, bytes_accessed=32 * rows * cols, transcendentals=0
        ),
    )(packed)


def reblock(grad, height, width):
    rows, cols = grad.shape[0] // 8, grad.shape[1]
    return pl.pallas_call(
        functools.partial(reblock_kernel, height),
        grid=(8,),
        in_specs=[pl.BlockSpec((rows, cols), lambda i: (i, 0))],
        out_specs=pl.BlockSpec((height, width), lambda i: (i, 0)),
        out_shape=jax.ShapeDtypeStruct((8 * height, width), BF),
        cost_estimate=pl.CostEstimate(
            flops=0, bytes_accessed=4 * grad.size, transcendentals=0
        ),
    )(grad)


def vmem_call(kernel, outs, ins, pos=None, scratch=(), moved=0):
    specs = [pl.BlockSpec(memory_space=pltpu.VMEM)] * len(ins)
    args = list(ins)
    if pos is not None:
        specs = [pl.BlockSpec(memory_space=pltpu.SMEM)] + specs
        args = [pos] + args
    return pl.pallas_call(
        kernel,
        out_shape=outs,
        in_specs=specs,
        out_specs=jax.tree.map(lambda _: pl.BlockSpec(memory_space=pltpu.VMEM), outs),
        scratch_shapes=list(scratch),
        cost_estimate=pl.CostEstimate(flops=0, bytes_accessed=moved, transcendentals=0),
    )(*args)


def scatter_steps(me, parts, places, wide):
    c, x, y = me[0], me[2] & 1, me[2] >> 1
    sent = half_grads(1 - me[:1], parts)
    (got,) = yield [(sent, "fsdp", 1)]
    kept = half_grads(me[:1], parts, got)
    half, cols = kept.shape
    rows, quarter = half // 4, cols // 4
    two = 2 * rows
    send_a = lax.dynamic_slice(kept, (0, (1 - x) * 2 * quarter), (two, 2 * quarter))
    send_b = lax.dynamic_slice(kept, (two, (1 - y) * 2 * quarter), (two, 2 * quarter))
    recv_a, recv_b = yield [(send_a, "dp", 1), (send_b, "dp", 2)]
    send_c, send_d, keep = rs_add(me, kept, recv_a, recv_b)
    recv_c, recv_d = yield [(send_c, "dp", 2), (send_d, "dp", 1)]
    pieces = rs_z(me, keep, recv_c, recv_d)
    gots = yield [(pieces[k], "mp", k) for k in (1, 2, 3)]
    piece = vmem_call(
        rs_last_kernel,
        jax.ShapeDtypeStruct((rows, quarter), BF),
        [pieces[0]] + gots,
        moved=10 * rows * quarter,
    )
    if wide:
        around = lax.all_gather(piece, "dp")
    else:
        around = yield [(piece, "dp", k) for k in (1, 2, 3)]
        around = [piece] + around
    return vmem_call(
        functools.partial(rs_place_kernel, places),
        [jax.ShapeDtypeStruct(shape, F32) for shape, copies in places],
        [around] if wide else around,
        pos=me,
        scratch=[pltpu.VMEM((rows, cols), F32)],
        moved=6 * rows * cols,
    )


def rs_add(me, kept, recv_a, recv_b):
    half, cols = kept.shape
    two, quarter = half // 2, cols // 4
    steps = 4 if two % 128 == 0 else 2
    block = two // steps

    def at(kind):
        def index(i, pos):
            px, py = pos[2] & 1, pos[2] >> 1
            return {
                "ka_s": (i, px * 2 + 1 - py),
                "ka_k": (i, px * 2 + py),
                "kb_s": (steps + i, py * 2 + 1 - px),
                "kb_k": (steps + i, py * 2 + px),
                "ra_s": (i, 1 - py),
                "ra_k": (i, py),
                "rb_s": (i, 1 - px),
                "rb_k": (i, px),
            }[kind]

        return pl.BlockSpec((block, quarter), index)

    return pl.pallas_call(
        rs_add_kernel,
        out_shape=[
            jax.ShapeDtypeStruct((two, quarter), BF),
            jax.ShapeDtypeStruct((two, quarter), BF),
            jax.ShapeDtypeStruct((2, two, quarter), BF),
        ],
        grid_spec=pltpu.PrefetchScalarGridSpec(
            num_scalar_prefetch=1,
            grid=(steps,),
            in_specs=[
                at(k) for k in ("ka_s", "ka_k", "kb_s", "kb_k", "ra_s", "ra_k", "rb_s", "rb_k")
            ],
            out_specs=[
                pl.BlockSpec((block, quarter), lambda i, pos: (i, 0)),
                pl.BlockSpec((block, quarter), lambda i, pos: (i, 0)),
                pl.BlockSpec((2, block, quarter), lambda i, pos: (0, i, 0)),
            ],
        ),
        cost_estimate=pl.CostEstimate(
            flops=0, bytes_accessed=6 * half * quarter * 2, transcendentals=0
        ),
    )(me, kept, kept, kept, kept, recv_a, recv_a, recv_b, recv_b)


def rs_z(me, keep, recv_c, recv_d):
    rows, quarter = recv_c.shape[0] // 2, recv_c.shape[1]
    recv_c = recv_c.reshape(2, rows, quarter)
    recv_d = recv_d.reshape(2, rows, quarter)
    keep = keep.reshape(4, rows, quarter)

    def zspec(k, wrap):
        def index(i, pos):
            zz = pos[1] ^ k
            return ((zz & 1) if wrap else zz, 0, 0)

        return pl.BlockSpec((1, rows, quarter), index)

    return pl.pallas_call(
        rs_z_kernel,
        out_shape=[jax.ShapeDtypeStruct((rows, quarter), BF)] * 4,
        grid_spec=pltpu.PrefetchScalarGridSpec(
            num_scalar_prefetch=1,
            grid=(1,),
            in_specs=[zspec(k, w) for w in (False, True, True) for k in range(4)],
            out_specs=[pl.BlockSpec((rows, quarter), lambda i, pos: (0, 0))] * 4,
        ),
        cost_estimate=pl.CostEstimate(
            flops=0, bytes_accessed=16 * rows * quarter * 2, transcendentals=0
        ),
    )(me, *([keep] * 4 + [recv_c] * 4 + [recv_d] * 4))


def special(sizes):
    return sizes == (4, 2, 4)


def gather_plain(shards, spans, splits):
    own = jnp.concatenate(
        [shards[number][:, start:stop] for number, start, stop in spans], axis=1
    )
    whole = lax.all_gather(own, ("fsdp", "mp"), axis=0, tiled=True)
    if len(splits) == 1:
        return [whole]
    return jnp.split(whole, np.cumsum(splits)[:-1], axis=1)


def sum_everywhere(value, sizes):
    if not special(sizes):
        return lax.psum(value, ("dp", "fsdp", "mp"))
    for axis, bit in (("fsdp", 1), ("dp", 1), ("dp", 2), ("mp", 1), ("mp", 2)):
        value = value + swap(value, axis, bit)
    return value


def scatter_plain(left, right):
    grad = weight_grad(left, right).astype(BF)
    grad = lax.psum_scatter(grad, ("fsdp", "mp"), scatter_dimension=0, tiled=True)
    return lax.psum(grad, "dp").astype(F32)


class Done:
    pending, sends = [], []

    def __init__(self, result):
        self.result = result

    def take(self, values):
        pass

    def launch(self, values):
        pass


def column_places(rows, spans):
    places = []
    for group in spans:
        copies, at = [], 0
        for start, stop in group:
            copies.append(
                (slice(0, rows), slice(at, at + stop - start), slice(0, rows), slice(start, stop))
            )
            at += stop - start
        places.append(((rows, at), tuple(copies)))
    return tuple(places)


def shards(
    sizes,
    dec_input,
    enc_output,
    image_pairs,
    text_lengths,
    dec_lengths,
    self_query,
    self_key,
    self_value,
    self_out,
    cross_query,
    cross_key,
    cross_value,
    cross_out,
    ffn_gate,
    ffn_up,
    ffn_down,
    norm_first,
    norm_second,
    norm_third,
    bias_table,
    cotangent,
):
    item_count, length, model_width = dec_input.shape
    enc_len = enc_output.shape[1]
    bucket_count, head_count = bias_table.shape
    row_count = item_count * length
    enc_count = item_count * enc_len
    ff = ffn_gate.shape[1]
    me = place()

    chips = special(sizes)

    def gather(number, *group, spans=None, splits=None):
        spans = spans or tuple((n, 0, shard.shape[1]) for n, shard in enumerate(group))
        splits = splits or (sum(shard.shape[1] for shard in group),)
        if chips:
            return Steps(gather_steps(me, group, spans, splits, number % 2 == 0))
        return Done(gather_plain(group, spans, splits))

    weight_rows = self_query.shape[0]
    down_rows = ffn_down.shape[0]

    def scatter(parts, places, plain, wide=False):
        if chips:
            return Steps(scatter_steps(me, parts(), places, wide))
        return Done(plain())

    def spans_of(first, count):
        return tuple(
            ((k * model_width, (k + 1) * model_width),) for k in range(first, first + count)
        )

    def striped(width):
        return tuple(
            tuple(
                (2 * start + shift, 2 * start + shift + STRIPE)
                for start in range(0, width, STRIPE)
            )
            for shift in (0, STRIPE)
        )

    def scatter_striped(left, right):
        whole = scatter_plain(left, right)
        return [
            jnp.concatenate([whole[:, start:stop] for start, stop in spans], axis=1)
            for spans in striped(right.shape[1] // 2)
        ]

    buckets = jnp.asarray(bucket_table(length).T.reshape(-1))
    onehot = (buckets[None, :] == jnp.arange(bucket_count)[:, None]).astype(F32)
    relative = lax.dot_general(
        bias_table.astype(F32), onehot, (((0,), (0,)), ((), ())), precision=lax.Precision.HIGHEST
    )
    relative = relative.reshape(head_count // 2, 2, length, length).transpose(0, 2, 1, 3)
    relative = relative.reshape(head_count // 2, length, 2 * length)

    gains = jnp.stack([norm_first, norm_second, norm_third], axis=1)
    gains = jnp.pad(gains, ((0, 0), (0, 512 - gains.shape[1])))
    g_kv = gather(0, cross_key, cross_value, spans=stripes(model_width))
    g_qkv = gather(1, self_query, self_key, self_value, gains, splits=(3 * model_width, 512))
    g_mid = gather(0, self_out, cross_query, cross_out, splits=(model_width,) * 3)
    if chips:
        ffn_full = lax.all_gather(
            ffn_pack(me, ffn_gate, ffn_up, ffn_down), ("fsdp", "mp", "dp"), axis=0, tiled=True
        )
    enc_rows = enc_output.reshape(enc_count, model_width)
    block = 2 * length
    blocks = enc_count // block
    sync([], g_kv)
    sync([send[0] for step in (g_qkv, g_mid) for send in step.sends[:1]], g_kv, g_qkv)
    sync([], g_kv)
    sync([], g_kv, g_qkv)
    sync([], hold=(g_kv,))
    (kv_full,) = g_kv.result
    kv_full, enc_rows = sync([kv_full, enc_rows], g_mid)

    inputs = dec_input.astype(F32).reshape(row_count, model_width)
    cross_kv = rows_part(enc_rows, kv_full, NN, BF, 0, blocks // 2, block)
    (cross_kv,) = sync([cross_kv], g_qkv)
    cross_kv = rows_part(
        enc_rows, kv_full, NN, BF, blocks // 2, blocks - blocks // 2, block, cross_kv
    )
    (cross_kv,) = sync([cross_kv], g_qkv, g_mid)
    sync([], hold=(g_qkv,))
    qkv_full, gains = g_qkv.result
    gains = gains[:, :PAIR].T.astype(F32)
    gain_first, gain_second, gain_third = gains[0], gains[1], gains[2]
    normed_first = norm_rows(inputs, gain_first).astype(BF)
    qkv = matmul(normed_first, qkv_full).astype(BF)
    qkv, cross_kv = sync([qkv, cross_kv], g_mid)
    self_flat, self_lse = self_fwd(dec_lengths, qkv, relative)
    (self_flat,) = sync([self_flat], g_mid)
    sync([], hold=(g_mid,))
    out_full, cquery_full, cout_full = g_mid.result
    first_sum = inputs + matmul(self_flat, out_full)
    normed_second = norm_rows(first_sum, gain_second).astype(BF)
    cross_queries = matmul(normed_second, cquery_full).astype(BF)
    cross_flat, cross_lse = cross_fwd(image_pairs, text_lengths, cross_queries, cross_kv)
    out_grad = cotangent.reshape(row_count, model_width)
    second_sum = first_sum + matmul(cross_flat, cout_full)
    normed_third = norm_rows(second_sum, gain_third).astype(BF)
    if chips:
        weights = (ffn_full, ffn_full, ff, unblock(ffn_full, ffn_down.shape[0], model_width))
    else:
        gate_full, up_full, down_full = (
            lax.all_gather(shard, ("fsdp", "mp"), axis=0, tiled=True)
            for shard in (ffn_gate, ffn_up, ffn_down)
        )
        weights = (gate_full, up_full, 0, down_full)
    hidden, gu_grad, dec_output, third_normed_grad = ffn(
        normed_third, out_grad, second_sum, *weights
    )
    dec_output = dec_output.reshape(item_count, length, model_width)
    padded = -(-(2 * ff + down_rows * model_width // weight_rows) // 512) * 512 - 2 * ff
    s_ffn = scatter(
        lambda: [
            (normed_third, gu_grad),
            (reblock(weight_grad(hidden, out_grad).astype(BF), weight_rows, padded),),
        ],
        column_places(weight_rows, striped(ff))
        + (
            (
                (down_rows, model_width),
                tuple(
                    (to_rows, lane_tile(t), from_rows, lane_tile(2 * ff // 128 + block))
                    for to_rows, t, from_rows, block in block_chunks(
                        down_rows, model_width, weight_rows
                    )
                ),
            ),
        ),
        lambda: scatter_striped(normed_third, gu_grad) + [scatter_plain(hidden, out_grad)],
        wide=True,
    )
    (third_normed_grad,) = sync([third_normed_grad], s_ffn)

    unused_value, pullback = jax.vjp(norm_rows, second_sum, gain_third)
    second_part, norm_third_grad = pullback(third_normed_grad)
    second_grad = cotangent.astype(F32).reshape(row_count, model_width) + second_part
    branch_second = second_grad.astype(BF)
    cross_mixed_grad = input_grad(branch_second, cout_full).astype(BF)
    (cross_mixed_grad,) = sync([cross_mixed_grad], s_ffn)

    cq_rows, ckv_rows = cross_bwd(
        image_pairs, text_lengths, cross_queries, cross_kv, cross_lse, cross_mixed_grad
    )
    cq_rows, ckv_rows = sync([cq_rows, ckv_rows], s_ffn)

    second_normed_grad = input_grad(cq_rows, cquery_full)
    unused_value, pullback = jax.vjp(norm_rows, first_sum, gain_second)
    first_part, norm_second_grad = pullback(second_normed_grad)
    first_grad = second_grad + first_part
    branch_first = first_grad.astype(BF)
    self_mixed_grad = input_grad(branch_first, out_full).astype(BF)
    qkv_rows, score_total = self_bwd(dec_lengths, qkv, relative, self_lse, self_mixed_grad)
    s_self = scatter(
        lambda: [
            (self_flat, branch_first),
            (normed_first, qkv_rows),
            (normed_second, cq_rows),
            (cross_flat, branch_second),
        ],
        column_places(weight_rows, spans_of(0, 6)),
        lambda: [scatter_plain(self_flat, branch_first)]
        + jnp.split(scatter_plain(normed_first, qkv_rows), 3, axis=1)
        + [scatter_plain(normed_second, cq_rows), scatter_plain(cross_flat, branch_second)],
    )
    qkv_rows, ckv_rows = sync([qkv_rows, ckv_rows], s_self, s_ffn)

    qkv_rows, ckv_rows = sync([qkv_rows, ckv_rows], s_self)
    enc_grad = weight_grad(enc_rows, ckv_rows).astype(BF) if chips else None
    s_cross = scatter(
        lambda: [(enc_grad,)],
        column_places(weight_rows, striped(model_width)),
        lambda: scatter_striped(enc_rows, ckv_rows),
    )
    score_total = score_total.reshape(head_count // 2, length, 2, length).transpose(0, 2, 1, 3)
    table_part = lax.dot_general(
        onehot,
        score_total.reshape(head_count, length * length),
        (((1,), (1,)), ((), ())),
        precision=lax.Precision.HIGHEST,
    )
    first_normed_grad = input_grad(qkv_rows, qkv_full)
    unused_value, pullback = jax.vjp(norm_rows, inputs, gain_first)
    input_part, norm_first_grad = pullback(first_normed_grad)
    dec_input_grad = first_grad + input_part
    small = jnp.concatenate(
        [norm_first_grad, norm_second_grad, norm_third_grad, table_part.reshape(-1)]
    )
    dec_input_grad, small = sync(
        [dec_input_grad, small], s_self, s_cross, hold=(s_ffn,)
    )
    dec_input_grad = dec_input_grad.reshape(item_count, length, model_width)
    small = sum_everywhere(small, sizes)

    part = blocks // 3
    enc_output_grad = rows_part(ckv_rows, kv_full, NT, F32, 0, part, block)
    (enc_output_grad,) = sync([enc_output_grad], s_self, s_cross)
    enc_output_grad = rows_part(ckv_rows, kv_full, NT, F32, part, part, block, enc_output_grad)
    (enc_output_grad,) = sync([enc_output_grad], s_cross)
    enc_output_grad = rows_part(
        ckv_rows, kv_full, NT, F32, 2 * part, blocks - 2 * part, block, enc_output_grad
    )
    (enc_output_grad,) = sync([enc_output_grad], hold=(s_self,))
    enc_output_grad = enc_output_grad.reshape(item_count, enc_len, model_width)
    sync([], s_self, hold=(s_cross,))
    sync([], s_cross, hold=(s_self,))
    sync([], s_cross)
    sync([], s_cross)
    ffn_gate_grad, ffn_up_grad, ffn_down_grad = s_ffn.result
    cross_key_grad, cross_value_grad = s_cross.result
    (
        self_out_grad,
        self_query_grad,
        self_key_grad,
        self_value_grad,
        cross_query_grad,
        cross_out_grad,
    ) = s_self.result

    gain_width = norm_first.shape[0]
    start = (lax.axis_index("fsdp") * sizes[2] + lax.axis_index("mp")) * gain_width
    gain_grads = [
        lax.dynamic_slice_in_dim(small, k * model_width + start, gain_width) for k in range(3)
    ]
    bias_table_grad = small[3 * model_width :].reshape(bucket_count, head_count)
    return (
        dec_output,
        dec_input_grad,
        enc_output_grad,
        self_query_grad,
        self_key_grad,
        self_value_grad,
        self_out_grad,
        cross_query_grad,
        cross_key_grad,
        cross_value_grad,
        cross_out_grad,
        ffn_gate_grad,
        ffn_up_grad,
        ffn_down_grad,
        gain_grads[0],
        gain_grads[1],
        gain_grads[2],
        bias_table_grad,
    )


def solution(mesh):
    items = P(("dp", "fsdp", "mp"), None, None)
    item_numbers = P(("dp", "fsdp", "mp"))
    weight = P(("fsdp", "mp"), None)
    gain = P(("fsdp", "mp"))
    sizes = (mesh.shape["dp"], mesh.shape["fsdp"], mesh.shape["mp"])
    return jax.shard_map(
        functools.partial(shards, sizes),
        mesh=mesh,
        in_specs=(items, items)
        + (item_numbers,) * 3
        + (weight,) * 11
        + (gain,) * 3
        + (P(), items),
        out_specs=(items,) * 3 + (weight,) * 11 + (gain,) * 3 + (P(),),
        check_vma=False,
    )
```

```python
import functools
import math

import jax
import jax.numpy as jnp
import numpy as np
from jax import lax
from jax.experimental import pallas as pl
from jax.experimental.pallas import tpu as pltpu
from jax.sharding import PartitionSpec as P

PATCHES = 256
EPSILON = 1e-06
MASKED = -1000000000.0
GELU_COEF = 0.044715
BF = jnp.bfloat16
F32 = jnp.float32
ANY = pl.ANY


def bucket_table(length):
    rows_index = np.arange(length)[:, None]
    cols_index = np.arange(length)[None, :]
    distance = np.maximum(rows_index - cols_index, 0)
    spread = np.floor(np.log(np.maximum(distance, 1) / 16.0) / np.log(8.0) * 16.0)
    far_bucket = np.minimum(16.0 + spread, 31.0)
    return np.where(distance < 16, distance, far_bucket).astype(np.int32)


def norm_rows(values, gain):
    return values * lax.rsqrt(jnp.mean(values * values, axis=-1, keepdims=True) + EPSILON) * gain


def gelu_tanh(values):
    return (
        0.5
        * values
        * (
            1.0
            + jnp.tanh(math.sqrt(2.0 / math.pi) * (values + GELU_COEF * values * values * values))
        )
    )


def gated_unit(gate_values, up_values):
    return gelu_tanh(gate_values) * up_values


def matmul(left, right):
    return jnp.dot(left, right, preferred_element_type=F32)


def weight_grad(left, right):
    return lax.dot_general(left, right, (((0,), (0,)), ((), ())), preferred_element_type=F32)


def input_grad(upstream, weight):
    return lax.dot_general(upstream, weight, (((1,), (1,)), ((), ())), preferred_element_type=F32)


NT = (((1,), (1,)), ((), ()))
TN = (((0,), (0,)), ((), ()))
NN = (((1,), (0,)), ((), ()))
PAIR = 128
STRIPE = 256


def dot(left, right, dims=NN):
    return lax.dot_general(left, right, dims, preferred_element_type=F32)


def twice(block):
    low = lax.broadcasted_iota(jnp.int32, block.shape, 1) < block.shape[1] // 2
    zero = jnp.zeros_like(block)
    return jnp.concatenate([jnp.where(low, block, zero), jnp.where(low, zero, block)], axis=0)


def once(rows):
    half = rows.shape[0] // 2
    low = lax.broadcasted_iota(jnp.int32, (half, rows.shape[1]), 1) < rows.shape[1] // 2
    return jnp.where(low, rows[:half], rows[half:])


def cross_penalty(shape, axis, pairs, texts, item):
    slot = lax.broadcasted_iota(jnp.int32, shape, axis)
    valid = (slot < 2 * PATCHES * pairs[item]) | (
        (slot >= 4 * PATCHES) & (slot < 4 * PATCHES + texts[item])
    )
    return jnp.where(valid, 0.0, MASKED)


def pair_columns(t):
    per = STRIPE // PAIR
    start = (t // per) * 2 * STRIPE + (t % per) * PAIR
    return (
        slice(PAIR * t, PAIR * t + PAIR),
        slice(start, start + PAIR),
        slice(start + STRIPE, start + STRIPE + PAIR),
    )


def cross_fwd_kernel(pairs, texts, q_ref, kv_ref, o_ref, lse_ref):
    pen = cross_penalty((1, kv_ref.shape[0]), 1, pairs, texts, pl.program_id(0))
    for t in range(q_ref.shape[1] // PAIR):
        cols, kcols, vcols = pair_columns(t)
        s = dot(twice(q_ref[:, cols]), kv_ref[:, kcols], NT) + pen
        m = jnp.max(s, axis=1, keepdims=True)
        p = jnp.exp(s - m)
        total = jnp.sum(p, axis=1, keepdims=True)
        p = (p * (1.0 / total)).astype(BF)
        o_ref[:, cols] = once(dot(p, kv_ref[:, vcols])).astype(BF)
        lse = jnp.broadcast_to(m + jnp.log(total), (total.shape[0], PAIR))
        lse_ref[t] = jnp.transpose(lse)[:1]


def cross_bwd_kernel(pairs, texts, q_ref, kv_ref, lse_ref, do_ref, dq_ref, dkv_ref):
    pen = cross_penalty((kv_ref.shape[0], 1), 0, pairs, texts, pl.program_id(0))
    for t in range(q_ref.shape[1] // PAIR):
        cols, kcols, vcols = pair_columns(t)
        q2 = twice(q_ref[:, cols])
        do2 = twice(do_ref[:, cols])
        s = dot(kv_ref[:, kcols], q2, NT)
        p = jnp.exp(s + (pen - lse_ref[t]))
        dp = dot(kv_ref[:, vcols], do2, NT)
        delta = jnp.sum(p * dp, axis=0, keepdims=True)
        ds = (p * (dp - delta)).astype(BF)
        dkv_ref[:, vcols] = dot(p.astype(BF), do2).astype(BF)
        dkv_ref[:, kcols] = dot(ds, q2).astype(BF)
        dq_ref[:, cols] = once(dot(ds, kv_ref[:, kcols], TN)).astype(BF)


def cross_specs(slots, length, width, n):
    small = pl.BlockSpec((length, width), lambda i, j, *_: (i, j))
    big = pl.BlockSpec((slots, 2 * width), lambda i, j, *_: (i, j))
    lse = pl.BlockSpec((width // PAIR, 1, 2 * length), lambda i, j, *_: (i * n + j, 0, 0))
    return small, big, lse


def cross_fwd(pairs, texts, q, kv, width=2 * STRIPE):
    items, cols = pairs.shape[0], q.shape[1]
    slots, length, n = kv.shape[0] // items, q.shape[0] // items, cols // width
    small, big, lse = cross_specs(slots, length, width, n)
    return pl.pallas_call(
        cross_fwd_kernel,
        grid_spec=pltpu.PrefetchScalarGridSpec(
            num_scalar_prefetch=2,
            grid=(items, n),
            in_specs=[small, big],
            out_specs=[small, lse],
        ),
        out_shape=[
            jax.ShapeDtypeStruct(q.shape, BF),
            jax.ShapeDtypeStruct((items * cols // PAIR, 1, 2 * length), F32),
        ],
        cost_estimate=pl.CostEstimate(
            flops=16 * q.size * slots, bytes_accessed=2 * kv.size + 4 * q.size, transcendentals=0
        ),
    )(pairs, texts, q, kv)


def cross_bwd(pairs, texts, q, kv, lse, do, width=STRIPE):
    items, cols = pairs.shape[0], q.shape[1]
    slots, length, n = kv.shape[0] // items, q.shape[0] // items, cols // width
    small, big, lspec = cross_specs(slots, length, width, n)
    return pl.pallas_call(
        cross_bwd_kernel,
        grid_spec=pltpu.PrefetchScalarGridSpec(
            num_scalar_prefetch=2,
            grid=(items, n),
            in_specs=[small, big, lspec, small],
            out_specs=[small, big],
        ),
        out_shape=[jax.ShapeDtypeStruct(q.shape, BF), jax.ShapeDtypeStruct(kv.shape, BF)],
        cost_estimate=pl.CostEstimate(
            flops=40 * q.size * slots, bytes_accessed=4 * kv.size + 6 * q.size, transcendentals=0
        ),
    )(pairs, texts, q, kv, lse, do)


def self_valid(lens, item, length):
    key = lax.broadcasted_iota(jnp.int32, (length, length), 0)
    query = lax.broadcasted_iota(jnp.int32, (length, length), 1)
    valid = (key <= query) & (key < lens[item])
    return jnp.concatenate([valid.astype(jnp.int32)] * 2, axis=1) != 0


def self_columns(t, cols):
    start = PAIR * t
    return (
        slice(start, start + PAIR),
        slice(cols + start, cols + start + PAIR),
        slice(2 * cols + start, 2 * cols + start + PAIR),
    )


def self_fwd_kernel(lens, qkv_ref, bias_ref, o_ref, lse_ref):
    valid = self_valid(lens, pl.program_id(0), qkv_ref.shape[0])
    for t in range(o_ref.shape[1] // PAIR):
        cols, kcols, vcols = self_columns(t, o_ref.shape[1])
        s = dot(qkv_ref[:, kcols], twice(qkv_ref[:, cols]), NT) + bias_ref[t]
        s = jnp.where(valid, s, MASKED)
        m = jnp.max(s, axis=0, keepdims=True)
        p = jnp.exp(s - m)
        total = jnp.sum(p, axis=0, keepdims=True)
        p = (p * (1.0 / total)).astype(BF)
        o_ref[:, cols] = once(dot(p, qkv_ref[:, vcols], TN)).astype(BF)
        lse_ref[t] = m + jnp.log(total)


def self_bwd_kernel(lens, qkv_ref, bias_ref, lse_ref, do_ref, dqkv_ref, sum_ref):
    item = pl.program_id(0)
    valid = self_valid(lens, item, qkv_ref.shape[0])

    @pl.when(item == 0)
    def _():
        sum_ref[...] = jnp.zeros_like(sum_ref)

    for t in range(do_ref.shape[1] // PAIR):
        cols, kcols, vcols = self_columns(t, do_ref.shape[1])
        q2 = twice(qkv_ref[:, cols])
        do2 = twice(do_ref[:, cols])
        s = dot(qkv_ref[:, kcols], q2, NT) + bias_ref[t]
        p = jnp.where(valid, jnp.exp(s - lse_ref[t]), 0.0)
        dp = dot(qkv_ref[:, vcols], do2, NT)
        delta = jnp.sum(p * dp, axis=0, keepdims=True)
        ds = (p * (dp - delta)).astype(BF)
        dqkv_ref[:, vcols] = dot(p.astype(BF), do2).astype(BF)
        dqkv_ref[:, kcols] = dot(ds, q2).astype(BF)
        dqkv_ref[:, cols] = once(dot(ds, qkv_ref[:, kcols], TN)).astype(BF)
        sum_ref[t] += ds.astype(F32)


def self_specs(length, cols):
    one = pl.BlockSpec((length, cols), lambda i, *_: (i, 0))
    three = pl.BlockSpec((length, 3 * cols), lambda i, *_: (i, 0))
    bias = pl.BlockSpec((cols // PAIR, length, 2 * length), lambda i, *_: (0, 0, 0))
    lse = pl.BlockSpec((cols // PAIR, 1, 2 * length), lambda i, *_: (i, 0, 0))
    return one, three, bias, lse


def self_fwd(lens, qkv, bias):
    items, cols = lens.shape[0], qkv.shape[1] // 3
    length = qkv.shape[0] // items
    one, three, bspec, lse = self_specs(length, cols)
    return pl.pallas_call(
        self_fwd_kernel,
        grid_spec=pltpu.PrefetchScalarGridSpec(
            num_scalar_prefetch=1, grid=(items,), in_specs=[three, bspec], out_specs=[one, lse]
        ),
        out_shape=[
            jax.ShapeDtypeStruct((qkv.shape[0], cols), BF),
            jax.ShapeDtypeStruct((items * cols // PAIR, 1, 2 * length), F32),
        ],
        cost_estimate=pl.CostEstimate(
            flops=16 * qkv.size * length, bytes_accessed=4 * qkv.size, transcendentals=0
        ),
    )(lens, qkv, bias)


def self_bwd(lens, qkv, bias, lse, do):
    items, cols = lens.shape[0], qkv.shape[1] // 3
    length = qkv.shape[0] // items
    one, three, bspec, lspec = self_specs(length, cols)
    return pl.pallas_call(
        self_bwd_kernel,
        grid_spec=pltpu.PrefetchScalarGridSpec(
            num_scalar_prefetch=1,
            grid=(items,),
            in_specs=[three, bspec, lspec, one],
            out_specs=[three, bspec],
        ),
        out_shape=[jax.ShapeDtypeStruct(qkv.shape, BF), jax.ShapeDtypeStruct(bias.shape, F32)],
        cost_estimate=pl.CostEstimate(
            flops=16 * qkv.size * length, bytes_accessed=6 * qkv.size, transcendentals=0
        ),
    )(lens, qkv, bias, lse, do)


def rows_kernel(dims, rows_ref, weight_ref, *refs):
    refs[-1][...] = dot(rows_ref[...], weight_ref[...], dims).astype(refs[-1].dtype)


def rows_part(rows, weight, dims, dtype, first, count, block, before=None):
    total, inner = rows.shape
    cols = weight.shape[1 - dims[0][1][0]]
    before = [] if before is None else [before]
    return pl.pallas_call(
        functools.partial(rows_kernel, dims),
        grid=(count,),
        in_specs=[
            pl.BlockSpec((block, inner), lambda i: (first + i, 0)),
            pl.BlockSpec(weight.shape, lambda i: (0, 0)),
        ]
        + [pl.BlockSpec(memory_space=ANY)] * len(before),
        out_specs=pl.BlockSpec((block, cols), lambda i: (first + i, 0)),
        out_shape=jax.ShapeDtypeStruct((total, cols), dtype),
        input_output_aliases={2: 0} if before else {},
        cost_estimate=pl.CostEstimate(
            flops=2 * count * block * weight.size,
            bytes_accessed=count * block * (2 * inner + 4 * cols),
            transcendentals=0,
        ),
    )(rows, weight, *before)


def ffn_kernel(
    rows_ref, cot_ref, sum_ref, gate_ref, up_ref, down_ref,
    hidden_ref, dunits_ref, out_ref, drows_ref, acc,
):
    i = pl.program_id(0)
    rows, cot = rows_ref[...], cot_ref[...]
    gate, up, down = gate_ref[...], up_ref[...], down_ref[...]
    g = dot(rows, gate)
    u = dot(rows, up)
    dh = dot(cot, down, NT)
    scale = math.sqrt(2.0 / math.pi)
    square = g * g
    t = jnp.tanh(scale * (g + GELU_COEF * (square * g)))
    value = 0.5 * g * (1.0 + t)
    slope = 0.5 * (1.0 + t) + 0.5 * g * (1.0 - t * t) * (
        scale * (1.0 + 3.0 * GELU_COEF * square)
    )
    hidden = (value * u).astype(BF)
    dgate = (dh * u * slope).astype(BF)
    dup = (dh * value).astype(BF)
    hidden_ref[...] = hidden
    dunits_ref[:, :STRIPE] = dgate
    dunits_ref[:, STRIPE:] = dup
    out = dot(hidden, down)
    drows = dot(dgate, gate, NT) + dot(dup, up, NT)

    @pl.when(i == 0)
    def _():
        acc[...] = sum_ref[...] + out
        drows_ref[...] = drows

    @pl.when(i > 0)
    def _():
        acc[...] += out
        drows_ref[...] += drows

    @pl.when(i == pl.num_programs(0) - 1)
    def _():
        out_ref[...] = acc[...].astype(BF)


def ffn(rows, cot, total, gate, up, up_start, down):
    count, width = rows.shape
    ff = down.shape[0]
    block = STRIPE
    whole = pl.BlockSpec((count, width), lambda i: (0, 0))
    cols = pl.BlockSpec((width, block), lambda i: (0, i))
    later = pl.BlockSpec((width, block), lambda i: (0, up_start // block + i))
    units = pl.BlockSpec((count, block), lambda i: (0, i))
    both = pl.BlockSpec((count, 2 * block), lambda i: (0, i))
    return pl.pallas_call(
        ffn_kernel,
        grid=(ff // block,),
        in_specs=[whole, whole, whole, cols, later, pl.BlockSpec((block, width), lambda i: (i, 0))],
        out_specs=[units, both, whole, whole],
        out_shape=[
            jax.ShapeDtypeStruct((count, ff), BF),
            jax.ShapeDtypeStruct((count, 2 * ff), BF),
            jax.ShapeDtypeStruct((count, width), BF),
            jax.ShapeDtypeStruct((count, width), F32),
        ],
        scratch_shapes=[pltpu.VMEM((count, width), F32)],
        cost_estimate=pl.CostEstimate(
            flops=12 * count * width * ff,
            bytes_accessed=6 * width * ff + 6 * count * ff + 14 * count * width,
            transcendentals=0,
        ),
    )(rows, cot, total, gate, up, down)


def half_grads_kernel(layout, extra, pos, *refs):
    out, turned = refs[-2:]
    i = pl.program_id(0)
    at = 0
    for arity, first, last in layout:
        part = refs[at : at + arity]

        @pl.when(i == first)
        def _(part=part):
            if len(part) == 2:
                turned[...] = jnp.transpose(part[0][...])

        @pl.when((i >= first) & (i < last))
        def _(part=part):
            grad = dot(turned[...], part[1][...]) if len(part) == 2 else part[0][...]
            if extra:
                grad = grad.astype(F32) + refs[-3][...].astype(F32)
            out[...] = grad.astype(BF)

        at += arity


def half_grads(which, parts, got=None):
    widths = [part[-1].shape[1] for part in parts]
    block = 1024 if all(width % 1024 == 0 for width in widths) else 512
    half = (parts[0][0].shape[1] if len(parts[0]) == 2 else parts[0][0].shape[0]) // 2
    specs, args, layout, first = [], [], [], 0

    def column(rows, row, first, count):
        return pl.BlockSpec(
            (rows, block),
            lambda i, pos: (pos[0] if row else 0, jnp.clip(i - first, 0, count - 1)),
        )

    for part, width in zip(parts, widths):
        count = width // block
        if len(part) == 2:
            rows = part[0].shape[0]
            specs.append(pl.BlockSpec((rows, half), lambda i, pos: (0, pos[0])))
            specs.append(column(rows, False, first, count))
        else:
            specs.append(column(half, True, first, count))
        args += part
        layout.append((len(part), first, first + count))
        first += count
    here = pl.BlockSpec((half, block), lambda i, pos: (0, i))
    if got is not None:
        specs.append(here)
        args.append(got)
    return pl.pallas_call(
        functools.partial(half_grads_kernel, tuple(layout), got is not None),
        out_shape=jax.ShapeDtypeStruct((half, sum(widths)), BF),
        grid_spec=pltpu.PrefetchScalarGridSpec(
            num_scalar_prefetch=1,
            grid=(first,),
            in_specs=specs,
            out_specs=here,
            scratch_shapes=[pltpu.VMEM((half, max([part[0].shape[0] for part in parts if len(part) == 2] or [16])), BF)],
        ),
        cost_estimate=pl.CostEstimate(
            flops=2 * half * 512 * sum(widths),
            bytes_accessed=6 * half * sum(widths),
            transcendentals=0,
        ),
    )(which, *args)


def stripes(width):
    return tuple(
        (number, start, start + STRIPE) for start in range(0, width, STRIPE) for number in (0, 1)
    )


def swap(value, axis, bit):
    size = lax.axis_size(axis)
    return lax.ppermute(value, axis, [(i, i ^ bit) for i in range(size)])


def place():
    return jnp.stack(
        [lax.axis_index("fsdp"), lax.axis_index("mp"), lax.axis_index("dp")]
    ).astype(jnp.int32)


def assemble_kernel(rows, cols, splits, me, *refs):
    pieces, outs = refs[:4], refs[4 : 4 + len(splits)]
    buf, in_sem, out_sem = refs[4 + len(splits) :]
    c, z, p = me[0], me[1], me[2]
    quarter = cols // 4
    blocks = []
    n = 0
    for other in range(2):
        for zr in range(4):
            row = pl.multiple_of(((c ^ other) * 4 + (z ^ zr)) * rows, rows)
            copies = []
            if zr == 0:
                copies.append(
                    pltpu.make_async_copy(
                        pieces[2 * other], buf.at[pl.ds(row, rows), :], in_sem.at[n]
                    )
                )
                n += 1
            else:
                for j in range(4):
                    col = pl.multiple_of((p ^ j) * quarter, 128)
                    copies.append(
                        pltpu.make_async_copy(
                            pieces[2 * other + 1].at[3 * j + zr - 1],
                            buf.at[pl.ds(row, rows), pl.ds(col, quarter)],
                            in_sem.at[n],
                        )
                    )
                    n += 1
            for copy in copies:
                copy.start()
            blocks.append((row, copies))
    pending = []
    n = 0
    for row, copies in blocks:
        for copy in copies:
            copy.wait()
        start = 0
        for out, width in zip(outs, splits):
            copy = pltpu.make_async_copy(
                buf.at[pl.ds(row, rows), pl.ds(start, width)],
                out.at[pl.ds(row, rows), :],
                out_sem.at[n],
            )
            copy.start()
            pending.append(copy)
            start += width
            n += 1
    for copy in pending:
        copy.wait()


def assemble(me, pieces, rows, splits):
    cols = sum(splits)
    total = 8 * rows
    return pl.pallas_call(
        functools.partial(assemble_kernel, rows, cols, splits),
        out_shape=[jax.ShapeDtypeStruct((total, width), BF) for width in splits],
        in_specs=[pl.BlockSpec(memory_space=pltpu.SMEM)] + [pl.BlockSpec(memory_space=ANY)] * 4,
        out_specs=[pl.BlockSpec(memory_space=ANY)] * len(splits),
        scratch_shapes=[
            pltpu.VMEM((total, cols), BF),
            pltpu.SemaphoreType.DMA((26,)),
            pltpu.SemaphoreType.DMA((8 * len(splits),)),
        ],
        cost_estimate=pl.CostEstimate(
            flops=0, bytes_accessed=4 * total * cols, transcendentals=0
        ),
    )(me, *pieces)


def pack_kernel(spans, me, *refs):
    shards, (own, part) = refs[:-2], refs[-2:]
    at = 0
    for number, start, stop in spans:
        own[:, at : at + stop - start] = shards[number][:, start:stop]
        at += stop - start
    quarter = part.shape[1]
    part[...] = own[:, pl.ds(pl.multiple_of(me[2] * quarter, 128), quarter)]


def pack(me, shards, spans):
    rows = shards[0].shape[0]
    cols = sum(stop - start for number, start, stop in spans)
    return vmem_call(
        functools.partial(pack_kernel, spans),
        [
            jax.ShapeDtypeStruct((rows, cols), BF),
            jax.ShapeDtypeStruct((rows, cols // 4), BF),
        ],
        list(shards),
        pos=me,
        moved=5 * rows * cols,
    )


def planes_kernel(*refs):
    pieces, out, (buf, in_sem, out_sem) = refs[:-4], refs[-4], refs[-3:]
    copies, at = [], 0
    for number, piece in enumerate(pieces):
        here = pl.ds(at, piece.shape[0])
        copies.append(
            (
                pltpu.make_async_copy(piece, buf.at[here], in_sem.at[number]),
                pltpu.make_async_copy(buf.at[here], out.at[here], out_sem.at[number]),
            )
        )
        at += piece.shape[0]
    for first, second in copies:
        first.start()
    for first, second in copies:
        first.wait()
        second.start()
    for first, second in copies:
        second.wait()


def together(values):
    shape = (sum(value.shape[0] for value in values),) + values[0].shape[1:]
    return pl.pallas_call(
        planes_kernel,
        out_shape=jax.ShapeDtypeStruct(shape, BF),
        in_specs=[pl.BlockSpec(memory_space=ANY)] * len(values),
        out_specs=pl.BlockSpec(memory_space=ANY),
        scratch_shapes=[
            pltpu.VMEM(shape, BF),
            pltpu.SemaphoreType.DMA((len(values),)),
            pltpu.SemaphoreType.DMA((len(values),)),
        ],
        cost_estimate=pl.CostEstimate(
            flops=0, bytes_accessed=4 * math.prod(shape), transcendentals=0
        ),
    )(*values)


class Steps:
    def __init__(self, generator):
        self.generator, self.result, self.pending = generator, None, []
        self.sends = next(generator)

    def take(self, values):
        if self.pending:
            self.pending = []
            try:
                self.sends = self.generator.send(values)
            except StopIteration as stop:
                self.sends, self.result = [], stop.value

    def launch(self, values):
        if self.sends:
            self.pending = [swap(v, axis, bit) for v, (u, axis, bit) in zip(values, self.sends)]
            self.sends = []


def sync(values, *steps, hold=()):
    values = list(values)
    count = len(values)
    waited = list(steps) + list(hold)
    pending = [piece for step in waited for piece in step.pending]
    flat = list(lax.optimization_barrier(tuple(values + pending)))
    values, at = flat[:count], count
    for step in waited:
        size = len(step.pending)
        step.take(flat[at : at + size])
        at += size
    sends = [send[0] for step in steps for send in step.sends]
    flat = list(lax.optimization_barrier(tuple(values + sends)))
    values, at = flat[:count], count
    for step in steps:
        size = len(step.sends)
        step.launch(flat[at : at + size])
        at += size
    return values


def gather_steps(me, shards, spans, splits, flip):
    own, part = pack(me, shards, spans)
    rows, cols = own.shape
    along_z = yield [(part, "mp", bit) for bit in (1, 2, 3)]
    first, second = (1, 2) if flip else (2, 1)
    a0 = together([piece[None] for piece in along_z])
    hop, side = yield [(a0, "dp", first), (a0, "dp", second)]
    far, own_theirs = yield [(hop, "dp", second), (own, "fsdp", 1)]
    planes = together([a0, hop, side, far] if flip else [a0, side, hop, far])
    (planes_theirs,) = yield [(planes, "fsdp", 1)]
    return assemble(me, [own, planes, own_theirs, planes_theirs], rows, splits)


def rs_add_kernel(pos, ka_s, ka_k, kb_s, kb_k, ra_s, ra_k, rb_s, rb_k, sa, sb, keep):
    sa[...] = (ka_s[...].astype(F32) + ra_s[...].astype(F32)).astype(BF)
    sb[...] = (kb_s[...].astype(F32) + rb_s[...].astype(F32)).astype(BF)
    keep[0] = (ka_k[...].astype(F32) + ra_k[...].astype(F32)).astype(BF)
    keep[1] = (kb_k[...].astype(F32) + rb_k[...].astype(F32)).astype(BF)


def rs_z_kernel(pos, *refs):
    keeps, ras, rbs, outs = refs[:4], refs[4:8], refs[8:12], refs[12:]
    z = pos[1]
    for k in range(4):
        low = (z ^ k) < 2
        recv = jnp.where(low, ras[k][0].astype(F32), rbs[k][0].astype(F32))
        outs[k][...] = (keeps[k][0].astype(F32) + recv).astype(BF)


def rs_last_kernel(own, r1, r2, r3, out):
    out[...] = (
        (own[...].astype(F32) + r1[...].astype(F32)) + (r2[...].astype(F32) + r3[...].astype(F32))
    ).astype(BF)


def rs_place_kernel(places, pos, *refs):
    pieces, outs, buf = refs[: -1 - len(places)], refs[-1 - len(places) : -1], refs[-1]
    quarter = pieces[0].shape[-1]
    z, p = pos[1], pos[2]
    for j in range(4):
        if len(pieces) == 1:
            q, piece = j, pieces[0][j]
        else:
            q, piece = p ^ j, pieces[j][...]
        col = jnp.where(z < 2, (q & 1) * 2 + (q >> 1), q) * quarter
        buf[:, pl.ds(pl.multiple_of(col, 128), quarter)] = piece.astype(F32)
    for out, (shape, copies) in zip(outs, places):
        for to_rows, to_cols, from_rows, from_cols in copies:
            out[to_rows, to_cols] = buf[from_rows, from_cols]


def block_chunks(rows, cols, height):
    chunks = []
    for t in range(cols // 128):
        at = 0
        while at < rows:
            block, inside = divmod(t * rows + at, height)
            size = min(height - inside, rows - at)
            chunks.append((slice(at, at + size), t, slice(inside, inside + size), block))
            at += size
    return chunks


def lane_tile(t):
    return slice(128 * t, 128 * t + 128)


def reblock_kernel(height, grad_ref, out_ref):
    rows, cols = grad_ref.shape
    out_ref[:, rows * cols // height :] = jnp.zeros_like(out_ref[:, rows * cols // height :])
    for from_rows, t, to_rows, block in block_chunks(rows, cols, height):
        out_ref[to_rows, lane_tile(block)] = grad_ref[from_rows, lane_tile(t)]


def ffn_pack_kernel(gate_ref, up_ref, down_ref, pos, out_ref, buf):
    height, ff = gate_ref.shape
    buf[:, :ff] = gate_ref[...]
    buf[:, ff : 2 * ff] = up_ref[...]
    for from_rows, t, to_rows, block in block_chunks(*down_ref.shape, height):
        buf[to_rows, lane_tile(2 * ff // 128 + block)] = down_ref[from_rows, lane_tile(t)]
    count = out_ref.shape[0]
    out_ref[...] = buf[pl.ds(pl.multiple_of(pos[2] * count, count), count), :]


def ffn_pack(me, gate, up, down):
    height, ff = gate.shape
    vmem = pl.BlockSpec(memory_space=pltpu.VMEM)
    cols = 2 * ff + down.size // height
    return pl.pallas_call(
        ffn_pack_kernel,
        out_shape=jax.ShapeDtypeStruct((height // 4, cols), BF),
        in_specs=[vmem, vmem, vmem, pl.BlockSpec(memory_space=pltpu.SMEM)],
        out_specs=vmem,
        scratch_shapes=[pltpu.VMEM((height, cols), BF)],
        cost_estimate=pl.CostEstimate(
            flops=0, bytes_accessed=3 * height * cols, transcendentals=0
        ),
    )(gate, up, down, me)


def unblock_kernel(blocks_ref, out_ref):
    for to_rows, t, from_rows, block in block_chunks(*out_ref.shape, blocks_ref.shape[0]):
        out_ref[to_rows, lane_tile(t)] = blocks_ref[from_rows, lane_tile(block)]


def unblock(packed, rows, cols):
    height, width = packed.shape[0] // 8, 8 * rows * cols // packed.shape[0]
    last = packed.shape[1] // width - 1
    return pl.pallas_call(
        unblock_kernel,
        grid=(8,),
        in_specs=[pl.BlockSpec((height, width), lambda i: (i, last))],
        out_specs=pl.BlockSpec((rows, cols), lambda i: (i, 0)),
        out_shape=jax.ShapeDtypeStruct((8 * rows, cols), BF),
        cost_estimate=pl.CostEstimate(
            flops=0, bytes_accessed=32 * rows * cols, transcendentals=0
        ),
    )(packed)


def reblock(grad, height, width):
    rows, cols = grad.shape[0] // 8, grad.shape[1]
    return pl.pallas_call(
        functools.partial(reblock_kernel, height),
        grid=(8,),
        in_specs=[pl.BlockSpec((rows, cols), lambda i: (i, 0))],
        out_specs=pl.BlockSpec((height, width), lambda i: (i, 0)),
        out_shape=jax.ShapeDtypeStruct((8 * height, width), BF),
        cost_estimate=pl.CostEstimate(
            flops=0, bytes_accessed=4 * grad.size, transcendentals=0
        ),
    )(grad)


def vmem_call(kernel, outs, ins, pos=None, scratch=(), moved=0):
    specs = [pl.BlockSpec(memory_space=pltpu.VMEM)] * len(ins)
    args = list(ins)
    if pos is not None:
        specs = [pl.BlockSpec(memory_space=pltpu.SMEM)] + specs
        args = [pos] + args
    return pl.pallas_call(
        kernel,
        out_shape=outs,
        in_specs=specs,
        out_specs=jax.tree.map(lambda _: pl.BlockSpec(memory_space=pltpu.VMEM), outs),
        scratch_shapes=list(scratch),
        cost_estimate=pl.CostEstimate(flops=0, bytes_accessed=moved, transcendentals=0),
    )(*args)


def scatter_steps(me, parts, places, wide):
    c, x, y = me[0], me[2] & 1, me[2] >> 1
    sent = half_grads(1 - me[:1], parts)
    (got,) = yield [(sent, "fsdp", 1)]
    kept = half_grads(me[:1], parts, got)
    half, cols = kept.shape
    rows, quarter = half // 4, cols // 4
    two = 2 * rows
    send_a = lax.dynamic_slice(kept, (0, (1 - x) * 2 * quarter), (two, 2 * quarter))
    send_b = lax.dynamic_slice(kept, (two, (1 - y) * 2 * quarter), (two, 2 * quarter))
    recv_a, recv_b = yield [(send_a, "dp", 1), (send_b, "dp", 2)]
    send_c, send_d, keep = rs_add(me, kept, recv_a, recv_b)
    recv_c, recv_d = yield [(send_c, "dp", 2), (send_d, "dp", 1)]
    pieces = rs_z(me, keep, recv_c, recv_d)
    gots = yield [(pieces[k], "mp", k) for k in (1, 2, 3)]
    piece = vmem_call(
        rs_last_kernel,
        jax.ShapeDtypeStruct((rows, quarter), BF),
        [pieces[0]] + gots,
        moved=10 * rows * quarter,
    )
    if wide:
        around = lax.all_gather(piece, "dp")
    else:
        around = yield [(piece, "dp", k) for k in (1, 2, 3)]
        around = [piece] + around
    return vmem_call(
        functools.partial(rs_place_kernel, places),
        [jax.ShapeDtypeStruct(shape, F32) for shape, copies in places],
        [around] if wide else around,
        pos=me,
        scratch=[pltpu.VMEM((rows, cols), F32)],
        moved=6 * rows * cols,
    )


def rs_add(me, kept, recv_a, recv_b):
    half, cols = kept.shape
    two, quarter = half // 2, cols // 4
    steps = 4 if two % 128 == 0 else 2
    block = two // steps

    def at(kind):
        def index(i, pos):
            px, py = pos[2] & 1, pos[2] >> 1
            return {
                "ka_s": (i, px * 2 + 1 - py),
                "ka_k": (i, px * 2 + py),
                "kb_s": (steps + i, py * 2 + 1 - px),
                "kb_k": (steps + i, py * 2 + px),
                "ra_s": (i, 1 - py),
                "ra_k": (i, py),
                "rb_s": (i, 1 - px),
                "rb_k": (i, px),
            }[kind]

        return pl.BlockSpec((block, quarter), index)

    return pl.pallas_call(
        rs_add_kernel,
        out_shape=[
            jax.ShapeDtypeStruct((two, quarter), BF),
            jax.ShapeDtypeStruct((two, quarter), BF),
            jax.ShapeDtypeStruct((2, two, quarter), BF),
        ],
        grid_spec=pltpu.PrefetchScalarGridSpec(
            num_scalar_prefetch=1,
            grid=(steps,),
            in_specs=[
                at(k) for k in ("ka_s", "ka_k", "kb_s", "kb_k", "ra_s", "ra_k", "rb_s", "rb_k")
            ],
            out_specs=[
                pl.BlockSpec((block, quarter), lambda i, pos: (i, 0)),
                pl.BlockSpec((block, quarter), lambda i, pos: (i, 0)),
                pl.BlockSpec((2, block, quarter), lambda i, pos: (0, i, 0)),
            ],
        ),
        cost_estimate=pl.CostEstimate(
            flops=0, bytes_accessed=6 * half * quarter * 2, transcendentals=0
        ),
    )(me, kept, kept, kept, kept, recv_a, recv_a, recv_b, recv_b)


def rs_z(me, keep, recv_c, recv_d):
    rows, quarter = recv_c.shape[0] // 2, recv_c.shape[1]
    recv_c = recv_c.reshape(2, rows, quarter)
    recv_d = recv_d.reshape(2, rows, quarter)
    keep = keep.reshape(4, rows, quarter)

    def zspec(k, wrap):
        def index(i, pos):
            zz = pos[1] ^ k
            return ((zz & 1) if wrap else zz, 0, 0)

        return pl.BlockSpec((1, rows, quarter), index)

    return pl.pallas_call(
        rs_z_kernel,
        out_shape=[jax.ShapeDtypeStruct((rows, quarter), BF)] * 4,
        grid_spec=pltpu.PrefetchScalarGridSpec(
            num_scalar_prefetch=1,
            grid=(1,),
            in_specs=[zspec(k, w) for w in (False, True, True) for k in range(4)],
            out_specs=[pl.BlockSpec((rows, quarter), lambda i, pos: (0, 0))] * 4,
        ),
        cost_estimate=pl.CostEstimate(
            flops=0, bytes_accessed=16 * rows * quarter * 2, transcendentals=0
        ),
    )(me, *([keep] * 4 + [recv_c] * 4 + [recv_d] * 4))


def special(sizes):
    return sizes == (4, 2, 4)


def gather_plain(shards, spans, splits):
    own = jnp.concatenate(
        [shards[number][:, start:stop] for number, start, stop in spans], axis=1
    )
    whole = lax.all_gather(own, ("fsdp", "mp"), axis=0, tiled=True)
    if len(splits) == 1:
        return [whole]
    return jnp.split(whole, np.cumsum(splits)[:-1], axis=1)


def scatter_plain(left, right):
    grad = weight_grad(left, right).astype(BF)
    grad = lax.psum_scatter(grad, ("fsdp", "mp"), scatter_dimension=0, tiled=True)
    return lax.psum(grad, "dp").astype(F32)


class Done:
    pending, sends = [], []

    def __init__(self, result):
        self.result = result

    def take(self, values):
        pass

    def launch(self, values):
        pass


def column_places(rows, spans):
    places = []
    for group in spans:
        copies, at = [], 0
        for start, stop in group:
            copies.append(
                (slice(0, rows), slice(at, at + stop - start), slice(0, rows), slice(start, stop))
            )
            at += stop - start
        places.append(((rows, at), tuple(copies)))
    return tuple(places)


def shards(
    sizes,
    dec_input,
    enc_output,
    image_pairs,
    text_lengths,
    dec_lengths,
    self_query,
    self_key,
    self_value,
    self_out,
    cross_query,
    cross_key,
    cross_value,
    cross_out,
    ffn_gate,
    ffn_up,
    ffn_down,
    norm_first,
    norm_second,
    norm_third,
    bias_table,
    cotangent,
):
    item_count, length, model_width = dec_input.shape
    enc_len = enc_output.shape[1]
    bucket_count, head_count = bias_table.shape
    row_count = item_count * length
    enc_count = item_count * enc_len
    ff = ffn_gate.shape[1]
    me = place()

    chips = special(sizes)

    def gather(number, *group, spans=None, splits=None):
        spans = spans or tuple((n, 0, shard.shape[1]) for n, shard in enumerate(group))
        splits = splits or (sum(shard.shape[1] for shard in group),)
        if chips:
            return Steps(gather_steps(me, group, spans, splits, number % 2 == 0))
        return Done(gather_plain(group, spans, splits))

    weight_rows = self_query.shape[0]
    down_rows = ffn_down.shape[0]

    def scatter(parts, places, plain, wide=False):
        if chips:
            return Steps(scatter_steps(me, parts(), places, wide))
        return Done(plain())

    def spans_of(first, count):
        return tuple(
            ((k * model_width, (k + 1) * model_width),) for k in range(first, first + count)
        )

    def striped(width):
        return tuple(
            tuple(
                (2 * start + shift, 2 * start + shift + STRIPE)
                for start in range(0, width, STRIPE)
            )
            for shift in (0, STRIPE)
        )

    def scatter_striped(left, right):
        whole = scatter_plain(left, right)
        return [
            jnp.concatenate([whole[:, start:stop] for start, stop in spans], axis=1)
            for spans in striped(right.shape[1] // 2)
        ]

    buckets = jnp.asarray(bucket_table(length).T.reshape(-1))
    onehot = (buckets[None, :] == jnp.arange(bucket_count)[:, None]).astype(F32)
    relative = lax.dot_general(
        bias_table.astype(F32), onehot, (((0,), (0,)), ((), ())), precision=lax.Precision.HIGHEST
    )
    relative = relative.reshape(head_count // 2, 2, length, length).transpose(0, 2, 1, 3)
    relative = relative.reshape(head_count // 2, length, 2 * length)

    gains = jnp.stack([norm_first, norm_second, norm_third], axis=1)
    gains = jnp.pad(gains, ((0, 0), (0, 512 - gains.shape[1])))
    g_kv = gather(0, cross_key, cross_value, spans=stripes(model_width))
    g_qkv = gather(1, self_query, self_key, self_value, gains, splits=(3 * model_width, 512))
    g_mid = gather(0, self_out, cross_query, cross_out, splits=(model_width,) * 3)
    enc_rows = enc_output.reshape(enc_count, model_width)
    block = 2 * length
    blocks = enc_count // block
    sync([], g_kv)
    sync([send[0] for step in (g_qkv, g_mid) for send in step.sends[:1]], g_kv, g_qkv)
    if chips:
        (ffn_part,) = sync([ffn_pack(me, ffn_gate, ffn_up, ffn_down)], g_kv)
        ffn_full = lax.all_gather(ffn_part, ("fsdp", "mp", "dp"), axis=0, tiled=True)
    sync([], g_kv)
    sync([], hold=(g_kv,))
    (kv_full,) = g_kv.result

    inputs = dec_input.astype(F32).reshape(row_count, model_width)
    cross_kv = rows_part(enc_rows, kv_full, NN, BF, 0, blocks // 2, block)
    (cross_kv,) = sync([cross_kv], g_qkv, g_mid)
    cross_kv = rows_part(
        enc_rows, kv_full, NN, BF, blocks // 2, blocks - blocks // 2, block, cross_kv
    )
    (cross_kv,) = sync([cross_kv], g_qkv, hold=(g_mid,))
    sync([], g_qkv, g_mid)
    sync([], hold=(g_qkv,))
    qkv_full, gains = g_qkv.result
    gains = gains[:, :PAIR].T.astype(F32)
    gain_first, gain_second, gain_third = gains[0], gains[1], gains[2]
    normed_first = norm_rows(inputs, gain_first).astype(BF)
    qkv = matmul(normed_first, qkv_full).astype(BF)
    qkv, cross_kv = sync([qkv, cross_kv], g_mid)
    self_flat, self_lse = self_fwd(dec_lengths, qkv, relative)
    (self_flat,) = sync([self_flat], g_mid)
    sync([], hold=(g_mid,))
    out_full, cquery_full, cout_full = g_mid.result
    first_sum = inputs + matmul(self_flat, out_full)
    normed_second = norm_rows(first_sum, gain_second).astype(BF)
    cross_queries = matmul(normed_second, cquery_full).astype(BF)
    cross_flat, cross_lse = cross_fwd(image_pairs, text_lengths, cross_queries, cross_kv)
    out_grad = cotangent.reshape(row_count, model_width)
    second_sum = first_sum + matmul(cross_flat, cout_full)
    normed_third = norm_rows(second_sum, gain_third).astype(BF)
    if chips:
        weights = (ffn_full, ffn_full, ff, unblock(ffn_full, ffn_down.shape[0], model_width))
    else:
        gate_full, up_full, down_full = (
            lax.all_gather(shard, ("fsdp", "mp"), axis=0, tiled=True)
            for shard in (ffn_gate, ffn_up, ffn_down)
        )
        weights = (gate_full, up_full, 0, down_full)
    hidden, gu_grad, dec_output, third_normed_grad = ffn(
        normed_third, out_grad, second_sum, *weights
    )
    dec_output = dec_output.reshape(item_count, length, model_width)
    padded = -(-(2 * ff + down_rows * model_width // weight_rows) // 512) * 512 - 2 * ff
    s_ffn = scatter(
        lambda: [
            (normed_third, gu_grad),
            (reblock(weight_grad(hidden, out_grad).astype(BF), weight_rows, padded),),
        ],
        column_places(weight_rows, striped(ff))
        + (
            (
                (down_rows, model_width),
                tuple(
                    (to_rows, lane_tile(t), from_rows, lane_tile(2 * ff // 128 + block))
                    for to_rows, t, from_rows, block in block_chunks(
                        down_rows, model_width, weight_rows
                    )
                ),
            ),
        ),
        lambda: scatter_striped(normed_third, gu_grad) + [scatter_plain(hidden, out_grad)],
        wide=True,
    )
    (third_normed_grad,) = sync([third_normed_grad], s_ffn)

    unused_value, pullback = jax.vjp(norm_rows, second_sum, gain_third)
    second_part, norm_third_grad = pullback(third_normed_grad)
    second_grad = cotangent.astype(F32).reshape(row_count, model_width) + second_part
    branch_second = second_grad.astype(BF)
    cross_mixed_grad = input_grad(branch_second, cout_full).astype(BF)
    (cross_mixed_grad,) = sync([cross_mixed_grad], s_ffn)

    cq_rows, ckv_rows = cross_bwd(
        image_pairs, text_lengths, cross_queries, cross_kv, cross_lse, cross_mixed_grad
    )
    cq_rows, ckv_rows = sync([cq_rows, ckv_rows], s_ffn)

    second_normed_grad = input_grad(cq_rows, cquery_full)
    unused_value, pullback = jax.vjp(norm_rows, first_sum, gain_second)
    first_part, norm_second_grad = pullback(second_normed_grad)
    first_grad = second_grad + first_part
    branch_first = first_grad.astype(BF)
    self_mixed_grad = input_grad(branch_first, out_full).astype(BF)
    qkv_rows, score_total = self_bwd(dec_lengths, qkv, relative, self_lse, self_mixed_grad)
    s_self = scatter(
        lambda: [
            (self_flat, branch_first),
            (normed_first, qkv_rows),
            (normed_second, cq_rows),
            (cross_flat, branch_second),
        ],
        column_places(weight_rows, spans_of(0, 6)),
        lambda: [scatter_plain(self_flat, branch_first)]
        + jnp.split(scatter_plain(normed_first, qkv_rows), 3, axis=1)
        + [scatter_plain(normed_second, cq_rows), scatter_plain(cross_flat, branch_second)],
    )
    qkv_rows, ckv_rows = sync([qkv_rows, ckv_rows], s_self, s_ffn)

    qkv_rows, ckv_rows = sync([qkv_rows, ckv_rows], s_self)
    enc_grad = weight_grad(enc_rows, ckv_rows).astype(BF) if chips else None
    score_total = score_total.reshape(head_count // 2, length, 2, length).transpose(0, 2, 1, 3)
    table_part = lax.dot_general(
        onehot,
        score_total.reshape(head_count, length * length),
        (((1,), (1,)), ((), ())),
        precision=lax.Precision.HIGHEST,
    )
    first_normed_grad = input_grad(qkv_rows, qkv_full)
    unused_value, pullback = jax.vjp(norm_rows, inputs, gain_first)
    input_part, norm_first_grad = pullback(first_normed_grad)
    dec_input_grad = first_grad + input_part
    gain_grads = jnp.stack([norm_first_grad, norm_second_grad, norm_third_grad], axis=1)
    if chips:
        copies = jnp.tile(table_part.reshape(weight_rows, -1), (8, 1))
        small = jnp.concatenate([gain_grads, copies], axis=1)
        small = jnp.pad(small, ((0, 0), (0, 512 - small.shape[1]))).astype(BF)
    else:
        small = gain_grads
    s_cross = scatter(
        lambda: [(enc_grad,), (small,)],
        column_places(
            weight_rows,
            striped(model_width) + (((2 * model_width, 2 * model_width + PAIR),),),
        ),
        lambda: scatter_striped(enc_rows, ckv_rows),
    )
    (dec_input_grad,) = sync([dec_input_grad], s_self, s_cross, hold=(s_ffn,))
    dec_input_grad = dec_input_grad.reshape(item_count, length, model_width)

    part = blocks // 3
    enc_output_grad = rows_part(ckv_rows, kv_full, NT, F32, 0, part, block)
    (enc_output_grad,) = sync([enc_output_grad], s_self, s_cross)
    enc_output_grad = rows_part(ckv_rows, kv_full, NT, F32, part, part, block, enc_output_grad)
    (enc_output_grad,) = sync([enc_output_grad], s_cross)
    enc_output_grad = rows_part(
        ckv_rows, kv_full, NT, F32, 2 * part, blocks - 2 * part, block, enc_output_grad
    )
    (enc_output_grad,) = sync([enc_output_grad], hold=(s_self,))
    enc_output_grad = enc_output_grad.reshape(item_count, enc_len, model_width)
    sync([], s_self, hold=(s_cross,))
    sync([], s_cross, hold=(s_self,))
    sync([], s_cross)
    sync([], s_cross)
    ffn_gate_grad, ffn_up_grad, ffn_down_grad = s_ffn.result
    cross_key_grad, cross_value_grad, *small = s_cross.result
    (
        self_out_grad,
        self_query_grad,
        self_key_grad,
        self_value_grad,
        cross_query_grad,
        cross_out_grad,
    ) = s_self.result

    if chips:
        gain_grads = [small[0][:, k] for k in range(3)]
        count = table_part.size // weight_rows
        bias_table_grad = small[0][:, 3 : 3 + count].reshape(bucket_count, head_count)
    else:
        gain_width = norm_first.shape[0]
        start = (lax.axis_index("fsdp") * sizes[2] + lax.axis_index("mp")) * gain_width
        gain_grads = lax.psum(gain_grads, ("dp", "fsdp", "mp"))
        gain_grads = list(lax.dynamic_slice_in_dim(gain_grads, start, gain_width).T)
        bias_table_grad = lax.psum(table_part, ("dp", "fsdp", "mp"))

    return (
        dec_output,
        dec_input_grad,
        enc_output_grad,
        self_query_grad,
        self_key_grad,
        self_value_grad,
        self_out_grad,
        cross_query_grad,
        cross_key_grad,
        cross_value_grad,
        cross_out_grad,
        ffn_gate_grad,
        ffn_up_grad,
        ffn_down_grad,
        gain_grads[0],
        gain_grads[1],
        gain_grads[2],
        bias_table_grad,
    )


def solution(mesh):
    items = P(("dp", "fsdp", "mp"), None, None)
    item_numbers = P(("dp", "fsdp", "mp"))
    weight = P(("fsdp", "mp"), None)
    gain = P(("fsdp", "mp"))
    sizes = (mesh.shape["dp"], mesh.shape["fsdp"], mesh.shape["mp"])
    return jax.shard_map(
        functools.partial(shards, sizes),
        mesh=mesh,
        in_specs=(items, items)
        + (item_numbers,) * 3
        + (weight,) * 11
        + (gain,) * 3
        + (P(), items),
        out_specs=(items,) * 3 + (weight,) * 11 + (gain,) * 3 + (P(),),
        check_vma=False,
    )
```

```python
import functools
import math

import jax
import jax.numpy as jnp
import numpy as np
from jax import lax
from jax.experimental import pallas as pl
from jax.experimental.pallas import tpu as pltpu
from jax.sharding import PartitionSpec as P

PATCHES = 256
EPSILON = 1e-06
MASKED = -1000000000.0
GELU_COEF = 0.044715
BF = jnp.bfloat16
F32 = jnp.float32
ANY = pl.ANY


def bucket_table(length):
    rows_index = np.arange(length)[:, None]
    cols_index = np.arange(length)[None, :]
    distance = np.maximum(rows_index - cols_index, 0)
    spread = np.floor(np.log(np.maximum(distance, 1) / 16.0) / np.log(8.0) * 16.0)
    far_bucket = np.minimum(16.0 + spread, 31.0)
    return np.where(distance < 16, distance, far_bucket).astype(np.int32)


def norm_rows(values, gain):
    return values * lax.rsqrt(jnp.mean(values * values, axis=-1, keepdims=True) + EPSILON) * gain


def gelu_tanh(values):
    return (
        0.5
        * values
        * (
            1.0
            + jnp.tanh(math.sqrt(2.0 / math.pi) * (values + GELU_COEF * values * values * values))
        )
    )


def gated_unit(gate_values, up_values):
    return gelu_tanh(gate_values) * up_values


def matmul(left, right):
    return jnp.dot(left, right, preferred_element_type=F32)


def weight_grad(left, right):
    return lax.dot_general(left, right, (((0,), (0,)), ((), ())), preferred_element_type=F32)


def input_grad(upstream, weight):
    return lax.dot_general(upstream, weight, (((1,), (1,)), ((), ())), preferred_element_type=F32)


NT = (((1,), (1,)), ((), ()))
TN = (((0,), (0,)), ((), ()))
NN = (((1,), (0,)), ((), ()))
PAIR = 128
STRIPE = 256


def dot(left, right, dims=NN):
    return lax.dot_general(left, right, dims, preferred_element_type=F32)


def twice(block):
    low = lax.broadcasted_iota(jnp.int32, block.shape, 1) < block.shape[1] // 2
    zero = jnp.zeros_like(block)
    return jnp.concatenate([jnp.where(low, block, zero), jnp.where(low, zero, block)], axis=0)


def once(rows):
    half = rows.shape[0] // 2
    low = lax.broadcasted_iota(jnp.int32, (half, rows.shape[1]), 1) < rows.shape[1] // 2
    return jnp.where(low, rows[:half], rows[half:])


def cross_penalty(shape, axis, pairs, texts, item):
    slot = lax.broadcasted_iota(jnp.int32, shape, axis)
    valid = (slot < 2 * PATCHES * pairs[item]) | (
        (slot >= 4 * PATCHES) & (slot < 4 * PATCHES + texts[item])
    )
    return jnp.where(valid, 0.0, MASKED)


def pair_columns(t):
    per = STRIPE // PAIR
    start = (t // per) * 2 * STRIPE + (t % per) * PAIR
    return (
        slice(PAIR * t, PAIR * t + PAIR),
        slice(start, start + PAIR),
        slice(start + STRIPE, start + STRIPE + PAIR),
    )


def cross_fwd_kernel(pairs, texts, q_ref, kv_ref, o_ref, lse_ref):
    pen = cross_penalty((1, kv_ref.shape[0]), 1, pairs, texts, pl.program_id(0))
    for t in range(q_ref.shape[1] // PAIR):
        cols, kcols, vcols = pair_columns(t)
        s = dot(twice(q_ref[:, cols]), kv_ref[:, kcols], NT) + pen
        m = jnp.max(s, axis=1, keepdims=True)
        p = jnp.exp(s - m)
        total = jnp.sum(p, axis=1, keepdims=True)
        p = (p * (1.0 / total)).astype(BF)
        o_ref[:, cols] = once(dot(p, kv_ref[:, vcols])).astype(BF)
        lse = jnp.broadcast_to(m + jnp.log(total), (total.shape[0], PAIR))
        lse_ref[t] = jnp.transpose(lse)[:1]


def cross_bwd_kernel(pairs, texts, q_ref, kv_ref, lse_ref, do_ref, dq_ref, dkv_ref):
    pen = cross_penalty((kv_ref.shape[0], 1), 0, pairs, texts, pl.program_id(0))
    for t in range(q_ref.shape[1] // PAIR):
        cols, kcols, vcols = pair_columns(t)
        q2 = twice(q_ref[:, cols])
        do2 = twice(do_ref[:, cols])
        s = dot(kv_ref[:, kcols], q2, NT)
        p = jnp.exp(s + (pen - lse_ref[t]))
        dp = dot(kv_ref[:, vcols], do2, NT)
        delta = jnp.sum(p * dp, axis=0, keepdims=True)
        ds = (p * (dp - delta)).astype(BF)
        dkv_ref[:, vcols] = dot(p.astype(BF), do2).astype(BF)
        dkv_ref[:, kcols] = dot(ds, q2).astype(BF)
        dq_ref[:, cols] = once(dot(ds, kv_ref[:, kcols], TN)).astype(BF)


def cross_specs(slots, length, width, n):
    small = pl.BlockSpec((length, width), lambda i, j, *_: (i, j))
    big = pl.BlockSpec((slots, 2 * width), lambda i, j, *_: (i, j))
    lse = pl.BlockSpec((width // PAIR, 1, 2 * length), lambda i, j, *_: (i * n + j, 0, 0))
    return small, big, lse


def cross_fwd(pairs, texts, q, kv, width=2 * STRIPE):
    items, cols = pairs.shape[0], q.shape[1]
    slots, length, n = kv.shape[0] // items, q.shape[0] // items, cols // width
    small, big, lse = cross_specs(slots, length, width, n)
    return pl.pallas_call(
        cross_fwd_kernel,
        grid_spec=pltpu.PrefetchScalarGridSpec(
            num_scalar_prefetch=2,
            grid=(items, n),
            in_specs=[small, big],
            out_specs=[small, lse],
        ),
        out_shape=[
            jax.ShapeDtypeStruct(q.shape, BF),
            jax.ShapeDtypeStruct((items * cols // PAIR, 1, 2 * length), F32),
        ],
        cost_estimate=pl.CostEstimate(
            flops=16 * q.size * slots, bytes_accessed=2 * kv.size + 4 * q.size, transcendentals=0
        ),
    )(pairs, texts, q, kv)


def cross_bwd(pairs, texts, q, kv, lse, do, width=STRIPE):
    items, cols = pairs.shape[0], q.shape[1]
    slots, length, n = kv.shape[0] // items, q.shape[0] // items, cols // width
    small, big, lspec = cross_specs(slots, length, width, n)
    return pl.pallas_call(
        cross_bwd_kernel,
        grid_spec=pltpu.PrefetchScalarGridSpec(
            num_scalar_prefetch=2,
            grid=(items, n),
            in_specs=[small, big, lspec, small],
            out_specs=[small, big],
        ),
        out_shape=[jax.ShapeDtypeStruct(q.shape, BF), jax.ShapeDtypeStruct(kv.shape, BF)],
        cost_estimate=pl.CostEstimate(
            flops=40 * q.size * slots, bytes_accessed=4 * kv.size + 6 * q.size, transcendentals=0
        ),
    )(pairs, texts, q, kv, lse, do)


def self_valid(lens, item, length):
    key = lax.broadcasted_iota(jnp.int32, (length, length), 0)
    query = lax.broadcasted_iota(jnp.int32, (length, length), 1)
    valid = (key <= query) & (key < lens[item])
    return jnp.concatenate([valid.astype(jnp.int32)] * 2, axis=1) != 0


def self_columns(t, cols):
    start = PAIR * t
    return (
        slice(start, start + PAIR),
        slice(cols + start, cols + start + PAIR),
        slice(2 * cols + start, 2 * cols + start + PAIR),
    )


def self_fwd_kernel(lens, qkv_ref, bias_ref, o_ref, lse_ref):
    valid = self_valid(lens, pl.program_id(0), qkv_ref.shape[0])
    for t in range(o_ref.shape[1] // PAIR):
        cols, kcols, vcols = self_columns(t, o_ref.shape[1])
        s = dot(qkv_ref[:, kcols], twice(qkv_ref[:, cols]), NT) + bias_ref[t]
        s = jnp.where(valid, s, MASKED)
        m = jnp.max(s, axis=0, keepdims=True)
        p = jnp.exp(s - m)
        total = jnp.sum(p, axis=0, keepdims=True)
        p = (p * (1.0 / total)).astype(BF)
        o_ref[:, cols] = once(dot(p, qkv_ref[:, vcols], TN)).astype(BF)
        lse_ref[t] = m + jnp.log(total)


def self_bwd_kernel(lens, qkv_ref, bias_ref, lse_ref, do_ref, dqkv_ref, sum_ref):
    item = pl.program_id(0)
    valid = self_valid(lens, item, qkv_ref.shape[0])

    @pl.when(item == 0)
    def _():
        sum_ref[...] = jnp.zeros_like(sum_ref)

    for t in range(do_ref.shape[1] // PAIR):
        cols, kcols, vcols = self_columns(t, do_ref.shape[1])
        q2 = twice(qkv_ref[:, cols])
        do2 = twice(do_ref[:, cols])
        s = dot(qkv_ref[:, kcols], q2, NT) + bias_ref[t]
        p = jnp.where(valid, jnp.exp(s - lse_ref[t]), 0.0)
        dp = dot(qkv_ref[:, vcols], do2, NT)
        delta = jnp.sum(p * dp, axis=0, keepdims=True)
        ds = (p * (dp - delta)).astype(BF)
        dqkv_ref[:, vcols] = dot(p.astype(BF), do2).astype(BF)
        dqkv_ref[:, kcols] = dot(ds, q2).astype(BF)
        dqkv_ref[:, cols] = once(dot(ds, qkv_ref[:, kcols], TN)).astype(BF)
        sum_ref[t] += ds.astype(F32)


def self_specs(length, cols):
    one = pl.BlockSpec((length, cols), lambda i, *_: (i, 0))
    three = pl.BlockSpec((length, 3 * cols), lambda i, *_: (i, 0))
    bias = pl.BlockSpec((cols // PAIR, length, 2 * length), lambda i, *_: (0, 0, 0))
    lse = pl.BlockSpec((cols // PAIR, 1, 2 * length), lambda i, *_: (i, 0, 0))
    return one, three, bias, lse


def self_fwd(lens, qkv, bias):
    items, cols = lens.shape[0], qkv.shape[1] // 3
    length = qkv.shape[0] // items
    one, three, bspec, lse = self_specs(length, cols)
    return pl.pallas_call(
        self_fwd_kernel,
        grid_spec=pltpu.PrefetchScalarGridSpec(
            num_scalar_prefetch=1, grid=(items,), in_specs=[three, bspec], out_specs=[one, lse]
        ),
        out_shape=[
            jax.ShapeDtypeStruct((qkv.shape[0], cols), BF),
            jax.ShapeDtypeStruct((items * cols // PAIR, 1, 2 * length), F32),
        ],
        cost_estimate=pl.CostEstimate(
            flops=16 * qkv.size * length, bytes_accessed=4 * qkv.size, transcendentals=0
        ),
    )(lens, qkv, bias)


def self_bwd(lens, qkv, bias, lse, do):
    items, cols = lens.shape[0], qkv.shape[1] // 3
    length = qkv.shape[0] // items
    one, three, bspec, lspec = self_specs(length, cols)
    return pl.pallas_call(
        self_bwd_kernel,
        grid_spec=pltpu.PrefetchScalarGridSpec(
            num_scalar_prefetch=1,
            grid=(items,),
            in_specs=[three, bspec, lspec, one],
            out_specs=[three, bspec],
        ),
        out_shape=[jax.ShapeDtypeStruct(qkv.shape, BF), jax.ShapeDtypeStruct(bias.shape, F32)],
        cost_estimate=pl.CostEstimate(
            flops=16 * qkv.size * length, bytes_accessed=6 * qkv.size, transcendentals=0
        ),
    )(lens, qkv, bias, lse, do)


def rows_kernel(dims, rows_ref, weight_ref, *refs):
    refs[-1][...] = dot(rows_ref[...], weight_ref[...], dims).astype(refs[-1].dtype)


def rows_part(rows, weight, dims, dtype, first, count, block, before=None):
    total, inner = rows.shape
    cols = weight.shape[1 - dims[0][1][0]]
    before = [] if before is None else [before]
    return pl.pallas_call(
        functools.partial(rows_kernel, dims),
        grid=(count,),
        in_specs=[
            pl.BlockSpec((block, inner), lambda i: (first + i, 0)),
            pl.BlockSpec(weight.shape, lambda i: (0, 0)),
        ]
        + [pl.BlockSpec(memory_space=ANY)] * len(before),
        out_specs=pl.BlockSpec((block, cols), lambda i: (first + i, 0)),
        out_shape=jax.ShapeDtypeStruct((total, cols), dtype),
        input_output_aliases={2: 0} if before else {},
        cost_estimate=pl.CostEstimate(
            flops=2 * count * block * weight.size,
            bytes_accessed=count * block * (2 * inner + 4 * cols),
            transcendentals=0,
        ),
    )(rows, weight, *before)


def ffn_kernel(
    rows_ref, cot_ref, sum_ref, gate_ref, up_ref, down_ref,
    hidden_ref, dunits_ref, out_ref, drows_ref, acc,
):
    i = pl.program_id(0)
    rows, cot = rows_ref[...], cot_ref[...]
    gate, up, down = gate_ref[...], up_ref[...], down_ref[...]
    g = dot(rows, gate)
    u = dot(rows, up)
    dh = dot(cot, down, NT)
    scale = math.sqrt(2.0 / math.pi)
    square = g * g
    t = jnp.tanh(scale * (g + GELU_COEF * (square * g)))
    value = 0.5 * g * (1.0 + t)
    slope = 0.5 * (1.0 + t) + 0.5 * g * (1.0 - t * t) * (
        scale * (1.0 + 3.0 * GELU_COEF * square)
    )
    hidden = (value * u).astype(BF)
    dgate = (dh * u * slope).astype(BF)
    dup = (dh * value).astype(BF)
    hidden_ref[...] = hidden
    dunits_ref[:, :STRIPE] = dgate
    dunits_ref[:, STRIPE:] = dup
    out = dot(hidden, down)
    drows = dot(dgate, gate, NT) + dot(dup, up, NT)

    @pl.when(i == 0)
    def _():
        acc[...] = sum_ref[...] + out
        drows_ref[...] = drows

    @pl.when(i > 0)
    def _():
        acc[...] += out
        drows_ref[...] += drows

    @pl.when(i == pl.num_programs(0) - 1)
    def _():
        out_ref[...] = acc[...].astype(BF)


def ffn(rows, cot, total, gate, up, up_start, down):
    count, width = rows.shape
    ff = down.shape[0]
    block = STRIPE
    whole = pl.BlockSpec((count, width), lambda i: (0, 0))
    cols = pl.BlockSpec((width, block), lambda i: (0, i))
    later = pl.BlockSpec((width, block), lambda i: (0, up_start // block + i))
    units = pl.BlockSpec((count, block), lambda i: (0, i))
    both = pl.BlockSpec((count, 2 * block), lambda i: (0, i))
    return pl.pallas_call(
        ffn_kernel,
        grid=(ff // block,),
        in_specs=[whole, whole, whole, cols, later, pl.BlockSpec((block, width), lambda i: (i, 0))],
        out_specs=[units, both, whole, whole],
        out_shape=[
            jax.ShapeDtypeStruct((count, ff), BF),
            jax.ShapeDtypeStruct((count, 2 * ff), BF),
            jax.ShapeDtypeStruct((count, width), BF),
            jax.ShapeDtypeStruct((count, width), F32),
        ],
        scratch_shapes=[pltpu.VMEM((count, width), F32)],
        cost_estimate=pl.CostEstimate(
            flops=12 * count * width * ff,
            bytes_accessed=6 * width * ff + 6 * count * ff + 14 * count * width,
            transcendentals=0,
        ),
    )(rows, cot, total, gate, up, down)


def half_grads_kernel(layout, extra, pos, *refs):
    out, turned = refs[-2:]
    i = pl.program_id(0)
    at = 0
    for arity, first, last in layout:
        part = refs[at : at + arity]

        @pl.when(i == first)
        def _(part=part):
            if len(part) == 2:
                turned[...] = jnp.transpose(part[0][...])

        @pl.when((i >= first) & (i < last))
        def _(part=part):
            grad = dot(turned[...], part[1][...]) if len(part) == 2 else part[0][...]
            if extra:
                grad = grad.astype(F32) + refs[-3][...].astype(F32)
            out[...] = grad.astype(BF)

        at += arity


def half_grads(which, parts, got=None):
    widths = [part[-1].shape[1] for part in parts]
    block = 1024 if all(width % 1024 == 0 for width in widths) else 512
    half = (parts[0][0].shape[1] if len(parts[0]) == 2 else parts[0][0].shape[0]) // 2
    specs, args, layout, first = [], [], [], 0

    def column(rows, row, first, count):
        return pl.BlockSpec(
            (rows, block),
            lambda i, pos: (pos[0] if row else 0, jnp.clip(i - first, 0, count - 1)),
        )

    for part, width in zip(parts, widths):
        count = width // block
        if len(part) == 2:
            rows = part[0].shape[0]
            specs.append(pl.BlockSpec((rows, half), lambda i, pos: (0, pos[0])))
            specs.append(column(rows, False, first, count))
        else:
            specs.append(column(half, True, first, count))
        args += part
        layout.append((len(part), first, first + count))
        first += count
    here = pl.BlockSpec((half, block), lambda i, pos: (0, i))
    if got is not None:
        specs.append(here)
        args.append(got)
    return pl.pallas_call(
        functools.partial(half_grads_kernel, tuple(layout), got is not None),
        out_shape=jax.ShapeDtypeStruct((half, sum(widths)), BF),
        grid_spec=pltpu.PrefetchScalarGridSpec(
            num_scalar_prefetch=1,
            grid=(first,),
            in_specs=specs,
            out_specs=here,
            scratch_shapes=[pltpu.VMEM((half, max([part[0].shape[0] for part in parts if len(part) == 2] or [16])), BF)],
        ),
        cost_estimate=pl.CostEstimate(
            flops=2 * half * 512 * sum(widths),
            bytes_accessed=6 * half * sum(widths),
            transcendentals=0,
        ),
    )(which, *args)


def stripes(width):
    return tuple(
        (number, start, start + STRIPE) for start in range(0, width, STRIPE) for number in (0, 1)
    )


def swap(value, axis, bit):
    size = lax.axis_size(axis)
    return lax.ppermute(value, axis, [(i, i ^ bit) for i in range(size)])


def place():
    return jnp.stack(
        [lax.axis_index("fsdp"), lax.axis_index("mp"), lax.axis_index("dp")]
    ).astype(jnp.int32)


def assemble_kernel(rows, cols, splits, me, *refs):
    pieces, outs = refs[:4], refs[4 : 4 + len(splits)]
    buf, in_sem, out_sem = refs[4 + len(splits) :]
    c, z, p = me[0], me[1], me[2]
    quarter = cols // 4
    blocks = []
    n = 0
    for other in range(2):
        for zr in range(4):
            row = pl.multiple_of(((c ^ other) * 4 + (z ^ zr)) * rows, rows)
            copies = []
            if zr == 0:
                copies.append(
                    pltpu.make_async_copy(
                        pieces[2 * other], buf.at[pl.ds(row, rows), :], in_sem.at[n]
                    )
                )
                n += 1
            else:
                for j in range(4):
                    col = pl.multiple_of((p ^ j) * quarter, 128)
                    copies.append(
                        pltpu.make_async_copy(
                            pieces[2 * other + 1].at[3 * j + zr - 1],
                            buf.at[pl.ds(row, rows), pl.ds(col, quarter)],
                            in_sem.at[n],
                        )
                    )
                    n += 1
            for copy in copies:
                copy.start()
            blocks.append((row, copies))
    pending = []
    n = 0
    for row, copies in blocks:
        for copy in copies:
            copy.wait()
        start = 0
        for out, width in zip(outs, splits):
            copy = pltpu.make_async_copy(
                buf.at[pl.ds(row, rows), pl.ds(start, width)],
                out.at[pl.ds(row, rows), :],
                out_sem.at[n],
            )
            copy.start()
            pending.append(copy)
            start += width
            n += 1
    for copy in pending:
        copy.wait()


def assemble(me, pieces, rows, splits):
    cols = sum(splits)
    total = 8 * rows
    return pl.pallas_call(
        functools.partial(assemble_kernel, rows, cols, splits),
        out_shape=[jax.ShapeDtypeStruct((total, width), BF) for width in splits],
        in_specs=[pl.BlockSpec(memory_space=pltpu.SMEM)] + [pl.BlockSpec(memory_space=ANY)] * 4,
        out_specs=[pl.BlockSpec(memory_space=ANY)] * len(splits),
        scratch_shapes=[
            pltpu.VMEM((total, cols), BF),
            pltpu.SemaphoreType.DMA((26,)),
            pltpu.SemaphoreType.DMA((8 * len(splits),)),
        ],
        cost_estimate=pl.CostEstimate(
            flops=0, bytes_accessed=4 * total * cols, transcendentals=0
        ),
    )(me, *pieces)


def pack_kernel(spans, me, *refs):
    shards, (own, part) = refs[:-2], refs[-2:]
    at = 0
    for number, start, stop in spans:
        own[:, at : at + stop - start] = shards[number][:, start:stop]
        at += stop - start
    quarter = part.shape[1]
    part[...] = own[:, pl.ds(pl.multiple_of(me[2] * quarter, 128), quarter)]


def pack(me, shards, spans):
    rows = shards[0].shape[0]
    cols = sum(stop - start for number, start, stop in spans)
    return vmem_call(
        functools.partial(pack_kernel, spans),
        [
            jax.ShapeDtypeStruct((rows, cols), BF),
            jax.ShapeDtypeStruct((rows, cols // 4), BF),
        ],
        list(shards),
        pos=me,
        moved=5 * rows * cols,
    )


def planes_kernel(*refs):
    pieces, out, (buf, in_sem, out_sem) = refs[:-4], refs[-4], refs[-3:]
    copies, at = [], 0
    for number, piece in enumerate(pieces):
        here = pl.ds(at, piece.shape[0])
        copies.append(
            (
                pltpu.make_async_copy(piece, buf.at[here], in_sem.at[number]),
                pltpu.make_async_copy(buf.at[here], out.at[here], out_sem.at[number]),
            )
        )
        at += piece.shape[0]
    for first, second in copies:
        first.start()
    for first, second in copies:
        first.wait()
        second.start()
    for first, second in copies:
        second.wait()


def together(values):
    shape = (sum(value.shape[0] for value in values),) + values[0].shape[1:]
    return pl.pallas_call(
        planes_kernel,
        out_shape=jax.ShapeDtypeStruct(shape, BF),
        in_specs=[pl.BlockSpec(memory_space=ANY)] * len(values),
        out_specs=pl.BlockSpec(memory_space=ANY),
        scratch_shapes=[
            pltpu.VMEM(shape, BF),
            pltpu.SemaphoreType.DMA((len(values),)),
            pltpu.SemaphoreType.DMA((len(values),)),
        ],
        cost_estimate=pl.CostEstimate(
            flops=0, bytes_accessed=4 * math.prod(shape), transcendentals=0
        ),
    )(*values)


class Steps:
    def __init__(self, generator):
        self.generator, self.result, self.pending = generator, None, []
        self.sends = next(generator)

    def take(self, values):
        if self.pending:
            self.pending = []
            try:
                self.sends = self.generator.send(values)
            except StopIteration as stop:
                self.sends, self.result = [], stop.value

    def launch(self, values):
        if self.sends:
            self.pending = [swap(v, axis, bit) for v, (u, axis, bit) in zip(values, self.sends)]
            self.sends = []


def sync(values, *steps, hold=()):
    values = list(values)
    count = len(values)
    waited = list(steps) + list(hold)
    pending = [piece for step in waited for piece in step.pending]
    flat = list(lax.optimization_barrier(tuple(values + pending)))
    values, at = flat[:count], count
    for step in waited:
        size = len(step.pending)
        step.take(flat[at : at + size])
        at += size
    sends = [send[0] for step in steps for send in step.sends]
    flat = list(lax.optimization_barrier(tuple(values + sends)))
    values, at = flat[:count], count
    for step in steps:
        size = len(step.sends)
        step.launch(flat[at : at + size])
        at += size
    return values


def gather_steps(me, shards, spans, splits, flip):
    own, part = pack(me, shards, spans)
    rows, cols = own.shape
    along_z = yield [(part, "mp", bit) for bit in (1, 2, 3)]
    first, second = (1, 2) if flip else (2, 1)
    a0 = together([piece[None] for piece in along_z])
    hop, side = yield [(a0, "dp", first), (a0, "dp", second)]
    far, own_theirs = yield [(hop, "dp", second), (own, "fsdp", 1)]
    planes = together([a0, hop, side, far] if flip else [a0, side, hop, far])
    (planes_theirs,) = yield [(planes, "fsdp", 1)]
    return assemble(me, [own, planes, own_theirs, planes_theirs], rows, splits)


def rs_add_kernel(pos, ka_s, ka_k, kb_s, kb_k, ra_s, ra_k, rb_s, rb_k, sa, sb, keep):
    sa[...] = (ka_s[...].astype(F32) + ra_s[...].astype(F32)).astype(BF)
    sb[...] = (kb_s[...].astype(F32) + rb_s[...].astype(F32)).astype(BF)
    keep[0] = (ka_k[...].astype(F32) + ra_k[...].astype(F32)).astype(BF)
    keep[1] = (kb_k[...].astype(F32) + rb_k[...].astype(F32)).astype(BF)


def rs_z_kernel(pos, *refs):
    keeps, ras, rbs, outs = refs[:4], refs[4:8], refs[8:12], refs[12:]
    z = pos[1]
    for k in range(4):
        low = (z ^ k) < 2
        recv = jnp.where(low, ras[k][0].astype(F32), rbs[k][0].astype(F32))
        outs[k][...] = (keeps[k][0].astype(F32) + recv).astype(BF)


def rs_last_kernel(own, r1, r2, r3, out):
    out[...] = (
        (own[...].astype(F32) + r1[...].astype(F32)) + (r2[...].astype(F32) + r3[...].astype(F32))
    ).astype(BF)


def rs_place_kernel(places, pos, *refs):
    pieces, outs, buf = refs[: -1 - len(places)], refs[-1 - len(places) : -1], refs[-1]
    quarter = pieces[0].shape[-1]
    z, p = pos[1], pos[2]
    for j in range(4):
        if len(pieces) == 1:
            q, piece = j, pieces[0][j]
        else:
            q, piece = p ^ j, pieces[j][...]
        col = jnp.where(z < 2, (q & 1) * 2 + (q >> 1), q) * quarter
        buf[:, pl.ds(pl.multiple_of(col, 128), quarter)] = piece.astype(F32)
    for out, (shape, copies) in zip(outs, places):
        for to_rows, to_cols, from_rows, from_cols in copies:
            out[to_rows, to_cols] = buf[from_rows, from_cols]


def block_chunks(rows, cols, height):
    chunks = []
    for t in range(cols // 128):
        at = 0
        while at < rows:
            block, inside = divmod(t * rows + at, height)
            size = min(height - inside, rows - at)
            chunks.append((slice(at, at + size), t, slice(inside, inside + size), block))
            at += size
    return chunks


def lane_tile(t):
    return slice(128 * t, 128 * t + 128)


def reblock_kernel(height, grad_ref, out_ref):
    rows, cols = grad_ref.shape
    out_ref[:, rows * cols // height :] = jnp.zeros_like(out_ref[:, rows * cols // height :])
    for from_rows, t, to_rows, block in block_chunks(rows, cols, height):
        out_ref[to_rows, lane_tile(block)] = grad_ref[from_rows, lane_tile(t)]


def ffn_pack_kernel(gate_ref, up_ref, down_ref, pos, out_ref, buf):
    height, ff = gate_ref.shape
    buf[:, :ff] = gate_ref[...]
    buf[:, ff : 2 * ff] = up_ref[...]
    for from_rows, t, to_rows, block in block_chunks(*down_ref.shape, height):
        buf[to_rows, lane_tile(2 * ff // 128 + block)] = down_ref[from_rows, lane_tile(t)]
    count = out_ref.shape[0]
    out_ref[...] = buf[pl.ds(pl.multiple_of(pos[2] * count, count), count), :]


def ffn_pack(me, gate, up, down):
    height, ff = gate.shape
    vmem = pl.BlockSpec(memory_space=pltpu.VMEM)
    cols = 2 * ff + down.size // height
    return pl.pallas_call(
        ffn_pack_kernel,
        out_shape=jax.ShapeDtypeStruct((height // 4, cols), BF),
        in_specs=[vmem, vmem, vmem, pl.BlockSpec(memory_space=pltpu.SMEM)],
        out_specs=vmem,
        scratch_shapes=[pltpu.VMEM((height, cols), BF)],
        cost_estimate=pl.CostEstimate(
            flops=0, bytes_accessed=3 * height * cols, transcendentals=0
        ),
    )(gate, up, down, me)


def unblock_kernel(blocks_ref, out_ref):
    for to_rows, t, from_rows, block in block_chunks(*out_ref.shape, blocks_ref.shape[0]):
        out_ref[to_rows, lane_tile(t)] = blocks_ref[from_rows, lane_tile(block)]


def unblock(packed, rows, cols):
    height, width = packed.shape[0] // 8, 8 * rows * cols // packed.shape[0]
    last = packed.shape[1] // width - 1
    return pl.pallas_call(
        unblock_kernel,
        grid=(8,),
        in_specs=[pl.BlockSpec((height, width), lambda i: (i, last))],
        out_specs=pl.BlockSpec((rows, cols), lambda i: (i, 0)),
        out_shape=jax.ShapeDtypeStruct((8 * rows, cols), BF),
        cost_estimate=pl.CostEstimate(
            flops=0, bytes_accessed=32 * rows * cols, transcendentals=0
        ),
    )(packed)


def reblock(grad, height, width):
    rows, cols = grad.shape[0] // 8, grad.shape[1]
    return pl.pallas_call(
        functools.partial(reblock_kernel, height),
        grid=(8,),
        in_specs=[pl.BlockSpec((rows, cols), lambda i: (i, 0))],
        out_specs=pl.BlockSpec((height, width), lambda i: (i, 0)),
        out_shape=jax.ShapeDtypeStruct((8 * height, width), BF),
        cost_estimate=pl.CostEstimate(
            flops=0, bytes_accessed=4 * grad.size, transcendentals=0
        ),
    )(grad)


def vmem_call(kernel, outs, ins, pos=None, scratch=(), moved=0):
    specs = [pl.BlockSpec(memory_space=pltpu.VMEM)] * len(ins)
    args = list(ins)
    if pos is not None:
        specs = [pl.BlockSpec(memory_space=pltpu.SMEM)] + specs
        args = [pos] + args
    return pl.pallas_call(
        kernel,
        out_shape=outs,
        in_specs=specs,
        out_specs=jax.tree.map(lambda _: pl.BlockSpec(memory_space=pltpu.VMEM), outs),
        scratch_shapes=list(scratch),
        cost_estimate=pl.CostEstimate(flops=0, bytes_accessed=moved, transcendentals=0),
    )(*args)


def scatter_steps(me, parts, places, wide):
    c, x, y = me[0], me[2] & 1, me[2] >> 1
    sent = half_grads(1 - me[:1], parts)
    (got,) = yield [(sent, "fsdp", 1)]
    kept = half_grads(me[:1], parts, got)
    half, cols = kept.shape
    rows, quarter = half // 4, cols // 4
    two = 2 * rows
    send_a = lax.dynamic_slice(kept, (0, (1 - x) * 2 * quarter), (two, 2 * quarter))
    send_b = lax.dynamic_slice(kept, (two, (1 - y) * 2 * quarter), (two, 2 * quarter))
    recv_a, recv_b = yield [(send_a, "dp", 1), (send_b, "dp", 2)]
    send_c, send_d, keep = rs_add(me, kept, recv_a, recv_b)
    recv_c, recv_d = yield [(send_c, "dp", 2), (send_d, "dp", 1)]
    pieces = rs_z(me, keep, recv_c, recv_d)
    gots = yield [(pieces[k], "mp", k) for k in (1, 2, 3)]
    piece = vmem_call(
        rs_last_kernel,
        jax.ShapeDtypeStruct((rows, quarter), BF),
        [pieces[0]] + gots,
        moved=10 * rows * quarter,
    )
    if wide:
        around = lax.all_gather(piece, "dp")
    else:
        around = yield [(piece, "dp", k) for k in (1, 2, 3)]
        around = [piece] + around
    return vmem_call(
        functools.partial(rs_place_kernel, places),
        [jax.ShapeDtypeStruct(shape, F32) for shape, copies in places],
        [around] if wide else around,
        pos=me,
        scratch=[pltpu.VMEM((rows, cols), F32)],
        moved=6 * rows * cols,
    )


def rs_add(me, kept, recv_a, recv_b):
    half, cols = kept.shape
    two, quarter = half // 2, cols // 4
    steps = 4 if two % 128 == 0 else 2
    block = two // steps

    def at(kind):
        def index(i, pos):
            px, py = pos[2] & 1, pos[2] >> 1
            return {
                "ka_s": (i, px * 2 + 1 - py),
                "ka_k": (i, px * 2 + py),
                "kb_s": (steps + i, py * 2 + 1 - px),
                "kb_k": (steps + i, py * 2 + px),
                "ra_s": (i, 1 - py),
                "ra_k": (i, py),
                "rb_s": (i, 1 - px),
                "rb_k": (i, px),
            }[kind]

        return pl.BlockSpec((block, quarter), index)

    return pl.pallas_call(
        rs_add_kernel,
        out_shape=[
            jax.ShapeDtypeStruct((two, quarter), BF),
            jax.ShapeDtypeStruct((two, quarter), BF),
            jax.ShapeDtypeStruct((2, two, quarter), BF),
        ],
        grid_spec=pltpu.PrefetchScalarGridSpec(
            num_scalar_prefetch=1,
            grid=(steps,),
            in_specs=[
                at(k) for k in ("ka_s", "ka_k", "kb_s", "kb_k", "ra_s", "ra_k", "rb_s", "rb_k")
            ],
            out_specs=[
                pl.BlockSpec((block, quarter), lambda i, pos: (i, 0)),
                pl.BlockSpec((block, quarter), lambda i, pos: (i, 0)),
                pl.BlockSpec((2, block, quarter), lambda i, pos: (0, i, 0)),
            ],
        ),
        cost_estimate=pl.CostEstimate(
            flops=0, bytes_accessed=6 * half * quarter * 2, transcendentals=0
        ),
    )(me, kept, kept, kept, kept, recv_a, recv_a, recv_b, recv_b)


def rs_z(me, keep, recv_c, recv_d):
    rows, quarter = recv_c.shape[0] // 2, recv_c.shape[1]
    recv_c = recv_c.reshape(2, rows, quarter)
    recv_d = recv_d.reshape(2, rows, quarter)
    keep = keep.reshape(4, rows, quarter)

    def zspec(k, wrap):
        def index(i, pos):
            zz = pos[1] ^ k
            return ((zz & 1) if wrap else zz, 0, 0)

        return pl.BlockSpec((1, rows, quarter), index)

    return pl.pallas_call(
        rs_z_kernel,
        out_shape=[jax.ShapeDtypeStruct((rows, quarter), BF)] * 4,
        grid_spec=pltpu.PrefetchScalarGridSpec(
            num_scalar_prefetch=1,
            grid=(1,),
            in_specs=[zspec(k, w) for w in (False, True, True) for k in range(4)],
            out_specs=[pl.BlockSpec((rows, quarter), lambda i, pos: (0, 0))] * 4,
        ),
        cost_estimate=pl.CostEstimate(
            flops=0, bytes_accessed=16 * rows * quarter * 2, transcendentals=0
        ),
    )(me, *([keep] * 4 + [recv_c] * 4 + [recv_d] * 4))


def special(sizes):
    return sizes == (4, 2, 4)


def gather_plain(shards, spans, splits):
    own = jnp.concatenate(
        [shards[number][:, start:stop] for number, start, stop in spans], axis=1
    )
    whole = lax.all_gather(own, ("fsdp", "mp"), axis=0, tiled=True)
    if len(splits) == 1:
        return [whole]
    return jnp.split(whole, np.cumsum(splits)[:-1], axis=1)


def scatter_plain(left, right):
    grad = weight_grad(left, right).astype(BF)
    grad = lax.psum_scatter(grad, ("fsdp", "mp"), scatter_dimension=0, tiled=True)
    return lax.psum(grad, "dp").astype(F32)


class Done:
    pending, sends = [], []

    def __init__(self, result):
        self.result = result

    def take(self, values):
        pass

    def launch(self, values):
        pass


def column_places(rows, spans):
    places = []
    for group in spans:
        copies, at = [], 0
        for start, stop in group:
            copies.append(
                (slice(0, rows), slice(at, at + stop - start), slice(0, rows), slice(start, stop))
            )
            at += stop - start
        places.append(((rows, at), tuple(copies)))
    return tuple(places)


def shards(
    sizes,
    dec_input,
    enc_output,
    image_pairs,
    text_lengths,
    dec_lengths,
    self_query,
    self_key,
    self_value,
    self_out,
    cross_query,
    cross_key,
    cross_value,
    cross_out,
    ffn_gate,
    ffn_up,
    ffn_down,
    norm_first,
    norm_second,
    norm_third,
    bias_table,
    cotangent,
):
    item_count, length, model_width = dec_input.shape
    enc_len = enc_output.shape[1]
    bucket_count, head_count = bias_table.shape
    row_count = item_count * length
    enc_count = item_count * enc_len
    ff = ffn_gate.shape[1]
    me = place()

    chips = special(sizes)

    def gather(number, *group, spans=None, splits=None):
        spans = spans or tuple((n, 0, shard.shape[1]) for n, shard in enumerate(group))
        splits = splits or (sum(shard.shape[1] for shard in group),)
        if chips:
            return Steps(gather_steps(me, group, spans, splits, number % 2 == 0))
        return Done(gather_plain(group, spans, splits))

    weight_rows = self_query.shape[0]
    down_rows = ffn_down.shape[0]

    def scatter(parts, places, plain, wide=False):
        if chips:
            return Steps(scatter_steps(me, parts(), places, wide))
        return Done(plain())

    def spans_of(first, count):
        return tuple(
            ((k * model_width, (k + 1) * model_width),) for k in range(first, first + count)
        )

    def striped(width):
        return tuple(
            tuple(
                (2 * start + shift, 2 * start + shift + STRIPE)
                for start in range(0, width, STRIPE)
            )
            for shift in (0, STRIPE)
        )

    def scatter_striped(left, right):
        whole = scatter_plain(left, right)
        return [
            jnp.concatenate([whole[:, start:stop] for start, stop in spans], axis=1)
            for spans in striped(right.shape[1] // 2)
        ]

    buckets = jnp.asarray(bucket_table(length).T.reshape(-1))
    onehot = (buckets[None, :] == jnp.arange(bucket_count)[:, None]).astype(F32)
    relative = lax.dot_general(
        bias_table.astype(F32), onehot, (((0,), (0,)), ((), ())), precision=lax.Precision.HIGHEST
    )
    relative = relative.reshape(head_count // 2, 2, length, length).transpose(0, 2, 1, 3)
    relative = relative.reshape(head_count // 2, length, 2 * length)

    gains = jnp.stack([norm_first, norm_second, norm_third], axis=1)
    gains = jnp.pad(gains, ((0, 0), (0, 512 - gains.shape[1])))
    g_kv = gather(0, cross_key, cross_value, spans=stripes(model_width))
    g_qkv = gather(1, self_query, self_key, self_value, gains, splits=(3 * model_width, 512))
    g_mid = gather(0, self_out, cross_query, cross_out, splits=(model_width,) * 3)
    enc_rows = enc_output.reshape(enc_count, model_width)
    block = 2 * length
    blocks = enc_count // block
    sync([], g_kv)
    sync([send[0] for step in (g_qkv, g_mid) for send in step.sends[:1]], g_kv, g_qkv)
    if chips:
        (ffn_part,) = sync([ffn_pack(me, ffn_gate, ffn_up, ffn_down)], g_kv)
        ffn_full = lax.all_gather(ffn_part, ("fsdp", "mp", "dp"), axis=0, tiled=True)
    sync([], g_kv)
    sync([], hold=(g_kv,))
    (kv_full,) = g_kv.result

    inputs = dec_input.astype(F32).reshape(row_count, model_width)
    cross_kv = rows_part(enc_rows, kv_full, NN, BF, 0, blocks // 2, block)
    (cross_kv,) = sync([cross_kv], g_qkv, g_mid)
    cross_kv = rows_part(
        enc_rows, kv_full, NN, BF, blocks // 2, blocks - blocks // 2, block, cross_kv
    )
    (cross_kv,) = sync([cross_kv], g_qkv, hold=(g_mid,))
    sync([], g_qkv, g_mid)
    sync([], hold=(g_qkv,))
    qkv_full, gains = g_qkv.result
    gains = gains[:, :PAIR].T.astype(F32)
    gain_first, gain_second, gain_third = gains[0], gains[1], gains[2]
    normed_first = norm_rows(inputs, gain_first).astype(BF)
    qkv = matmul(normed_first, qkv_full).astype(BF)
    qkv, cross_kv = sync([qkv, cross_kv], g_mid)
    self_flat, self_lse = self_fwd(dec_lengths, qkv, relative)
    (self_flat,) = sync([self_flat], g_mid)
    sync([], hold=(g_mid,))
    out_full, cquery_full, cout_full = g_mid.result
    first_sum = inputs + matmul(self_flat, out_full)
    normed_second = norm_rows(first_sum, gain_second).astype(BF)
    cross_queries = matmul(normed_second, cquery_full).astype(BF)
    cross_flat, cross_lse = cross_fwd(image_pairs, text_lengths, cross_queries, cross_kv)
    out_grad = cotangent.reshape(row_count, model_width)
    second_sum = first_sum + matmul(cross_flat, cout_full)
    normed_third = norm_rows(second_sum, gain_third).astype(BF)
    if chips:
        weights = (ffn_full, ffn_full, ff, unblock(ffn_full, ffn_down.shape[0], model_width))
    else:
        gate_full, up_full, down_full = (
            lax.all_gather(shard, ("fsdp", "mp"), axis=0, tiled=True)
            for shard in (ffn_gate, ffn_up, ffn_down)
        )
        weights = (gate_full, up_full, 0, down_full)
    hidden, gu_grad, dec_output, third_normed_grad = ffn(
        normed_third, out_grad, second_sum, *weights
    )
    dec_output = dec_output.reshape(item_count, length, model_width)
    padded = -(-(2 * ff + down_rows * model_width // weight_rows) // 512) * 512 - 2 * ff
    s_ffn = scatter(
        lambda: [
            (normed_third, gu_grad),
            (reblock(weight_grad(hidden, out_grad).astype(BF), weight_rows, padded),),
        ],
        column_places(weight_rows, striped(ff))
        + (
            (
                (down_rows, model_width),
                tuple(
                    (to_rows, lane_tile(t), from_rows, lane_tile(2 * ff // 128 + block))
                    for to_rows, t, from_rows, block in block_chunks(
                        down_rows, model_width, weight_rows
                    )
                ),
            ),
        ),
        lambda: scatter_striped(normed_third, gu_grad) + [scatter_plain(hidden, out_grad)],
        wide=True,
    )
    (third_normed_grad,) = sync([third_normed_grad], s_ffn)

    unused_value, pullback = jax.vjp(norm_rows, second_sum, gain_third)
    second_part, norm_third_grad = pullback(third_normed_grad)
    second_grad = cotangent.astype(F32).reshape(row_count, model_width) + second_part
    branch_second = second_grad.astype(BF)
    cross_mixed_grad = input_grad(branch_second, cout_full).astype(BF)
    (cross_mixed_grad,) = sync([cross_mixed_grad], s_ffn)

    cq_rows, ckv_rows = cross_bwd(
        image_pairs, text_lengths, cross_queries, cross_kv, cross_lse, cross_mixed_grad
    )
    cq_rows, ckv_rows = sync([cq_rows, ckv_rows], s_ffn)

    second_normed_grad = input_grad(cq_rows, cquery_full)
    unused_value, pullback = jax.vjp(norm_rows, first_sum, gain_second)
    first_part, norm_second_grad = pullback(second_normed_grad)
    first_grad = second_grad + first_part
    branch_first = first_grad.astype(BF)
    self_mixed_grad = input_grad(branch_first, out_full).astype(BF)
    qkv_rows, score_total = self_bwd(dec_lengths, qkv, relative, self_lse, self_mixed_grad)
    s_self = scatter(
        lambda: [
            (self_flat, branch_first),
            (normed_first, qkv_rows),
            (normed_second, cq_rows),
            (cross_flat, branch_second),
        ],
        column_places(weight_rows, spans_of(0, 6)),
        lambda: [scatter_plain(self_flat, branch_first)]
        + jnp.split(scatter_plain(normed_first, qkv_rows), 3, axis=1)
        + [scatter_plain(normed_second, cq_rows), scatter_plain(cross_flat, branch_second)],
    )
    qkv_rows, ckv_rows = sync([qkv_rows, ckv_rows], s_self, s_ffn)

    qkv_rows, ckv_rows = sync([qkv_rows, ckv_rows], s_self)
    enc_grad = weight_grad(enc_rows, ckv_rows).astype(BF) if chips else ckv_rows
    enc_grad, qkv_rows = sync([enc_grad, qkv_rows], s_self, hold=(s_ffn,))
    score_total = score_total.reshape(head_count // 2, length, 2, length).transpose(0, 2, 1, 3)
    table_part = lax.dot_general(
        onehot,
        score_total.reshape(head_count, length * length),
        (((1,), (1,)), ((), ())),
        precision=lax.Precision.HIGHEST,
    )
    first_normed_grad = input_grad(qkv_rows, qkv_full)
    unused_value, pullback = jax.vjp(norm_rows, inputs, gain_first)
    input_part, norm_first_grad = pullback(first_normed_grad)
    dec_input_grad = first_grad + input_part
    gain_grads = jnp.stack([norm_first_grad, norm_second_grad, norm_third_grad], axis=1)
    if chips:
        copies = jnp.tile(table_part.reshape(weight_rows, -1), (8, 1))
        small = jnp.concatenate([gain_grads, copies], axis=1)
        small = jnp.pad(small, ((0, 0), (0, 512 - small.shape[1]))).astype(BF)
    else:
        small = gain_grads
    s_cross = scatter(
        lambda: [(enc_grad,), (small,)],
        column_places(
            weight_rows,
            striped(model_width) + (((2 * model_width, 2 * model_width + PAIR),),),
        ),
        lambda: scatter_striped(enc_rows, ckv_rows),
    )
    (dec_input_grad,) = sync([dec_input_grad], s_cross)
    dec_input_grad = dec_input_grad.reshape(item_count, length, model_width)

    part = blocks // 3
    enc_output_grad = rows_part(ckv_rows, kv_full, NT, F32, 0, part, block)
    (enc_output_grad,) = sync([enc_output_grad], s_self, s_cross)
    enc_output_grad = rows_part(ckv_rows, kv_full, NT, F32, part, part, block, enc_output_grad)
    (enc_output_grad,) = sync([enc_output_grad], s_cross)
    enc_output_grad = rows_part(
        ckv_rows, kv_full, NT, F32, 2 * part, blocks - 2 * part, block, enc_output_grad
    )
    (enc_output_grad,) = sync([enc_output_grad], hold=(s_self,))
    enc_output_grad = enc_output_grad.reshape(item_count, enc_len, model_width)
    sync([], s_self, hold=(s_cross,))
    sync([], s_cross, hold=(s_self,))
    sync([], s_cross)
    sync([], s_cross)
    ffn_gate_grad, ffn_up_grad, ffn_down_grad = s_ffn.result
    cross_key_grad, cross_value_grad, *small = s_cross.result
    (
        self_out_grad,
        self_query_grad,
        self_key_grad,
        self_value_grad,
        cross_query_grad,
        cross_out_grad,
    ) = s_self.result

    if chips:
        gain_grads = [small[0][:, k] for k in range(3)]
        count = table_part.size // weight_rows
        bias_table_grad = small[0][:, 3 : 3 + count].reshape(bucket_count, head_count)
    else:
        gain_width = norm_first.shape[0]
        start = (lax.axis_index("fsdp") * sizes[2] + lax.axis_index("mp")) * gain_width
        gain_grads = lax.psum(gain_grads, ("dp", "fsdp", "mp"))
        gain_grads = list(lax.dynamic_slice_in_dim(gain_grads, start, gain_width).T)
        bias_table_grad = lax.psum(table_part, ("dp", "fsdp", "mp"))

    return (
        dec_output,
        dec_input_grad,
        enc_output_grad,
        self_query_grad,
        self_key_grad,
        self_value_grad,
        self_out_grad,
        cross_query_grad,
        cross_key_grad,
        cross_value_grad,
        cross_out_grad,
        ffn_gate_grad,
        ffn_up_grad,
        ffn_down_grad,
        gain_grads[0],
        gain_grads[1],
        gain_grads[2],
        bias_table_grad,
    )


def solution(mesh):
    items = P(("dp", "fsdp", "mp"), None, None)
    item_numbers = P(("dp", "fsdp", "mp"))
    weight = P(("fsdp", "mp"), None)
    gain = P(("fsdp", "mp"))
    sizes = (mesh.shape["dp"], mesh.shape["fsdp"], mesh.shape["mp"])
    return jax.shard_map(
        functools.partial(shards, sizes),
        mesh=mesh,
        in_specs=(items, items)
        + (item_numbers,) * 3
        + (weight,) * 11
        + (gain,) * 3
        + (P(), items),
        out_specs=(items,) * 3 + (weight,) * 11 + (gain,) * 3 + (P(),),
        check_vma=False,
    )
```
